128 devices in a mesh: grid: 32 (over z, x, core), pert: 4 (over y).
Axes of the slice: x: 4, y: 4, z: 4, core: 2. Of those that a mesh axis runs over, the one named last changes fastest.
Arguments:
- basis_values: bfloat16 [131072, 1024], P(('grid', 'pert')), may hold values from -6 to 6
- point_coords: float32 [3, 131072], P(None, 'grid'), may hold values from 0 to 4
- point_weights: float32 [131072], P('grid'), may hold values from 0.005 to 0.05
- xc_kernel: float32 [131072], P('grid'), may hold values from -2 to -0.5
- gauss_widths: float32 [64], replicated, may hold values from 0.3 to 3
- atom_coords: float32 [3, 256], replicated, may hold values from 0 to 4
- resp_density: bfloat16 [4, 128, 256, 256], P('pert', 'grid'), may hold values from -0.0059814453 to 0.0059814453
- tile_list: int32 [64, 16], P('grid'), may hold values from 0 to 127, as said below
- tile_home: int32 [128], replicated, may hold values from 0 to 127, as said below
- atom_list: int32 [64, 16], P('grid'), may hold values from 0 to 255, all different within a row
- atom_home: int32 [256], replicated, may hold values from 0 to 255, each once
Outputs:
- hamiltonian: float32 [4, 128, 256, 256], P('pert', 'grid')
- coefficients: float32 [4, 256, 64], P('pert', 'grid')
- potential: float32 [4, 131072], P('pert', 'grid')
The draws below stay inside these ranges and needn't reach their ends.
Inputs may be any that keep to these rules, and one draw needn't show every extreme that they name: `tile_list`: the 2 batches of one index of grid, rows of aligned blocks of 2, name 32 different tiles; at most 2 of them have tile_home in any one aligned block of 4 positions, and exactly 2 in at least one such block. `tile_home`: each tile has one stored position. `atom_list`: the 16 atoms of a batch are different; every atom is a neighbour of some batch, and atoms are shared: the 64 batches name 1024 slots, four or more for each atom on average, so that an atom is in general a neighbour of batches on several indices of grid.
All inputs are finite; a program needn't handle non-finite values.
Results may differ from the reference program's by a relative error of at most 0.0015.
Values may be sent and summed in bfloat16 or wider, within the bound.
No kernel may reach another device: no remote copies, remote signals or barrier semaphores. Data moves between devices by JAX's collectives and lax.ppermute only.
A program may use at most 192 MiB of HBM per device.

```python
import math
import jax
import jax.numpy as jnp
from jax import lax

BLK = 256
NBLK = 4
LM = 64
BATCH_PTS = 2048
NEI = 16
PERT = 4
BASIS = 1024
PAIRS = 16
REQ = 32
CAP = 2
TILE_DEV = 4
NTILES = 128
NATOM = 256
BATCHES = 64
POINTS = 131072


def tile_plan(key):
    groups = NTILES // TILE_DEV
    home_perm = jax.random.permutation(jax.random.fold_in(key, 11), NTILES).astype(jnp.int32)
    inverse = jnp.argsort(home_perm).astype(jnp.int32)

    def one_device(dev_key):
        subkeys = jax.random.split(dev_key, 4)
        others = jax.random.permutation(subkeys[0], groups * CAP - CAP) + CAP
        positions = jnp.concatenate([jnp.arange(CAP), others])[:REQ]
        rotate = jax.random.randint(subkeys[1], (), 0, groups)
        offsets = jax.random.randint(subkeys[2], (groups,), 0, TILE_DEV)
        owners = (positions // CAP + rotate) % groups
        local_slot = (positions % CAP + offsets[owners]) % TILE_DEV
        homes = (owners * TILE_DEV + local_slot).astype(jnp.int32)
        return jax.random.permutation(subkeys[3], homes)
    dev_keys = jax.random.split(jax.random.fold_in(key, 12), groups)
    wanted_homes = jax.vmap(one_device)(dev_keys)
    tile_ids = inverse[wanted_homes].reshape(BATCHES, PAIRS).astype(jnp.int32)
    return (home_perm, tile_ids)


def draw_tile_home(key, part):
    return tile_plan(key)[0]


def draw_tile_list(key, part):
    return tile_plan(key)[1]


def block_levels(stream_key, extent, cuts, least, high):
    def one(dim, shards_of):
        draws = jax.random.uniform(jax.random.fold_in(jax.random.fold_in(stream_key, 6), dim), (shards_of,), jnp.float32, least / len(cuts), high / len(cuts))
        return jnp.repeat(jnp.exp(draws), extent[dim] // shards_of).reshape((-1,) + (1,) * (len(extent) - dim - 1))

    factor_of = one(*cuts[0])
    for cut in cuts[1:]:
        factor_of = factor_of * one(*cut)
    return factor_of


def different_ones(stream_key, rows, count, top, lift):
    ranking = jax.random.permutation(jax.random.fold_in(stream_key, 1), count)
    boost = ranking
    for power in range(3):
        boost = boost * boost // count
    boost = boost * lift // count
    tickets = jax.random.randint(jax.random.fold_in(stream_key, 2), (rows, count), 0, 4096) + boost
    holders = jax.random.permutation(jax.random.fold_in(stream_key, 3), rows)[jnp.arange(count) % rows]
    tickets = jnp.where(jnp.arange(rows)[:, None] == holders[None, :], 1 << 14, tickets)
    merit = tickets * count + jnp.arange(count)
    return lax.top_k(merit.astype(jnp.int32), top)[1].astype(jnp.int32)


def gaussian(own_key, shape, deviation, bound, cuts=(), held_as=jnp.bfloat16):
    result = jax.random.normal(own_key, shape, jnp.float32) * deviation
    if len(cuts) > 0:
        result = block_levels(own_key, shape, cuts, -0.22, 0.18) * result
    return jnp.clip(result, min=-bound, max=bound).astype(held_as)


def setup_inputs(seed: int = 0) -> dict:
    arg_keys = jax.random.split(jax.random.key(seed), 12)
    return {
        "basis_values": gaussian(arg_keys[0], (POINTS, BASIS), 1.0, 6.0, ((0, 128),)),
        "point_coords": jnp.clip(4.0 * jax.random.uniform(arg_keys[1], (3, POINTS), jnp.float32) ** block_levels(arg_keys[1], (3, POINTS), ((1, 32),), -0.2, 0.2), 0.0, 4.0),
        "point_weights": jnp.clip(jnp.exp(math.log(0.05) - 2.3025851 * jax.random.uniform(arg_keys[2], (POINTS,), jnp.float32) ** block_levels(arg_keys[2], (POINTS,), ((0, 32),), -0.2, 0.2)), 0.005, 0.05),
        "xc_kernel": jnp.clip(-2.0 + 1.5 * jax.random.uniform(arg_keys[3], (POINTS,), jnp.float32) ** block_levels(arg_keys[3], (POINTS,), ((0, 32),), -0.2, 0.2), -2.0, -0.5),
        "gauss_widths": jnp.clip(jnp.exp(jax.random.uniform(arg_keys[4], (LM,), jnp.float32, math.log(0.3), math.log(3.0))), 0.3, 3.0),
        "atom_coords": jnp.clip(jax.random.uniform(arg_keys[5], (3, NATOM), jnp.float32, 0.0, 4.0), 0.0, 4.0),
        "resp_density": gaussian(arg_keys[6], (PERT, NTILES, BLK, BLK), 0.001, 0.0059814453, ((0, 4), (1, 32))),
        "tile_list": draw_tile_list(jax.random.fold_in(arg_keys[11], 71), 0),
        "tile_home": draw_tile_home(jax.random.fold_in(arg_keys[11], 71), 0),
        "atom_list": different_ones(arg_keys[9], BATCHES, NATOM, NEI, 512),
        "atom_home": jax.random.permutation(arg_keys[10], NATOM).astype(jnp.int32),
    }


SOFTEN = 0.25
ROOT_TWO = 1.4142135623730951

def pair_dist(coords_rows, atom_pos):
    delta = coords_rows[:, :, None] - atom_pos[:, None, :]
    return lax.optimization_barrier(jnp.sum(delta * delta, axis=0)) + SOFTEN

def reference(basis_values, point_coords, point_weights, xc_kernel, gauss_widths, atom_coords, resp_density, tile_list, tile_home, atom_list, atom_home):
    phi_all = basis_values.reshape(BATCHES, BATCH_PTS, BASIS)
    coords_all = point_coords.reshape(3, BATCHES, BATCH_PTS).transpose(1, 0, 2)
    weight_all = point_weights.reshape(BATCHES, BATCH_PTS)
    xc_all = xc_kernel.reshape(BATCHES, BATCH_PTS)
    spread = 2.0 * gauss_widths * gauss_widths
    erf_scale = ROOT_TWO * gauss_widths
    ham_out = []
    coeff_out = []
    pot_out = []
    for pert_index in range(PERT):
        tile_data = resp_density[pert_index]

        def density_step(coeffs, batch_data):
            phi_rows, coords_rows, weight_rows, tile_ids, atom_ids = batch_data
            tile_homes = tile_home[tile_ids]
            dens_matrix = tile_data[tile_homes].reshape(NBLK, NBLK, BLK, BLK).transpose(0, 2, 1, 3).reshape(BASIS, BASIS)
            mixed_rows = jnp.dot(phi_rows, dens_matrix, preferred_element_type=jnp.float32)
            response = lax.optimization_barrier(jnp.sum(mixed_rows * phi_rows.astype(jnp.float32), axis=1))
            dist_sq = pair_dist(coords_rows, atom_coords[:, atom_ids])
            gaussians = jnp.exp(-dist_sq[:, :, None] / spread).reshape(BATCH_PTS, NEI * LM)
            partial_value = jnp.dot(weight_rows * response, gaussians, precision=lax.Precision.HIGHEST)
            coeffs = coeffs.at[atom_home[atom_ids]].add(partial_value.reshape(NEI, LM))
            return (coeffs, response)
        coeffs, responses = lax.scan(density_step, jnp.zeros((NATOM, LM), jnp.float32), (phi_all, coords_all, weight_all, tile_list, atom_list))

        def potential_step(hamiltonian, batch_data):
            phi_rows, coords_rows, weight_rows, xc_rows, response, tile_ids, atom_ids = batch_data
            distance = jnp.sqrt(pair_dist(coords_rows, atom_coords[:, atom_ids]))
            kernel = (lax.erf(distance[:, :, None] / erf_scale) / distance[:, :, None]).reshape(BATCH_PTS, NEI * LM)
            coeff_vec = coeffs[atom_home[atom_ids]].reshape(NEI * LM)
            hartree = jnp.dot(kernel, coeff_vec, precision=lax.Precision.HIGHEST)
            potential = hartree + xc_rows * response
            scaled = (phi_rows.astype(jnp.float32) * (weight_rows * potential)[:, None]).astype(jnp.bfloat16)
            ham_matrix = jnp.dot(phi_rows.T, scaled, preferred_element_type=jnp.float32)
            ham_tiles = ham_matrix.reshape(NBLK, BLK, NBLK, BLK).transpose(0, 2, 1, 3).reshape(PAIRS, BLK, BLK)
            hamiltonian = hamiltonian.at[tile_home[tile_ids]].add(ham_tiles)
            return (hamiltonian, potential)
        hamiltonian, potentials = lax.scan(potential_step, jnp.zeros((NTILES, BLK, BLK), jnp.float32), (phi_all, coords_all, weight_all, xc_all, responses, tile_list, atom_list))
        ham_out.append(hamiltonian)
        coeff_out.append(coeffs)
        pot_out.append(potentials.reshape(POINTS))
    return (jnp.stack(ham_out), jnp.stack(coeff_out), jnp.stack(pot_out))
```

```python
import jax
import jax.numpy as jnp
from jax import lax
from jax.experimental import pallas as pl
from jax.experimental.pallas import tpu as pltpu
from jax.sharding import PartitionSpec as P

SOFTEN = 0.25
ROOT_TWO = 1.4142135623730951
HALF = 512
PIECES = 8
BLK = 256
NB = 4
PHI_MAX_SQ = 36.0
KERNEL_MAX = 2.0
F16_TOP = 32000.0
HIGH = lax.Precision.HIGHEST


def ring(shift):
    return [(i, (i + shift) % 4) for i in range(4)]


def grid_perm(dz, dx, dc):
    def at(z, x, c):
        return ((z % 4) * 4 + x % 4) * 2 + c

    return [
        (at(z, x, c), at(z + dz, x + dx, c ^ dc))
        for z in range(4)
        for x in range(4)
        for c in range(2)
    ]


def load_pieces(piece_refs, held, sems):
    for i, ref in enumerate(piece_refs):
        pltpu.make_async_copy(ref, held.at[i], sems.at[i]).start()


def density_body(order, where, *refs):
    pieces = refs[:PIECES]
    tiles, table, weights, rho, pacc, held, dmat, tbuf, psem, dsem, tsem = refs[PIECES:]
    for b in range(2):
        for t in range(16):
            pltpu.make_async_copy(
                tiles.at[where[b * 16 + t]],
                dmat.at[b, pl.ds((t // 4) * BLK, BLK), pl.ds((t % 4) * BLK, BLK)],
                dsem.at[b],
            ).start()
    load_pieces(pieces, held, psem)
    pltpu.make_async_copy(table.at[order[0]], tbuf.at[0], tsem.at[0]).start()
    pacc[...] = jnp.zeros_like(pacc)
    for b in range(2):
        pltpu.make_async_copy(dmat.at[b], dmat.at[b], dsem.at[b]).wait()

    def step(i, _):
        slot = lax.rem(i, 2)

        @pl.when(i + 1 < PIECES)
        def _():
            pltpu.make_async_copy(
                table.at[order[i + 1]], tbuf.at[1 - slot], tsem.at[1 - slot]
            ).start()

        pi = order[i]
        b = pi // 4
        pltpu.make_async_copy(held.at[i], held.at[i], psem.at[i]).wait()
        piece = held[i]
        total = jnp.zeros((1, HALF), jnp.float32)
        for block in range(NB):
            rows = pl.ds(block * BLK, BLK)
            mixed = jnp.dot(dmat[b, rows, :], piece, preferred_element_type=jnp.float32)
            total = total + jnp.sum(
                mixed * held[i, rows, :].astype(jnp.float32), axis=0, keepdims=True
            )
        rho[pi] = total
        weighted = weights[pi] * total
        pltpu.make_async_copy(table.at[pi], tbuf.at[slot], tsem.at[slot]).wait()
        for block in range(8):
            rows = pl.ds(block * 128, 128)
            part = pacc[b, rows, :]
            for lane in range(HALF // 128):
                cols = slice(lane * 128, (lane + 1) * 128)
                part = part + tbuf[slot, rows, cols] * weighted[:, cols]
            pacc[b, rows, :] = part
        return 0

    lax.fori_loop(0, PIECES, step, 0)


def ham_body(order, *refs):
    pieces = refs[:PIECES]
    (table, coeff, weights, xc, rho, pot, ham, held, tbuf, scaled, psem, tsem) = refs[PIECES:]
    load_pieces(pieces, held, psem)
    pltpu.make_async_copy(table.at[order[0]], tbuf.at[0], tsem.at[0]).start()
    ham[...] = jnp.zeros_like(ham)

    def step(i, _):
        slot = lax.rem(i, 2)

        @pl.when(i + 1 < PIECES)
        def _():
            pltpu.make_async_copy(
                table.at[order[i + 1]], tbuf.at[1 - slot], tsem.at[1 - slot]
            ).start()

        pi = order[i]
        b = pi // 4
        pltpu.make_async_copy(table.at[pi], tbuf.at[slot], tsem.at[slot]).wait()
        sums = []
        for lane in range(HALF // 128):
            cols = slice(lane * 128, (lane + 1) * 128)
            part = jnp.zeros((8, 128), jnp.float32)
            for block in range(16):
                rows = pl.ds(block * 64, 64)
                prod = tbuf[slot, rows, cols] * coeff[b, rows, :]
                part = part + jnp.sum(prod.reshape(8, 8, 128), axis=0)
            sums.append(jnp.sum(part, axis=0, keepdims=True))
        hartree = jnp.concatenate(sums, axis=1)
        potential = hartree + xc[pi] * rho[pi]
        pot[pi] = potential
        scale_row = weights[pi] * potential
        pltpu.make_async_copy(held.at[i], held.at[i], psem.at[i]).wait()
        scaled[...] = (held[i].astype(jnp.float32) * scale_row).astype(jnp.bfloat16)
        for block in range(NB):
            rows = pl.ds(block * BLK, BLK)
            part = lax.dot_general(
                held[i, rows, :],
                scaled[...],
                (((1,), (1,)), ((), ())),
                preferred_element_type=jnp.float32,
            )
            for col in range(NB):
                at = b * 16 + block * NB + col
                ham[at] = ham[at] + part[:, col * BLK : (col + 1) * BLK]
        return 0

    lax.fori_loop(0, PIECES, step, 0)


def any_spec():
    return pl.BlockSpec(memory_space=pl.ANY)


def vmem_spec():
    return pl.BlockSpec(memory_space=pltpu.VMEM)


def smem_spec():
    return pl.BlockSpec(memory_space=pltpu.SMEM)


def density_call(order, where, pieces, tiles, table, weights):
    nbasis = NB * BLK
    return pl.pallas_call(
        density_body,
        out_shape=(
            jax.ShapeDtypeStruct((PIECES, 1, HALF), jnp.float32),
            jax.ShapeDtypeStruct((2, nbasis, 128), jnp.float32),
        ),
        in_specs=[smem_spec(), smem_spec()] + [any_spec()] * (PIECES + 2) + [vmem_spec()],
        out_specs=(vmem_spec(), vmem_spec()),
        scratch_shapes=[
            pltpu.VMEM((PIECES, nbasis, HALF), jnp.bfloat16),
            pltpu.VMEM((2, nbasis, nbasis), jnp.bfloat16),
            pltpu.VMEM((2, nbasis, HALF), jnp.float32),
            pltpu.SemaphoreType.DMA((PIECES,)),
            pltpu.SemaphoreType.DMA((2,)),
            pltpu.SemaphoreType.DMA((2,)),
        ],
        compiler_params=pltpu.CompilerParams(vmem_limit_bytes=40 << 20),
        cost_estimate=pl.CostEstimate(
            flops=2 * 4096 * 1024 * 1024, bytes_accessed=32 << 20, transcendentals=0
        ),
        name="density",
    )(order, where, *pieces, tiles, table, weights)


def ham_call(order, pieces, table, coeff, weights, xc, rho):
    nbasis = NB * BLK
    return pl.pallas_call(
        ham_body,
        out_shape=(
            jax.ShapeDtypeStruct((PIECES, 1, HALF), jnp.float32),
            jax.ShapeDtypeStruct((2 * NB * NB, BLK, BLK), jnp.float32),
        ),
        in_specs=[smem_spec()] + [any_spec()] * (PIECES + 1) + [vmem_spec()] * 4,
        out_specs=(vmem_spec(), vmem_spec()),
        scratch_shapes=[
            pltpu.VMEM((PIECES, nbasis, HALF), jnp.bfloat16),
            pltpu.VMEM((2, nbasis, HALF), jnp.float32),
            pltpu.VMEM((nbasis, HALF), jnp.bfloat16),
            pltpu.SemaphoreType.DMA((PIECES,)),
            pltpu.SemaphoreType.DMA((2,)),
        ],
        compiler_params=pltpu.CompilerParams(vmem_limit_bytes=48 << 20),
        cost_estimate=pl.CostEstimate(
            flops=2 * 4096 * 1024 * 1024, bytes_accessed=32 << 20, transcendentals=0
        ),
        name="ham",
    )(order, *pieces, table, coeff, weights, xc, rho)


def ring_sum(parts, axis_name, send_up, send_down, split_axis):
    far = parts[2]
    half = far.shape[split_axis] // 2
    low = lax.slice_in_dim(far, 0, half, axis=split_axis)
    high = lax.slice_in_dim(far, half, 2 * half, axis=split_axis)
    from_below = lax.ppermute(low, axis_name, send_up)
    from_above = lax.ppermute(high, axis_name, send_down)

    def cut(x, lo, hi):
        return lax.slice_in_dim(x, lo, hi, axis=split_axis)

    def plus(a, b):
        return (a.astype(jnp.float32) + b.astype(jnp.float32)).astype(jnp.float16)

    up = lax.concatenate(
        [plus(cut(parts[1], 0, half), from_below), cut(parts[1], half, 2 * half)], split_axis
    )
    down = lax.concatenate(
        [cut(parts[3], 0, half), plus(cut(parts[3], half, 2 * half), from_above)], split_axis
    )
    got_below = lax.ppermute(up, axis_name, send_up)
    got_above = lax.ppermute(down, axis_name, send_down)
    return (
        parts[0].astype(jnp.float32)
        + got_below.astype(jnp.float32)
        + got_above.astype(jnp.float32)
    )


def per_device(
    basis_values,
    point_coords,
    point_weights,
    xc_kernel,
    gauss_widths,
    atom_coords,
    resp_density,
    tile_list,
    tile_home,
    atom_list,
    atom_home,
):
    groups = lax.axis_size("grid")
    me = lax.axis_index("grid")
    plane = lax.axis_index("pert")
    my_z, my_x, my_c = me // 8, (me // 2) % 4, me % 2
    tile_dev = resp_density.shape[1]
    neighbors = atom_list.shape[1]
    moments = gauss_widths.shape[0]
    natoms = atom_home.shape[0]
    ntiles = tile_home.shape[0]
    slots_here = 2 * neighbors

    own = [basis_values[:HALF].T, basis_values[HALF:].T]
    below0 = lax.ppermute(own[0], "pert", ring(1))
    above1 = lax.ppermute(own[1], "pert", ring(3))
    below1 = lax.ppermute(own[1], "pert", ring(1))
    above0 = lax.ppermute(own[0], "pert", ring(3))
    far0 = lax.ppermute(below0, "pert", ring(1))
    far1 = lax.ppermute(above1, "pert", ring(3))
    pieces = [own[0], own[1], below0, below1, above0, above1, far0, far1]
    steps = jnp.array([0, 0, 3, 3, 1, 1, 2, 2], jnp.int32)
    halves = jnp.array([0, 1] * 4, jnp.int32)
    order = ((plane + steps) % 4) * 2 + halves

    tiles = lax.all_gather(resp_density[0], "grid", axis=0, tiled=True)
    wanted = tile_list.reshape(-1)
    tile_match = wanted[:, None] == jnp.arange(ntiles, dtype=jnp.int32)[None, :]
    homes = jnp.sum(jnp.where(tile_match, tile_home[None, :], 0), axis=1)
    homes_beside = lax.ppermute(homes, "grid", grid_perm(0, 0, 1))

    atom_match = atom_list[:, :, None] == jnp.arange(natoms, dtype=jnp.int32)
    atom_pos = jnp.sum(jnp.where(atom_match[None], atom_coords[:, None, None, :], 0.0), axis=3)
    atom_homes = jnp.sum(jnp.where(atom_match, atom_home, 0), axis=2).reshape(-1)
    delta = point_coords.reshape(3, 2, 4, 1, HALF) - atom_pos[:, :, None, :, None]
    dist_sq = (jnp.sum(delta * delta, axis=0) + SOFTEN).reshape(PIECES, neighbors, 1, HALF)
    spread = (2.0 * gauss_widths * gauss_widths)[None, None, :, None]
    erf_scale = (ROOT_TWO * gauss_widths)[None, None, :, None]
    gauss = jnp.exp(-dist_sq / spread).reshape(PIECES, neighbors * moments, HALF)
    distance = jnp.sqrt(dist_sq)
    hart = (lax.erf(distance / erf_scale) / distance).reshape(PIECES, neighbors * moments, HALF)
    weights = point_weights.reshape(PIECES, 1, HALF)
    xc = xc_kernel.reshape(PIECES, 1, HALF)

    rho, pacc = density_call(order, homes, pieces, tiles, gauss, weights)
    partial_value = jnp.sum(pacc, axis=2).reshape(slots_here, moments)
    top = jnp.max(jnp.abs(xc * rho))
    extra = jnp.concatenate(
        [atom_homes.astype(jnp.float32), jnp.full((moments - slots_here,), top)]
    )
    payload = jnp.concatenate([partial_value, extra[None, :]], axis=0)
    sent = jnp.broadcast_to(payload[None], (groups, slots_here + 1, moments))
    got = lax.all_to_all(sent, "grid", split_axis=0, concat_axis=0, tiled=True)
    all_partial = got[:, :slots_here].reshape(groups * slots_here, moments)
    all_homes = got[:, slots_here, :slots_here].reshape(-1)
    rows = jnp.concatenate(
        [jnp.arange(natoms, dtype=jnp.float32), atom_homes.astype(jnp.float32)]
    )
    select = (rows[:, None] == all_homes[None, :]).astype(jnp.float32)
    summed = jnp.dot(select, all_partial, precision=HIGH)
    all_coeffs, my_coeffs = summed[:natoms], summed[natoms:]
    atom_dev = natoms // groups
    own_coeffs = lax.dynamic_slice_in_dim(all_coeffs, me * atom_dev, atom_dev, axis=0)
    coeff = jnp.broadcast_to(
        my_coeffs.reshape(2, neighbors * moments, 1), (2, neighbors * moments, 128)
    )
    pot_bound = jnp.max(got[:, slots_here, slots_here]) + KERNEL_MAX * neighbors * jnp.max(
        jnp.sum(jnp.abs(all_coeffs), axis=1)
    )
    ham_bound = PHI_MAX_SQ * 2048 * 0.05 * groups * pot_bound * 1.01 + 1e-20

    pot, ham = ham_call(order, pieces, hart, coeff, weights, xc, rho)

    mine = (ham * (F16_TOP / ham_bound)).astype(jnp.float16)
    beside = lax.ppermute(mine, "grid", grid_perm(0, 0, 1))
    dz = jnp.arange(4, dtype=jnp.int32)[:, None, None]
    dx = jnp.arange(4, dtype=jnp.int32)[None, :, None]
    place = jnp.arange(tile_dev, dtype=jnp.int32)[None, None, :]
    slot_home = (
        ((((my_z + dz) % 4) * 4 + (my_x + dx) % 4) * 2 + my_c) * tile_dev + place
    ).reshape(-1)

    def placed(tiles_of, homes_of):
        match = slot_home[:, None] == homes_of[None, :]
        index = jnp.sum(jnp.where(match, jnp.arange(slots_here, dtype=jnp.int32), 0), axis=1)
        found = jnp.any(match, axis=1)
        return jnp.where(found[:, None, None], jnp.take(tiles_of, index, axis=0), 0).astype(
            jnp.float32
        )

    dense = (placed(mine, homes) + placed(beside, homes_beside)).astype(jnp.float16)
    dense = dense.reshape(4, 4, tile_dev, BLK, BLK)
    z_up, z_down = grid_perm(1, 0, 0), grid_perm(-1, 0, 0)
    x_up, x_down = grid_perm(0, 1, 0), grid_perm(0, -1, 0)
    half = BLK // 2
    upper = dense[:, :, :, :half]
    lower = dense[:, :, :, half:]
    upper = ring_sum([upper[d] for d in range(4)], "grid", z_up, z_down, 0)
    lower = ring_sum([lower[:, d] for d in range(4)], "grid", x_up, x_down, 0)
    upper = upper.astype(jnp.float16)
    lower = lower.astype(jnp.float16)
    upper = ring_sum([upper[d] for d in range(4)], "grid", x_up, x_down, 0)
    lower = ring_sum([lower[d] for d in range(4)], "grid", z_up, z_down, 0)
    hamiltonian = jnp.concatenate([upper, lower], axis=1) * (ham_bound / F16_TOP)
    return (hamiltonian[None], own_coeffs[None], pot.reshape(1, -1))


def solution(mesh):
    placed = (
        P(("grid", "pert"), None),
        P(None, "grid"),
        P("grid"),
        P("grid"),
        P(),
        P(),
        P("pert", "grid", None, None),
        P("grid", None),
        P(),
        P("grid", None),
        P(),
    )
    return jax.shard_map(
        per_device,
        mesh=mesh,
        in_specs=placed,
        out_specs=(P("pert", "grid", None, None), P("pert", "grid", None), P("pert", "grid")),
        check_vma=False,
    )
```

```python
import jax
import jax.numpy as jnp
from jax import lax
from jax.experimental import pallas as pl
from jax.experimental.pallas import tpu as pltpu
from jax.sharding import PartitionSpec as P

SOFTEN = 0.25
ROOT_TWO = 1.4142135623730951
HALF = 512
PIECES = 8
BLK = 256
NB = 4
PHI_MAX_SQ = 36.0
KERNEL_MAX = 2.0
F16_TOP = 32000.0
PAY_ROWS = 24


def ring(shift):
    return [(i, (i + shift) % 4) for i in range(4)]


def grid_perm(dz, dx, dc):
    def at(z, x, c):
        return ((z % 4) * 4 + x % 4) * 2 + c

    return [
        (at(z, x, c), at(z + dz, x + dx, c ^ dc))
        for z in range(4)
        for x in range(4)
        for c in range(2)
    ]


def load_pieces(piece_refs, held, sems):
    for i, ref in enumerate(piece_refs):
        pltpu.make_async_copy(ref, held.at[i], sems.at[i]).start()


def split3(x):
    first = x.astype(jnp.bfloat16)
    rest = x - first.astype(jnp.float32)
    second = rest.astype(jnp.bfloat16)
    third = (rest - second.astype(jnp.float32)).astype(jnp.bfloat16)
    return first, second, third


def density_body(order, where, *refs):
    pieces = refs[:PIECES]
    (tiles, table, weights, xc, rho, sent, pacc, block_out, held, dmat, tbuf, psem, dsem, tsem) = (
        refs[PIECES:]
    )
    for b in range(2):
        for t in range(16):
            pltpu.make_async_copy(
                tiles.at[where[b * 16 + t]],
                dmat.at[b, pl.ds((t // 4) * BLK, BLK), pl.ds((t % 4) * BLK, BLK)],
                dsem.at[b],
            ).start()
    load_pieces(pieces, held, psem)
    pltpu.make_async_copy(table.at[order[0]], tbuf.at[0], tsem.at[0]).start()
    pacc[...] = jnp.zeros_like(pacc)
    block_out[...] = jnp.zeros_like(block_out)
    for b in range(2):
        pltpu.make_async_copy(dmat.at[b], dmat.at[b], dsem.at[b]).wait()

    def step(i, top):
        slot = lax.rem(i, 2)

        @pl.when(i + 1 < PIECES)
        def _():
            pltpu.make_async_copy(
                table.at[order[i + 1]], tbuf.at[1 - slot], tsem.at[1 - slot]
            ).start()

        pi = order[i]
        b = pi // 4
        pltpu.make_async_copy(held.at[i], held.at[i], psem.at[i]).wait()
        piece = held[i]
        total = jnp.zeros((1, HALF), jnp.float32)
        for block in range(NB):
            rows = pl.ds(block * BLK, BLK)
            mixed = jnp.dot(dmat[b, rows, :], piece, preferred_element_type=jnp.float32)
            total = total + jnp.sum(
                mixed * held[i, rows, :].astype(jnp.float32), axis=0, keepdims=True
            )
        rho[pi] = total
        weighted = weights[pi] * total
        pltpu.make_async_copy(table.at[pi], tbuf.at[slot], tsem.at[slot]).wait()
        for block in range(8):
            rows = pl.ds(block * 128, 128)
            part = pacc[b, rows, :]
            for lane in range(HALF // 128):
                cols = slice(lane * 128, (lane + 1) * 128)
                part = part + tbuf[slot, rows, cols] * weighted[:, cols]
            pacc[b, rows, :] = part
        return jnp.maximum(top, jnp.abs(xc[pi] * total))

    top = lax.fori_loop(0, PIECES, step, jnp.zeros((1, HALF), jnp.float32))
    ones = jnp.ones((8, 128), jnp.bfloat16)
    for b in range(2):
        total = jnp.zeros((8, NB * BLK), jnp.float32)
        for term in split3(pacc[b]):
            total = total + lax.dot_general(
                ones, term, (((1,), (1,)), ((), ())), preferred_element_type=jnp.float32
            )
        for r in range(8):
            block_out[pl.ds(b * 8 + r, 1), :] = total[0:1, r * 128 : (r + 1) * 128]
    block_out[pl.ds(16, 1), :] = jnp.broadcast_to(jnp.max(top, axis=1, keepdims=True), (1, 128))
    for dest in range(32):
        sent[dest] = block_out[...]


def potential_body(table, got, even, odd, weights, xc, rho, coeffs, pot, scale, bound, *scratch):
    tbuf, column, tsem = scratch
    for i in range(2):
        pltpu.make_async_copy(table.at[i], tbuf.at[i], tsem.at[i]).start()
    first = jnp.zeros((even.shape[0], 128), jnp.float32)
    second = jnp.zeros((even.shape[0], 128), jnp.float32)
    for term in split3(got[...]):
        first = first + jnp.dot(even[...], term, preferred_element_type=jnp.float32)
        second = second + jnp.dot(odd[...], term, preferred_element_type=jnp.float32)
    summed = first[:, :64] + second[:, 64:]
    natoms = coeffs.shape[0]
    coeffs[...] = summed[:natoms]
    turned = summed[natoms:].T
    for k in range(32):
        column[pl.ds(k * 64, 64), :] = jnp.broadcast_to(turned[:, k : k + 1], (64, 128))
    top = jnp.zeros((1, 128), jnp.float32)
    for k in range(32):
        top = jnp.maximum(top, got[pl.ds(k * PAY_ROWS + 16, 1), :])
    heavy = jnp.max(jnp.sum(jnp.abs(summed[:natoms]), axis=1, keepdims=True), axis=0, keepdims=True)
    bound[...] = top + jnp.broadcast_to(heavy, (1, 128)) * (KERNEL_MAX * 16)

    def step(i, _):
        slot = lax.rem(i, 3)

        @pl.when(i + 2 < PIECES)
        def _():
            ahead = lax.rem(i + 2, 3)
            pltpu.make_async_copy(table.at[i + 2], tbuf.at[ahead], tsem.at[ahead]).start()

        base = (i // 4) * 1024
        pltpu.make_async_copy(table.at[i], tbuf.at[slot], tsem.at[slot]).wait()
        parts = [jnp.zeros((8, 128), jnp.float32) for _ in range(HALF // 128)]
        for block in range(16):
            factor = column[pl.ds(base + block * 64, 64), :]
            for lane in range(HALF // 128):
                prod = tbuf[slot, block * 64 : (block + 1) * 64, lane * 128 : (lane + 1) * 128]
                parts[lane] = parts[lane] + jnp.sum((prod * factor).reshape(8, 8, 128), axis=0)
        hartree = jnp.concatenate([jnp.sum(p, axis=0, keepdims=True) for p in parts], axis=1)
        potential = hartree + xc[i] * rho[i]
        pot[i] = potential
        scale[i] = weights[i] * potential
        return 0

    lax.fori_loop(0, PIECES, step, 0)


def ham_body(order, listed, slots, starts, *refs):
    pieces = refs[: 2 * PIECES]
    scale_mine, scale_beside, out, held, dense, rows_of, psem, osem = refs[2 * PIECES :]
    for i in range(2 * PIECES):
        pi = order[i % PIECES]
        pltpu.make_async_copy(
            pieces[i],
            held.at[i // PIECES, pi // 4, :, pl.ds(pl.multiple_of((pi % 4) * HALF, HALF), HALF)],
            psem,
        ).start()
    for b in range(2):
        rows_of[0, b] = scale_mine[b]
        rows_of[1, b] = scale_beside[b]

    def clear(s, _):
        dense[s] = jnp.zeros((BLK, BLK), jnp.float32)
        return 0

    lax.fori_loop(0, dense.shape[0], clear, 0)
    pltpu.make_async_copy(held, held, psem).wait()

    def product(n, flag):
        code = listed[n]
        side, tile = code // 32, code % 32
        b, row, col = tile // 16, (tile // 4) % 4, tile % 4
        left = held[side, b, pl.ds(pl.multiple_of(row * BLK, BLK), BLK), :]
        right = held[side, b, pl.ds(pl.multiple_of(col * BLK, BLK), BLK), :]
        right = (right.astype(jnp.float32) * (rows_of[side, b] * flag)).astype(jnp.bfloat16)
        return lax.dot_general(
            left, right, (((1,), (1,)), ((), ())), preferred_element_type=jnp.float32
        )

    for quarter in range(4):
        begin, end = starts[quarter], starts[quarter + 1]

        def pair(k, _):
            n = begin + 2 * k
            other = jnp.minimum(n + 1, end - 1)
            one = product(n, 1.0)
            two = product(other, jnp.where(n + 1 < end, 1.0, 0.0).astype(jnp.float32))
            dense[slots[n]] += one
            dense[slots[other]] += two
            return 0

        lax.fori_loop(0, (end - begin + 1) // 2, pair, 0)
        part = pl.ds(quarter * 16, 16)
        pltpu.make_async_copy(dense.at[part], out.at[part], osem.at[quarter]).start()
    for quarter in range(4):
        part = pl.ds(quarter * 16, 16)
        pltpu.make_async_copy(dense.at[part], out.at[part], osem.at[quarter]).wait()


def any_spec():
    return pl.BlockSpec(memory_space=pl.ANY)


def vmem_spec():
    return pl.BlockSpec(memory_space=pltpu.VMEM)


def smem_spec():
    return pl.BlockSpec(memory_space=pltpu.SMEM)


def density_call(order, where, pieces, tiles, table, weights, xc):
    nbasis = NB * BLK
    return pl.pallas_call(
        density_body,
        out_shape=(
            jax.ShapeDtypeStruct((PIECES, 1, HALF), jnp.float32),
            jax.ShapeDtypeStruct((32, PAY_ROWS, 128), jnp.float32),
        ),
        in_specs=[smem_spec(), smem_spec()] + [any_spec()] * (PIECES + 2) + [vmem_spec()] * 2,
        out_specs=(vmem_spec(), vmem_spec()),
        scratch_shapes=[
            pltpu.VMEM((2, nbasis, 128), jnp.float32),
            pltpu.VMEM((PAY_ROWS, 128), jnp.float32),
            pltpu.VMEM((PIECES, nbasis, HALF), jnp.bfloat16),
            pltpu.VMEM((2, nbasis, nbasis), jnp.bfloat16),
            pltpu.VMEM((2, nbasis, HALF), jnp.float32),
            pltpu.SemaphoreType.DMA((PIECES,)),
            pltpu.SemaphoreType.DMA((2,)),
            pltpu.SemaphoreType.DMA((2,)),
        ],
        compiler_params=pltpu.CompilerParams(vmem_limit_bytes=36 << 20),
        cost_estimate=pl.CostEstimate(
            flops=2 * 4096 * 1024 * 1024, bytes_accessed=32 << 20, transcendentals=0
        ),
        name="density",
    )(order, where, *pieces, tiles, table, weights, xc)


def potential_call(table, got, even, odd, weights, xc, rho, natoms):
    row = jax.ShapeDtypeStruct((PIECES, 1, HALF), jnp.float32)
    return pl.pallas_call(
        potential_body,
        out_shape=(
            jax.ShapeDtypeStruct((natoms, 64), jnp.float32),
            row,
            row,
            jax.ShapeDtypeStruct((1, 128), jnp.float32),
        ),
        in_specs=[any_spec()] + [vmem_spec()] * 6,
        out_specs=(vmem_spec(),) * 4,
        scratch_shapes=[
            pltpu.VMEM((3, NB * BLK, HALF), jnp.float32),
            pltpu.VMEM((2048, 128), jnp.float32),
            pltpu.SemaphoreType.DMA((3,)),
        ],
        compiler_params=pltpu.CompilerParams(vmem_limit_bytes=16 << 20),
        cost_estimate=pl.CostEstimate(
            flops=16 << 20, bytes_accessed=16 << 20, transcendentals=0
        ),
        name="potential",
    )(table, got, even, odd, weights, xc, rho)


def ham_call(order, listed, slots, starts, pieces, scale_mine, scale_beside):
    nbasis = NB * BLK
    return pl.pallas_call(
        ham_body,
        out_shape=jax.ShapeDtypeStruct((64, BLK, BLK), jnp.float32),
        in_specs=[smem_spec()] * 4 + [any_spec()] * (2 * PIECES) + [vmem_spec()] * 2,
        out_specs=any_spec(),
        scratch_shapes=[
            pltpu.VMEM((2, 2, nbasis, 4 * HALF), jnp.bfloat16),
            pltpu.VMEM((64, BLK, BLK), jnp.float32),
            pltpu.VMEM((2, 2, 1, 4 * HALF), jnp.float32),
            pltpu.SemaphoreType.DMA,
            pltpu.SemaphoreType.DMA((4,)),
        ],
        compiler_params=pltpu.CompilerParams(vmem_limit_bytes=40 << 20),
        cost_estimate=pl.CostEstimate(
            flops=2 * 4096 * 1024 * 1024, bytes_accessed=32 << 20, transcendentals=0
        ),
        name="ham",
    )(order, listed, slots, starts, *pieces, scale_mine, scale_beside)


def cast(x):
    return x.astype(jnp.float16)


def wide(x):
    return x.astype(jnp.float32)


def ring_sum(parts, axis_name, send_up, send_down):
    half = parts[2].shape[0] // 2
    from_below = lax.ppermute(cast(parts[2][:half]), axis_name, send_up)
    from_above = lax.ppermute(cast(parts[2][half:]), axis_name, send_down)
    up = jnp.concatenate([cast(parts[1][:half] + wide(from_below)), cast(parts[1][half:])])
    down = jnp.concatenate([cast(parts[3][:half]), cast(parts[3][half:] + wide(from_above))])
    got_below = lax.ppermute(up, axis_name, send_up)
    got_above = lax.ppermute(down, axis_name, send_down)
    return parts[0] + wide(got_below) + wide(got_above)


def direct_sum(parts, axis_name, perms):
    total = parts[0]
    got = [lax.ppermute(cast(parts[d]), axis_name, perms[d]) for d in (2, 1, 3)]
    for g in got:
        total = total + wide(g)
    return total


def per_device(
    basis_values,
    point_coords,
    point_weights,
    xc_kernel,
    gauss_widths,
    atom_coords,
    resp_density,
    tile_list,
    tile_home,
    atom_list,
    atom_home,
):
    groups = lax.axis_size("grid")
    me = lax.axis_index("grid")
    plane = lax.axis_index("pert")
    my_z, my_x, my_c = me // 8, (me // 2) % 4, me % 2
    tile_dev = resp_density.shape[1]
    neighbors = atom_list.shape[1]
    moments = gauss_widths.shape[0]
    natoms = atom_home.shape[0]
    ntiles = tile_home.shape[0]
    slots_here = 2 * neighbors

    own = [basis_values[:HALF].T, basis_values[HALF:].T]
    below0 = lax.ppermute(own[0], "pert", ring(1))
    above1 = lax.ppermute(own[1], "pert", ring(3))
    below1 = lax.ppermute(own[1], "pert", ring(1))
    above0 = lax.ppermute(own[0], "pert", ring(3))
    far0 = lax.ppermute(below0, "pert", ring(1))
    far1 = lax.ppermute(above1, "pert", ring(3))
    pieces = [own[0], own[1], below0, below1, above0, above1, far0, far1]
    beside = [lax.ppermute(piece, "grid", grid_perm(0, 0, 1)) for piece in pieces]
    steps = jnp.array([0, 0, 3, 3, 1, 1, 2, 2], jnp.int32)
    halves = jnp.array([0, 1] * 4, jnp.int32)
    order = ((plane + steps) % 4) * 2 + halves

    tiles = lax.all_gather(resp_density[0], "grid", axis=0, tiled=True)
    wanted = tile_list.reshape(-1)
    tile_match = wanted[:, None] == jnp.arange(ntiles, dtype=jnp.int32)[None, :]
    homes = jnp.sum(jnp.where(tile_match, tile_home[None, :], 0), axis=1)
    homes_beside = lax.ppermute(homes, "grid", grid_perm(0, 0, 1))

    every_home = jnp.concatenate([homes, homes_beside])
    owner, place = every_home // tile_dev, every_home % tile_dev
    off_z = (owner // 8 - my_z) % 4
    off_x = ((owner // 2) % 4 - my_x) % 4
    slot = (off_z * 4 + off_x) * tile_dev + place
    count = 2 * slots_here
    ids = jnp.arange(count, dtype=jnp.int32)
    valid = owner % 2 == my_c
    key = jnp.where(valid, slot, 64) * count + ids
    rank = jnp.sum((key[None, :] < key[:, None]).astype(jnp.int32), axis=1)
    ranked = rank[None, :] == ids[:, None]
    listed = jnp.sum(jnp.where(ranked, ids[None, :], 0), axis=1)
    slots = jnp.sum(jnp.where(ranked & valid[None, :], slot[None, :], 0), axis=1)
    edges = jnp.arange(8, dtype=jnp.int32) * 16
    starts = jnp.sum((valid[None, :] & (slot[None, :] < edges[:, None])).astype(jnp.int32), axis=1)

    atom_match = atom_list[:, :, None] == jnp.arange(natoms, dtype=jnp.int32)
    atom_pos = jnp.sum(jnp.where(atom_match[None], atom_coords[:, None, None, :], 0.0), axis=3)
    atom_homes = jnp.sum(jnp.where(atom_match, atom_home, 0), axis=2).reshape(-1)
    delta = point_coords.reshape(3, 2, 4, 1, HALF) - atom_pos[:, :, None, :, None]
    dist_sq = (jnp.sum(delta * delta, axis=0) + SOFTEN).reshape(PIECES, neighbors, 1, HALF)
    spread = (2.0 * gauss_widths * gauss_widths)[None, None, :, None]
    erf_scale = (ROOT_TWO * gauss_widths)[None, None, :, None]
    gauss = jnp.exp(-dist_sq / spread).reshape(PIECES, neighbors * moments, HALF)
    distance = jnp.sqrt(dist_sq)
    hart = (lax.erf(distance / erf_scale) / distance).reshape(PIECES, neighbors * moments, HALF)
    weights = point_weights.reshape(PIECES, 1, HALF)
    xc = xc_kernel.reshape(PIECES, 1, HALF)

    row = jnp.pad(atom_homes.astype(jnp.float32), (0, 128 - slots_here))
    home_rows = lax.all_to_all(
        jnp.broadcast_to(row[None, None], (groups, 8, 128)), "grid", 0, 0, tiled=True
    )[:, 0, :slots_here]
    wanted_rows = jnp.concatenate(
        [jnp.arange(natoms, dtype=jnp.float32), atom_homes.astype(jnp.float32)]
    )

    def chooser(which):
        held = jnp.pad(
            home_rows.reshape(groups, slots_here // 2, 2)[:, :, which],
            ((0, 0), (0, PAY_ROWS - slots_here // 2)),
            constant_values=-1.0,
        ).reshape(-1)
        return (wanted_rows[:, None] == held[None, :]).astype(jnp.bfloat16)

    even, odd = chooser(0), chooser(1)
    gauss, hart, even, odd, listed, slots, starts = lax.optimization_barrier(
        (gauss, hart, even, odd, listed, slots, starts)
    )

    rho, sent = density_call(order, homes, pieces, tiles, gauss, weights, xc)
    got = lax.all_to_all(sent, "grid", split_axis=0, concat_axis=0, tiled=True)
    all_coeffs, pot, scale, bound = potential_call(
        hart, got.reshape(groups * PAY_ROWS, 128), even, odd, weights, xc, rho, natoms
    )
    atom_dev = natoms // groups
    own_coeffs = lax.dynamic_slice_in_dim(all_coeffs, me * atom_dev, atom_dev, axis=0)
    ham_bound = PHI_MAX_SQ * 2048 * 0.05 * groups * bound[0, 0] * 1.01 + 1e-20

    scale_beside = lax.ppermute(scale, "grid", grid_perm(0, 0, 1))
    dense = ham_call(
        order,
        listed,
        slots,
        starts,
        pieces + beside,
        scale.reshape(2, 1, 4 * HALF),
        scale_beside.reshape(2, 1, 4 * HALF),
    )

    dense = dense.reshape(4, 4, tile_dev, BLK, BLK)
    factor = F16_TOP / ham_bound
    z_up, z_down = grid_perm(1, 0, 0), grid_perm(-1, 0, 0)
    x_up, x_down = grid_perm(0, 1, 0), grid_perm(0, -1, 0)
    half = BLK // 2
    upper = ring_sum([dense[d, :, :, :half] * factor for d in range(4)], "grid", z_up, z_down)
    lower = ring_sum([dense[:, d, :, half:] * factor for d in range(4)], "grid", x_up, x_down)
    z_perms = {d: grid_perm(d, 0, 0) for d in range(1, 4)}
    x_perms = {d: grid_perm(0, d, 0) for d in range(1, 4)}
    upper = direct_sum([upper[d] for d in range(4)], "grid", x_perms)
    lower = direct_sum([lower[d] for d in range(4)], "grid", z_perms)
    hamiltonian = jnp.concatenate([upper, lower], axis=1) * (ham_bound / F16_TOP)
    return (hamiltonian[None], own_coeffs[None], pot.reshape(1, -1))


def solution(mesh):
    placed = (
        P(("grid", "pert"), None),
        P(None, "grid"),
        P("grid"),
        P("grid"),
        P(),
        P(),
        P("pert", "grid", None, None),
        P("grid", None),
        P(),
        P("grid", None),
        P(),
    )
    return jax.shard_map(
        per_device,
        mesh=mesh,
        in_specs=placed,
        out_specs=(P("pert", "grid", None, None), P("pert", "grid", None), P("pert", "grid")),
        check_vma=False,
    )
```

```python
import jax
import jax.numpy as jnp
from jax import lax
from jax.experimental import pallas as pl
from jax.experimental.pallas import tpu as pltpu
from jax.sharding import PartitionSpec as P

SOFTEN = 0.25
ROOT_TWO = 1.4142135623730951
HALF = 512
PIECES = 8
CHUNKS = 5
BLK = 256
NB = 4
PHI_MAX_SQ = 36.0
KERNEL_MAX = 2.0
F16_TOP = 32000.0
PAY_ROWS = 24


def ring(shift):
    return [(i, (i + shift) % 4) for i in range(4)]


def grid_perm(dz, dx, dc):
    def at(z, x, c):
        return ((z % 4) * 4 + x % 4) * 2 + c

    return [
        (at(z, x, c), at(z + dz, x + dx, c ^ dc))
        for z in range(4)
        for x in range(4)
        for c in range(2)
    ]


def core_perm(shift, second):
    def at(z, x, c):
        return ((z % 4) * 4 + x % 4) * 2 + c

    pairs = []
    for z in range(4):
        for x in range(4):
            for c in range(2):
                along_z = (c == 0) != second
                there = at(z + shift, x, c) if along_z else at(z, x + shift, c)
                pairs.append((at(z, x, c), there))
    return pairs


def half_views(chunk_refs):
    views = []
    for ref in chunk_refs:
        if ref.shape[-1] == HALF:
            views.append((ref, None))
        else:
            views.extend((ref, h) for h in range(2))
    return views


def split3(x):
    first = x.astype(jnp.bfloat16)
    rest = x - first.astype(jnp.float32)
    second = rest.astype(jnp.bfloat16)
    third = (rest - second.astype(jnp.float32)).astype(jnp.bfloat16)
    return first, second, third


def density_body(order, where, *refs):
    chunks = refs[:CHUNKS]
    (tiles, table, weights, xc, rho, sent, pacc, block_out, held, dmat, tbuf, psem, dsem, tsem) = (
        refs[CHUNKS:]
    )
    for b in range(2):
        for t in range(16):
            pltpu.make_async_copy(
                tiles.at[where[b * 16 + t]],
                dmat.at[b, pl.ds((t // 4) * BLK, BLK), pl.ds((t % 4) * BLK, BLK)],
                dsem.at[b],
            ).start()
    for i, (ref, h) in enumerate(half_views(chunks)):
        view = ref if h is None else ref.at[:, pl.ds(h * HALF, HALF)]
        pltpu.make_async_copy(view, held.at[i], psem.at[i]).start()
    pltpu.make_async_copy(table.at[order[0]], tbuf.at[0], tsem.at[0]).start()
    pacc[...] = jnp.zeros_like(pacc)
    block_out[...] = jnp.zeros_like(block_out)
    for b in range(2):
        pltpu.make_async_copy(dmat.at[b], dmat.at[b], dsem.at[b]).wait()

    def step(i, top):
        slot = lax.rem(i, 2)

        @pl.when(i + 1 < PIECES)
        def _():
            pltpu.make_async_copy(
                table.at[order[i + 1]], tbuf.at[1 - slot], tsem.at[1 - slot]
            ).start()

        pi = order[i]
        b = pi // 4
        pltpu.make_async_copy(held.at[i], held.at[i], psem.at[i]).wait()
        piece = held[i]
        total = jnp.zeros((1, HALF), jnp.float32)
        for block in range(NB):
            rows = pl.ds(block * BLK, BLK)
            mixed = jnp.dot(dmat[b, rows, :], piece, preferred_element_type=jnp.float32)
            total = total + jnp.sum(
                mixed * held[i, rows, :].astype(jnp.float32), axis=0, keepdims=True
            )
        rho[pi] = total
        weighted = weights[pi] * total
        pltpu.make_async_copy(table.at[pi], tbuf.at[slot], tsem.at[slot]).wait()
        for block in range(8):
            rows = pl.ds(block * 128, 128)
            part = pacc[b, rows, :]
            for lane in range(HALF // 128):
                cols = slice(lane * 128, (lane + 1) * 128)
                part = part + tbuf[slot, rows, cols] * weighted[:, cols]
            pacc[b, rows, :] = part
        return jnp.maximum(top, jnp.abs(xc[pi] * total))

    top = lax.fori_loop(0, PIECES, step, jnp.zeros((1, HALF), jnp.float32))
    ones = jnp.ones((8, 128), jnp.bfloat16)
    for b in range(2):
        total = jnp.zeros((8, NB * BLK), jnp.float32)
        for term in split3(pacc[b]):
            total = total + lax.dot_general(
                ones, term, (((1,), (1,)), ((), ())), preferred_element_type=jnp.float32
            )
        for r in range(8):
            block_out[pl.ds(b * 8 + r, 1), :] = total[0:1, r * 128 : (r + 1) * 128]
    block_out[pl.ds(16, 1), :] = jnp.broadcast_to(jnp.max(top, axis=1, keepdims=True), (1, 128))
    for dest in range(32):
        sent[dest] = block_out[...]


def potential_body(table, got, even, odd, weights, xc, rho, coeffs, pot, scale, bound, *scratch):
    tbuf, column, tsem = scratch
    for i in range(2):
        pltpu.make_async_copy(table.at[i], tbuf.at[i], tsem.at[i]).start()
    first = jnp.zeros((even.shape[0], 128), jnp.float32)
    second = jnp.zeros((even.shape[0], 128), jnp.float32)
    for term in split3(got[...]):
        first = first + jnp.dot(even[...], term, preferred_element_type=jnp.float32)
        second = second + jnp.dot(odd[...], term, preferred_element_type=jnp.float32)
    summed = first[:, :64] + second[:, 64:]
    natoms = coeffs.shape[0]
    coeffs[...] = summed[:natoms]
    turned = summed[natoms:].T
    for k in range(32):
        column[pl.ds(k * 64, 64), :] = jnp.broadcast_to(turned[:, k : k + 1], (64, 128))
    top = jnp.zeros((1, 128), jnp.float32)
    for k in range(32):
        top = jnp.maximum(top, got[pl.ds(k * PAY_ROWS + 16, 1), :])
    heavy = jnp.max(jnp.sum(jnp.abs(summed[:natoms]), axis=1, keepdims=True), axis=0, keepdims=True)
    bound[...] = top + jnp.broadcast_to(heavy, (1, 128)) * (KERNEL_MAX * 16)

    def step(i, _):
        slot = lax.rem(i, 3)

        @pl.when(i + 2 < PIECES)
        def _():
            ahead = lax.rem(i + 2, 3)
            pltpu.make_async_copy(table.at[i + 2], tbuf.at[ahead], tsem.at[ahead]).start()

        base = (i // 4) * 1024
        pltpu.make_async_copy(table.at[i], tbuf.at[slot], tsem.at[slot]).wait()
        parts = [jnp.zeros((8, 128), jnp.float32) for _ in range(HALF // 128)]
        for block in range(16):
            factor = column[pl.ds(base + block * 64, 64), :]
            for lane in range(HALF // 128):
                prod = tbuf[slot, block * 64 : (block + 1) * 64, lane * 128 : (lane + 1) * 128]
                parts[lane] = parts[lane] + jnp.sum((prod * factor).reshape(8, 8, 128), axis=0)
        hartree = jnp.concatenate([jnp.sum(p, axis=0, keepdims=True) for p in parts], axis=1)
        potential = hartree + xc[i] * rho[i]
        pot[i] = potential
        scale[i] = weights[i] * potential
        return 0

    lax.fori_loop(0, PIECES, step, 0)


def ham_body(order, slots, place, *refs):
    chunks = refs[: 2 * CHUNKS]
    scale_mine, scale_beside, dense, held, rows_of, psem = refs[2 * CHUNKS :]
    core = place[0]
    for side in range(2):
        i = 0
        for ref in chunks[side * CHUNKS : (side + 1) * CHUNKS]:
            width = ref.shape[-1]
            pi = order[i]
            lanes = pl.ds(pl.multiple_of((pi % 4) * HALF, HALF), width)
            for half in range(2):
                at = (1 - core) if half else core
                pltpu.make_async_copy(
                    ref.at[:, half], held.at[side, pi // 4, at, :, :, lanes], psem
                ).start()
            i += width // HALF
    for b in range(2):
        rows_of[0, b] = scale_mine[b]
        rows_of[1, b] = scale_beside[b]

    def clear(s, _):
        dense[s] = jnp.zeros(dense.shape[1:], jnp.float32)
        return 0

    lax.fori_loop(0, dense.shape[0], clear, 0)
    pltpu.make_async_copy(held, held, psem).wait()

    def product(side, b, col):
        left = held[side, b, 0].reshape(2 * BLK, 4 * HALF)
        right = jnp.concatenate([held[side, b, core, col], held[side, b, 1 - core, col]], axis=0)
        right = (right.astype(jnp.float32) * rows_of[side, b]).astype(jnp.bfloat16)
        return lax.dot_general(
            left, right, (((1,), (1,)), ((), ())), preferred_element_type=jnp.float32
        )

    def step(n, _):
        side, b, cols = n // 4, (n // 2) % 2, (n % 2) * 2
        parts = [product(side, b, cols + k) for k in range(2)]
        for k in range(2):
            for row in range(NB):
                slot = slots[side * 32 + b * 16 + row * NB + cols + k]
                dense[slot] += parts[k][row * 128 : (row + 1) * 128]
        return 0

    lax.fori_loop(0, 8, step, 0)


def any_spec():
    return pl.BlockSpec(memory_space=pl.ANY)


def vmem_spec():
    return pl.BlockSpec(memory_space=pltpu.VMEM)


def smem_spec():
    return pl.BlockSpec(memory_space=pltpu.SMEM)


def density_call(order, where, chunks, tiles, table, weights, xc):
    nbasis = NB * BLK
    return pl.pallas_call(
        density_body,
        out_shape=(
            jax.ShapeDtypeStruct((PIECES, 1, HALF), jnp.float32),
            jax.ShapeDtypeStruct((32, PAY_ROWS, 128), jnp.float32),
        ),
        in_specs=[smem_spec(), smem_spec()] + [any_spec()] * (CHUNKS + 2) + [vmem_spec()] * 2,
        out_specs=(vmem_spec(), vmem_spec()),
        scratch_shapes=[
            pltpu.VMEM((2, nbasis, 128), jnp.float32),
            pltpu.VMEM((PAY_ROWS, 128), jnp.float32),
            pltpu.VMEM((PIECES, nbasis, HALF), jnp.bfloat16),
            pltpu.VMEM((2, nbasis, nbasis), jnp.bfloat16),
            pltpu.VMEM((2, nbasis, HALF), jnp.float32),
            pltpu.SemaphoreType.DMA((PIECES,)),
            pltpu.SemaphoreType.DMA((2,)),
            pltpu.SemaphoreType.DMA((2,)),
        ],
        compiler_params=pltpu.CompilerParams(vmem_limit_bytes=36 << 20),
        cost_estimate=pl.CostEstimate(
            flops=2 * 4096 * 1024 * 1024, bytes_accessed=32 << 20, transcendentals=0
        ),
        name="density",
    )(order, where, *chunks, tiles, table, weights, xc)


def potential_call(table, got, even, odd, weights, xc, rho, natoms):
    row = jax.ShapeDtypeStruct((PIECES, 1, HALF), jnp.float32)
    return pl.pallas_call(
        potential_body,
        out_shape=(
            jax.ShapeDtypeStruct((natoms, 64), jnp.float32),
            row,
            row,
            jax.ShapeDtypeStruct((1, 128), jnp.float32),
        ),
        in_specs=[any_spec()] + [vmem_spec()] * 6,
        out_specs=(vmem_spec(),) * 4,
        scratch_shapes=[
            pltpu.VMEM((3, NB * BLK, HALF), jnp.float32),
            pltpu.VMEM((2048, 128), jnp.float32),
            pltpu.SemaphoreType.DMA((3,)),
        ],
        compiler_params=pltpu.CompilerParams(vmem_limit_bytes=16 << 20),
        cost_estimate=pl.CostEstimate(
            flops=16 << 20, bytes_accessed=16 << 20, transcendentals=0
        ),
        name="potential",
    )(table, got, even, odd, weights, xc, rho)


def ham_call(order, slots, place, chunks, scale_mine, scale_beside):
    nbasis = NB * BLK
    return pl.pallas_call(
        ham_body,
        out_shape=jax.ShapeDtypeStruct((128, 128, BLK), jnp.float32),
        in_specs=[smem_spec()] * 3 + [any_spec()] * (2 * CHUNKS) + [vmem_spec()] * 2,
        out_specs=vmem_spec(),
        scratch_shapes=[
            pltpu.VMEM((2, 2, 2, NB, 128, 4 * HALF), jnp.bfloat16),
            pltpu.VMEM((2, 2, 1, 4 * HALF), jnp.float32),
            pltpu.SemaphoreType.DMA,
        ],
        compiler_params=pltpu.CompilerParams(vmem_limit_bytes=38 << 20),
        cost_estimate=pl.CostEstimate(
            flops=2 * 4096 * 1024 * 1024, bytes_accessed=32 << 20, transcendentals=0
        ),
        name="ham",
    )(
        order,
        slots,
        place,
        *[c.reshape(NB, 2, 128, c.shape[-1]) for c in chunks],
        scale_mine,
        scale_beside,
    )


def cast(x):
    return x.astype(jnp.float16)


def wide(x):
    return x.astype(jnp.float32)


def ring_sum(parts):
    half = parts[2].shape[0] // 2
    from_below = lax.ppermute(cast(parts[2][:half]), "grid", core_perm(1, False))
    from_above = lax.ppermute(cast(parts[2][half:]), "grid", core_perm(-1, False))
    up = jnp.concatenate([cast(parts[1][:half] + wide(from_below)), cast(parts[1][half:])])
    down = jnp.concatenate([cast(parts[3][:half]), cast(parts[3][half:] + wide(from_above))])
    got_below = lax.ppermute(up, "grid", core_perm(1, False))
    got_above = lax.ppermute(down, "grid", core_perm(-1, False))
    return parts[0] + wide(got_below) + wide(got_above)


def direct_sum(parts):
    total = parts[0]
    got = [lax.ppermute(cast(parts[d]), "grid", core_perm(d, True)) for d in (2, 1, 3)]
    for g in got:
        total = total + wide(g)
    return total


def per_device(
    basis_values,
    point_coords,
    point_weights,
    xc_kernel,
    gauss_widths,
    atom_coords,
    resp_density,
    tile_list,
    tile_home,
    atom_list,
    atom_home,
):
    groups = lax.axis_size("grid")
    me = lax.axis_index("grid")
    plane = lax.axis_index("pert")
    my_z, my_x, my_c = me // 8, (me // 2) % 4, me % 2
    tile_dev = resp_density.shape[1]
    neighbors = atom_list.shape[1]
    moments = gauss_widths.shape[0]
    natoms = atom_home.shape[0]
    ntiles = tile_home.shape[0]
    slots_here = 2 * neighbors

    own = basis_values.T
    below = lax.ppermute(own, "pert", ring(1))
    above = lax.ppermute(own, "pert", ring(3))
    far0 = lax.ppermute(below[:, :HALF], "pert", ring(1))
    far1 = lax.ppermute(above[:, HALF:], "pert", ring(3))
    chunks = [own, below, above, far0, far1]
    beside = [lax.ppermute(chunk, "grid", grid_perm(0, 0, 1)) for chunk in chunks]
    steps = jnp.array([0, 0, 3, 3, 1, 1, 2, 2], jnp.int32)
    halves = jnp.array([0, 1] * 4, jnp.int32)
    order = ((plane + steps) % 4) * 2 + halves

    tiles = lax.all_gather(resp_density[0], "grid", axis=0, tiled=True)
    wanted = tile_list.reshape(-1)
    tile_match = wanted[:, None] == jnp.arange(ntiles, dtype=jnp.int32)[None, :]
    homes = jnp.sum(jnp.where(tile_match, tile_home[None, :], 0), axis=1)
    homes_beside = lax.ppermute(homes, "grid", grid_perm(0, 0, 1))

    every_home = jnp.concatenate([homes, homes_beside])
    owner = every_home // tile_dev
    off_z = (owner // 8 - my_z) % 4
    off_x = ((owner // 2) % 4 - my_x) % 4
    ahead = jnp.where(my_c == 0, off_z * 4 + off_x, off_x * 4 + off_z)
    slots = ahead * (2 * tile_dev) + every_home % (2 * tile_dev)
    core_place = my_c.reshape(1).astype(jnp.int32)

    atom_match = atom_list[:, :, None] == jnp.arange(natoms, dtype=jnp.int32)
    atom_pos = jnp.sum(jnp.where(atom_match[None], atom_coords[:, None, None, :], 0.0), axis=3)
    atom_homes = jnp.sum(jnp.where(atom_match, atom_home, 0), axis=2).reshape(-1)
    delta = point_coords.reshape(3, 2, 4, 1, HALF) - atom_pos[:, :, None, :, None]
    dist_sq = (jnp.sum(delta * delta, axis=0) + SOFTEN).reshape(PIECES, neighbors, 1, HALF)
    spread = (2.0 * gauss_widths * gauss_widths)[None, None, :, None]
    erf_scale = (ROOT_TWO * gauss_widths)[None, None, :, None]
    gauss = jnp.exp(-dist_sq / spread).reshape(PIECES, neighbors * moments, HALF)
    distance = jnp.sqrt(dist_sq)
    hart = (lax.erf(distance / erf_scale) / distance).reshape(PIECES, neighbors * moments, HALF)
    weights = point_weights.reshape(PIECES, 1, HALF)
    xc = xc_kernel.reshape(PIECES, 1, HALF)

    row = jnp.pad(atom_homes.astype(jnp.float32), (0, 128 - slots_here))
    home_rows = lax.all_to_all(
        jnp.broadcast_to(row[None, None], (groups, 8, 128)), "grid", 0, 0, tiled=True
    )[:, 0, :slots_here]
    wanted_rows = jnp.concatenate(
        [jnp.arange(natoms, dtype=jnp.float32), atom_homes.astype(jnp.float32)]
    )

    def chooser(which):
        held = jnp.pad(
            home_rows.reshape(groups, slots_here // 2, 2)[:, :, which],
            ((0, 0), (0, PAY_ROWS - slots_here // 2)),
            constant_values=-1.0,
        ).reshape(-1)
        return (wanted_rows[:, None] == held[None, :]).astype(jnp.bfloat16)

    even, odd = chooser(0), chooser(1)
    gauss, hart, even, odd, slots = lax.optimization_barrier((gauss, hart, even, odd, slots))

    rho, sent = density_call(order, homes, chunks, tiles, gauss, weights, xc)
    got = lax.all_to_all(sent, "grid", split_axis=0, concat_axis=0, tiled=True)
    all_coeffs, pot, scale, bound = potential_call(
        hart, got.reshape(groups * PAY_ROWS, 128), even, odd, weights, xc, rho, natoms
    )
    atom_dev = natoms // groups
    own_coeffs = lax.dynamic_slice_in_dim(all_coeffs, me * atom_dev, atom_dev, axis=0)
    ham_bound = PHI_MAX_SQ * 2048 * 0.05 * groups * bound[0, 0] * 1.01 + 1e-20

    scale_beside = lax.ppermute(scale, "grid", grid_perm(0, 0, 1))
    dense = ham_call(
        order,
        slots,
        core_place,
        chunks + beside,
        scale.reshape(2, 1, 4 * HALF),
        scale_beside.reshape(2, 1, 4 * HALF),
    )

    dense = dense.reshape(4, 4, 2 * tile_dev, 128, BLK)
    factor = F16_TOP / ham_bound
    chip = direct_sum(list(ring_sum([dense[d] * factor for d in range(4)])))
    chip = chip.reshape(2, tile_dev, 128, BLK)
    first_core = my_c == 0
    keep = jnp.where(first_core, chip[0], chip[1])
    give = jnp.where(first_core, chip[1], chip[0])
    came = wide(lax.ppermute(cast(give), "grid", grid_perm(0, 0, 1)))
    hamiltonian = jnp.concatenate(
        [jnp.where(first_core, keep, came), jnp.where(first_core, came, keep)], axis=1
    ) * (ham_bound / F16_TOP)
    return (hamiltonian[None], own_coeffs[None], pot.reshape(1, -1))


def solution(mesh):
    placed = (
        P(("grid", "pert"), None),
        P(None, "grid"),
        P("grid"),
        P("grid"),
        P(),
        P(),
        P("pert", "grid", None, None),
        P("grid", None),
        P(),
        P("grid", None),
        P(),
    )
    return jax.shard_map(
        per_device,
        mesh=mesh,
        in_specs=placed,
        out_specs=(P("pert", "grid", None, None), P("pert", "grid", None), P("pert", "grid")),
        check_vma=False,
    )
```

```python
import jax
import jax.numpy as jnp
from jax import lax
from jax.experimental import pallas as pl
from jax.experimental.pallas import tpu as pltpu
from jax.sharding import PartitionSpec as P

SOFTEN = 0.25
ROOT_TWO = 1.4142135623730951
HALF = 512
PIECES = 8
CHUNKS = 8
SOURCES = 5
EARLY = 6
BLK = 256
NB = 4
PHI_MAX_SQ = 36.0
KERNEL_MAX = 2.0
F16_TOP = 32000.0
PAY_ROWS = 24


def ring(shift):
    return [(i, (i + shift) % 4) for i in range(4)]


def grid_perm(dz, dx, dc):
    def at(z, x, c):
        return ((z % 4) * 4 + x % 4) * 2 + c

    return [
        (at(z, x, c), at(z + dz, x + dx, c ^ dc))
        for z in range(4)
        for x in range(4)
        for c in range(2)
    ]


def core_perm(shift, second):
    def at(z, x, c):
        return ((z % 4) * 4 + x % 4) * 2 + c

    pairs = []
    for z in range(4):
        for x in range(4):
            for c in range(2):
                along_z = (c == 0) != second
                there = at(z + shift, x, c) if along_z else at(z, x + shift, c)
                pairs.append((at(z, x, c), there))
    return pairs


def split3(x):
    first = x.astype(jnp.bfloat16)
    rest = x - first.astype(jnp.float32)
    second = rest.astype(jnp.bfloat16)
    third = (rest - second.astype(jnp.float32)).astype(jnp.bfloat16)
    return first, second, third


def assemble_body(place, which, where, *refs):
    sources = [refs[:SOURCES], refs[SOURCES : 2 * SOURCES]]
    dmat, sem = refs[2 * SOURCES :]
    core = place[0]
    for side in range(2):
        half = (1 - core) if side else core

        def fetch(n, _, side=side, half=half):
            b, row, col = n // 16, (n // 4) % 4, n % 4
            target = dmat.at[
                b,
                pl.ds(pl.multiple_of(row * BLK + half * 128, 128), 128),
                pl.ds(pl.multiple_of(col * BLK, BLK), BLK),
            ]
            for k in range(SOURCES):

                @pl.when(which[side * 32 + n] == k)
                def _(k=k):
                    pltpu.make_async_copy(
                        sources[side][k].at[where[side * 32 + n]], target, sem
                    ).start()

            return 0

        lax.fori_loop(0, 32, fetch, 0)
    pltpu.make_async_copy(dmat, dmat, sem).wait()


def density_steps(order, first, count, chunks, dmat, table, weights, xc, rho, pacc, bufs, top):
    held, tbuf, psem, tsem = bufs
    for i in range(count):
        pltpu.make_async_copy(chunks[i], held.at[i], psem.at[i]).start()
    pltpu.make_async_copy(table.at[order[first]], tbuf.at[0], tsem.at[0]).start()

    def step(i, top):
        slot = lax.rem(i, 2)

        @pl.when(i + 1 < count)
        def _():
            pltpu.make_async_copy(
                table.at[order[first + i + 1]], tbuf.at[1 - slot], tsem.at[1 - slot]
            ).start()

        pi = order[first + i]
        b = pi // 4
        pltpu.make_async_copy(held.at[i], held.at[i], psem.at[i]).wait()
        piece = held[i]
        total = jnp.zeros((1, HALF), jnp.float32)
        for block in range(NB):
            rows = pl.ds(block * BLK, BLK)
            mixed = jnp.dot(dmat[b, rows, :], piece, preferred_element_type=jnp.float32)
            total = total + jnp.sum(
                mixed * held[i, rows, :].astype(jnp.float32), axis=0, keepdims=True
            )
        rho[pi] = total
        weighted = weights[pi] * total
        pltpu.make_async_copy(table.at[pi], tbuf.at[slot], tsem.at[slot]).wait()
        for block in range(8):
            rows = pl.ds(block * 128, 128)
            part = pacc[b, rows, :]
            for lane in range(HALF // 128):
                cols = slice(lane * 128, (lane + 1) * 128)
                part = part + tbuf[slot, rows, cols] * weighted[:, cols]
            pacc[b, rows, :] = part
        return jnp.maximum(top, jnp.abs(xc[pi] * total))

    return lax.fori_loop(0, count, step, top)


def density_first_body(order, *refs):
    chunks = refs[:EARLY]
    table, dmat, weights, xc, rho, pacc, top, *bufs = refs[EARLY:]
    pacc[...] = jnp.zeros_like(pacc)
    rho[...] = jnp.zeros_like(rho)
    top[...] = density_steps(
        order, 0, EARLY, chunks, dmat, table, weights, xc, rho, pacc, bufs,
        jnp.zeros((1, HALF), jnp.float32),
    )


def density_last_body(order, *refs):
    count = PIECES - EARLY
    chunks = refs[:count]
    (table, dmat, weights, xc, rho_in, pacc_in, top_in, rho, sent, pacc, block_out, *bufs) = (
        refs[count:]
    )
    pacc[...] = pacc_in[...]
    rho[...] = rho_in[...]
    block_out[...] = jnp.zeros_like(block_out)
    top = density_steps(
        order, EARLY, count, chunks, dmat, table, weights, xc, rho, pacc, bufs, top_in[...]
    )
    ones = jnp.ones((8, 128), jnp.bfloat16)
    for b in range(2):
        total = jnp.zeros((8, NB * BLK), jnp.float32)
        for term in split3(pacc[b]):
            total = total + lax.dot_general(
                ones, term, (((1,), (1,)), ((), ())), preferred_element_type=jnp.float32
            )
        for r in range(8):
            block_out[pl.ds(b * 8 + r, 1), :] = total[0:1, r * 128 : (r + 1) * 128]
    block_out[pl.ds(16, 1), :] = jnp.broadcast_to(jnp.max(top, axis=1, keepdims=True), (1, 128))
    for dest in range(32):
        sent[dest] = block_out[...]


def potential_body(table, got, even, odd, weights, xc, rho, coeffs, pot, scale, bound, *scratch):
    tbuf, column, tsem = scratch
    for i in range(2):
        pltpu.make_async_copy(table.at[i], tbuf.at[i], tsem.at[i]).start()
    first = jnp.zeros((even.shape[0], 128), jnp.float32)
    second = jnp.zeros((even.shape[0], 128), jnp.float32)
    for term in split3(got[...]):
        first = first + jnp.dot(even[...], term, preferred_element_type=jnp.float32)
        second = second + jnp.dot(odd[...], term, preferred_element_type=jnp.float32)
    summed = first[:, :64] + second[:, 64:]
    natoms = coeffs.shape[0]
    coeffs[...] = summed[:natoms]
    turned = summed[natoms:].T
    for k in range(32):
        column[pl.ds(k * 64, 64), :] = jnp.broadcast_to(turned[:, k : k + 1], (64, 128))
    top = jnp.zeros((1, 128), jnp.float32)
    for k in range(32):
        top = jnp.maximum(top, got[pl.ds(k * PAY_ROWS + 16, 1), :])
    heavy = jnp.max(jnp.sum(jnp.abs(summed[:natoms]), axis=1, keepdims=True), axis=0, keepdims=True)
    bound[...] = top + jnp.broadcast_to(heavy, (1, 128)) * (KERNEL_MAX * 16)

    def step(i, _):
        slot = lax.rem(i, 3)

        @pl.when(i + 2 < PIECES)
        def _():
            ahead = lax.rem(i + 2, 3)
            pltpu.make_async_copy(table.at[i + 2], tbuf.at[ahead], tsem.at[ahead]).start()

        base = (i // 4) * 1024
        pltpu.make_async_copy(table.at[i], tbuf.at[slot], tsem.at[slot]).wait()
        parts = [jnp.zeros((8, 128), jnp.float32) for _ in range(HALF // 128)]
        for block in range(16):
            factor = column[pl.ds(base + block * 64, 64), :]
            for lane in range(HALF // 128):
                prod = tbuf[slot, block * 64 : (block + 1) * 64, lane * 128 : (lane + 1) * 128]
                parts[lane] = parts[lane] + jnp.sum((prod * factor).reshape(8, 8, 128), axis=0)
        hartree = jnp.concatenate([jnp.sum(p, axis=0, keepdims=True) for p in parts], axis=1)
        potential = hartree + xc[i] * rho[i]
        pot[i] = potential
        scale[i] = weights[i] * potential
        return 0

    lax.fori_loop(0, PIECES, step, 0)


def ham_body(order, slots, place, *refs):
    chunks = refs[: 2 * CHUNKS]
    scale_mine, scale_beside, *rest = refs[2 * CHUNKS :]
    outs, (dense, held, rows_of, psem, osem) = rest[:4], rest[4:]
    core = place[0]
    for side in range(2):
        i = 0
        for ref in chunks[side * CHUNKS : (side + 1) * CHUNKS]:
            width = ref.shape[-1]
            pi = order[i]
            lanes = pl.ds(pl.multiple_of((pi % 4) * HALF, HALF), width)
            for half in range(2):
                at = (1 - core) if half else core
                pltpu.make_async_copy(
                    ref.at[:, half], held.at[side, pi // 4, at, :, :, lanes], psem
                ).start()
            i += width // HALF
    for b in range(2):
        rows_of[0, b] = scale_mine[b]
        rows_of[1, b] = scale_beside[b]

    def clear(s, _):
        dense[s] = jnp.zeros(dense.shape[1:], jnp.float32)
        return 0

    lax.fori_loop(0, dense.shape[0], clear, 0)
    pltpu.make_async_copy(held, held, psem).wait()

    def product(side, b, col):
        left = held[side, b, 0].reshape(2 * BLK, 4 * HALF)
        right = jnp.concatenate([held[side, b, core, col], held[side, b, 1 - core, col]], axis=0)
        right = (right.astype(jnp.float32) * rows_of[side, b]).astype(jnp.bfloat16)
        return lax.dot_general(
            left, right, (((1,), (1,)), ((), ())), preferred_element_type=jnp.float32
        )

    def step(n, _):
        side, b, cols = n // 4, (n // 2) % 2, (n % 2) * 2
        parts = [product(side, b, cols + k) for k in range(2)]
        for k in range(2):
            for row in range(NB):
                slot = slots[side * 32 + b * 16 + row * NB + cols + k]
                dense[slot] += parts[k][row * 128 : (row + 1) * 128]
        return 0

    lax.fori_loop(0, 8, step, 0)
    for d in range(4):
        pltpu.make_async_copy(dense.at[pl.ds(d * 32, 32)], outs[d], osem.at[d]).start()
    for d in range(4):
        pltpu.make_async_copy(dense.at[pl.ds(d * 32, 32)], outs[d], osem.at[d]).wait()


def any_spec():
    return pl.BlockSpec(memory_space=pl.ANY)


def vmem_spec():
    return pl.BlockSpec(memory_space=pltpu.VMEM)


def smem_spec():
    return pl.BlockSpec(memory_space=pltpu.SMEM)


def assemble_call(place, which, where, sources):
    nbasis = NB * BLK
    return pl.pallas_call(
        assemble_body,
        out_shape=jax.ShapeDtypeStruct((2, nbasis, nbasis), jnp.bfloat16),
        in_specs=[smem_spec()] * 3 + [any_spec()] * (2 * SOURCES),
        out_specs=vmem_spec(),
        scratch_shapes=[pltpu.SemaphoreType.DMA],
        compiler_params=pltpu.CompilerParams(vmem_limit_bytes=8 << 20),
        cost_estimate=pl.CostEstimate(flops=0, bytes_accessed=8 << 20, transcendentals=0),
        name="assemble",
    )(place, which, where, *sources)


def density_buffers(count):
    nbasis = NB * BLK
    return [
        pltpu.VMEM((count, nbasis, HALF), jnp.bfloat16),
        pltpu.VMEM((2, nbasis, HALF), jnp.float32),
        pltpu.SemaphoreType.DMA((count,)),
        pltpu.SemaphoreType.DMA((2,)),
    ]


def density_cost(count):
    return pl.CostEstimate(
        flops=2 * count * HALF * 1024 * 1024, bytes_accessed=count * (3 << 20), transcendentals=0
    )


def density_first(order, chunks, table, dmat, weights, xc):
    return pl.pallas_call(
        density_first_body,
        out_shape=(
            jax.ShapeDtypeStruct((PIECES, 1, HALF), jnp.float32),
            jax.ShapeDtypeStruct((2, NB * BLK, 128), jnp.float32),
            jax.ShapeDtypeStruct((1, HALF), jnp.float32),
        ),
        in_specs=[smem_spec()] + [any_spec()] * (EARLY + 1) + [vmem_spec()] * 3,
        out_specs=(vmem_spec(),) * 3,
        scratch_shapes=density_buffers(EARLY),
        compiler_params=pltpu.CompilerParams(vmem_limit_bytes=30 << 20),
        cost_estimate=density_cost(EARLY),
        name="density_first",
    )(order, *chunks, table, dmat, weights, xc)


def density_last(order, chunks, table, dmat, weights, xc, rho, pacc, top):
    count = PIECES - EARLY
    return pl.pallas_call(
        density_last_body,
        out_shape=(
            jax.ShapeDtypeStruct((PIECES, 1, HALF), jnp.float32),
            jax.ShapeDtypeStruct((32, PAY_ROWS, 128), jnp.float32),
        ),
        in_specs=[smem_spec()] + [any_spec()] * (count + 1) + [vmem_spec()] * 6,
        out_specs=(vmem_spec(),) * 2,
        scratch_shapes=[
            pltpu.VMEM((2, NB * BLK, 128), jnp.float32),
            pltpu.VMEM((PAY_ROWS, 128), jnp.float32),
        ]
        + density_buffers(count),
        compiler_params=pltpu.CompilerParams(vmem_limit_bytes=24 << 20),
        cost_estimate=density_cost(count),
        name="density_last",
    )(order, *chunks, table, dmat, weights, xc, rho, pacc, top)


def potential_call(table, got, even, odd, weights, xc, rho, natoms):
    row = jax.ShapeDtypeStruct((PIECES, 1, HALF), jnp.float32)
    return pl.pallas_call(
        potential_body,
        out_shape=(
            jax.ShapeDtypeStruct((natoms, 64), jnp.float32),
            row,
            row,
            jax.ShapeDtypeStruct((1, 128), jnp.float32),
        ),
        in_specs=[any_spec()] + [vmem_spec()] * 6,
        out_specs=(vmem_spec(),) * 4,
        scratch_shapes=[
            pltpu.VMEM((3, NB * BLK, HALF), jnp.float32),
            pltpu.VMEM((2048, 128), jnp.float32),
            pltpu.SemaphoreType.DMA((3,)),
        ],
        compiler_params=pltpu.CompilerParams(vmem_limit_bytes=16 << 20),
        cost_estimate=pl.CostEstimate(
            flops=16 << 20, bytes_accessed=16 << 20, transcendentals=0
        ),
        name="potential",
    )(table, got, even, odd, weights, xc, rho)


def ham_call(order, slots, place, chunks, scale_mine, scale_beside):
    nbasis = NB * BLK
    return pl.pallas_call(
        ham_body,
        out_shape=(jax.ShapeDtypeStruct((32, 128, BLK), jnp.float32),) * 4,
        in_specs=[smem_spec()] * 3 + [any_spec()] * (2 * CHUNKS) + [vmem_spec()] * 2,
        out_specs=(any_spec(),) * 4,
        scratch_shapes=[
            pltpu.VMEM((128, 128, BLK), jnp.float32),
            pltpu.VMEM((2, 2, 2, NB, 128, 4 * HALF), jnp.bfloat16),
            pltpu.VMEM((2, 2, 1, 4 * HALF), jnp.float32),
            pltpu.SemaphoreType.DMA,
            pltpu.SemaphoreType.DMA((4,)),
        ],
        compiler_params=pltpu.CompilerParams(vmem_limit_bytes=38 << 20),
        cost_estimate=pl.CostEstimate(
            flops=2 * 4096 * 1024 * 1024, bytes_accessed=32 << 20, transcendentals=0
        ),
        name="ham",
    )(
        order,
        slots,
        place,
        *[c.reshape(NB, 2, 128, c.shape[-1]) for c in chunks],
        scale_mine,
        scale_beside,
    )


def cast(x):
    return x.astype(jnp.float16)


def wide(x):
    return x.astype(jnp.float32)


def ring_sum(parts, factor):
    half = parts[2].shape[0] // 2
    from_below = lax.ppermute(cast(parts[2][:half] * factor), "grid", core_perm(1, False))
    from_above = lax.ppermute(cast(parts[2][half:] * factor), "grid", core_perm(-1, False))
    zero = jnp.zeros_like(from_below)
    up = cast(parts[1] * factor + wide(jnp.concatenate([from_below, zero])))
    down = cast(parts[3] * factor + wide(jnp.concatenate([zero, from_above])))
    got_below = lax.ppermute(up, "grid", core_perm(1, False))
    got_above = lax.ppermute(down, "grid", core_perm(-1, False))
    return parts[0] * factor + wide(got_below) + wide(got_above)


def direct_sum(parts):
    total = parts[0]
    got = [lax.ppermute(cast(parts[d]), "grid", core_perm(d, True)) for d in (2, 1, 3)]
    for g in got:
        total = total + wide(g)
    return total


def per_device(
    basis_values,
    point_coords,
    point_weights,
    xc_kernel,
    gauss_widths,
    atom_coords,
    resp_density,
    tile_list,
    tile_home,
    atom_list,
    atom_home,
):
    groups = lax.axis_size("grid")
    me = lax.axis_index("grid")
    plane = lax.axis_index("pert")
    my_z, my_x, my_c = me // 8, (me // 2) % 4, me % 2
    tile_dev = resp_density.shape[1]
    neighbors = atom_list.shape[1]
    moments = gauss_widths.shape[0]
    natoms = atom_home.shape[0]
    ntiles = tile_home.shape[0]
    slots_here = 2 * neighbors

    own0, own1 = basis_values[:HALF].T, basis_values[HALF:].T
    below0 = lax.ppermute(own0, "pert", ring(1))
    above1 = lax.ppermute(own1, "pert", ring(3))
    below1 = lax.ppermute(own1, "pert", ring(1))
    above0 = lax.ppermute(own0, "pert", ring(3))
    steps = jnp.array([0, 0, 3, 3, 1, 1, 2, 2], jnp.int32)
    halves = jnp.array([0, 1] * 4, jnp.int32)
    order = ((plane + steps) % 4) * 2 + halves

    swap = grid_perm(0, 0, 1)
    first_core = my_c == 0
    top_half, low_half = resp_density[0, :, :128], resp_density[0, :, 128:]
    kept = jnp.where(first_core, top_half, low_half)
    came = lax.ppermute(jnp.where(first_core, low_half, top_half), "grid", swap)
    base = jnp.concatenate(
        [jnp.where(first_core, kept, came), jnp.where(first_core, came, kept)], axis=0
    )
    ring_tiles = [lax.ppermute(base, "grid", core_perm(-d, False)) for d in (1, 2, 3)]

    wanted = tile_list.reshape(-1)
    tile_match = wanted[:, None] == jnp.arange(ntiles, dtype=jnp.int32)[None, :]
    homes = jnp.sum(jnp.where(tile_match, tile_home[None, :], 0), axis=1)
    homes_beside = lax.ppermute(homes, "grid", grid_perm(0, 0, 1))

    every_home = jnp.concatenate([homes, homes_beside])
    owner = every_home // tile_dev
    off_z = (owner // 8 - my_z) % 4
    off_x = ((owner // 2) % 4 - my_x) % 4
    ahead = jnp.where(my_c == 0, off_z * 4 + off_x, off_x * 4 + off_z)
    slots = ahead * (2 * tile_dev) + every_home % (2 * tile_dev)
    core_place = my_c.reshape(1).astype(jnp.int32)

    my_owner = homes // tile_dev
    to_z = (my_owner // 8 - my_z) % 4
    to_x = ((my_owner // 2) % 4 - my_x) % 4
    in_chip = homes % (2 * tile_dev)

    def found(one, two):
        source = jnp.where(two == 2, 2 + one // 2, jnp.where(two == 3, 4, two))
        return source, jnp.where(two == 2, one % 2, one) * (2 * tile_dev) + in_chip

    own_first = jnp.where(first_core, to_z, to_x)
    own_second = jnp.where(first_core, to_x, to_z)
    which_own, where_own = found(own_first, own_second)
    which_other, where_other = found(own_second, own_first)
    which = jnp.concatenate([which_own, which_other])
    where = jnp.concatenate([where_own, where_other])

    atom_match = atom_list[:, :, None] == jnp.arange(natoms, dtype=jnp.int32)
    atom_pos = jnp.sum(jnp.where(atom_match[None], atom_coords[:, None, None, :], 0.0), axis=3)
    atom_homes = jnp.sum(jnp.where(atom_match, atom_home, 0), axis=2).reshape(-1)
    delta = point_coords.reshape(3, 2, 4, 1, HALF) - atom_pos[:, :, None, :, None]
    dist_sq = (jnp.sum(delta * delta, axis=0) + SOFTEN).reshape(PIECES, neighbors, 1, HALF)
    spread = (2.0 * gauss_widths * gauss_widths)[None, None, :, None]
    erf_scale = (ROOT_TWO * gauss_widths)[None, None, :, None]
    gauss = jnp.exp(-dist_sq / spread).reshape(PIECES, neighbors * moments, HALF)
    distance = jnp.sqrt(dist_sq)
    hart = (lax.erf(distance / erf_scale) / distance).reshape(PIECES, neighbors * moments, HALF)
    weights = point_weights.reshape(PIECES, 1, HALF)
    xc = xc_kernel.reshape(PIECES, 1, HALF)

    ring_tiles, gauss = lax.optimization_barrier((ring_tiles, gauss))
    stored = jnp.concatenate([base] + ring_tiles, axis=0)
    ahead_tiles = lax.ppermute(stored, "grid", core_perm(-1, True))
    behind_tiles = lax.ppermute(stored, "grid", core_perm(1, True))

    row = jnp.pad(atom_homes.astype(jnp.float32), (0, 128 - slots_here))
    home_rows = lax.all_to_all(
        jnp.broadcast_to(row[None, None], (groups, 8, 128)), "grid", 0, 0, tiled=True
    )[:, 0, :slots_here]
    wanted_rows = jnp.concatenate(
        [jnp.arange(natoms, dtype=jnp.float32), atom_homes.astype(jnp.float32)]
    )

    def chooser(which):
        held = jnp.pad(
            home_rows.reshape(groups, slots_here // 2, 2)[:, :, which],
            ((0, 0), (0, PAY_ROWS - slots_here // 2)),
            constant_values=-1.0,
        ).reshape(-1)
        return (wanted_rows[:, None] == held[None, :]).astype(jnp.bfloat16)

    even, odd = chooser(0), chooser(1)
    below0, above1, hart = lax.optimization_barrier((below0, above1, hart))
    far0 = lax.ppermute(below0, "pert", ring(1))
    far1 = lax.ppermute(above1, "pert", ring(3))
    chunks = [own0, own1, below0, below1, above0, above1, far0, far1]
    beside = [lax.ppermute(chunk, "grid", swap) for chunk in chunks]

    ahead_tiles, behind_tiles, even, odd, slots = lax.optimization_barrier(
        (ahead_tiles, behind_tiles, even, odd, slots)
    )
    rows2 = 4 * tile_dev
    far_tiles0 = lax.ppermute(ahead_tiles[:rows2], "grid", core_perm(-1, True))
    far_tiles1 = lax.ppermute(behind_tiles[rows2:], "grid", core_perm(1, True))
    sources = [stored, ahead_tiles, far_tiles0, far_tiles1, behind_tiles]
    sources = sources + [lax.ppermute(s, "grid", swap) for s in sources]
    dmat = assemble_call(core_place, which, where, sources)

    rho, pacc, top = density_first(order, chunks[:EARLY], gauss, dmat, weights, xc)
    rho, sent = density_last(order, chunks[EARLY:], gauss, dmat, weights, xc, rho, pacc, top)
    got = lax.all_to_all(sent, "grid", split_axis=0, concat_axis=0, tiled=True)
    all_coeffs, pot, scale, bound = potential_call(
        hart, got.reshape(groups * PAY_ROWS, 128), even, odd, weights, xc, rho, natoms
    )
    atom_dev = natoms // groups
    own_coeffs = lax.dynamic_slice_in_dim(all_coeffs, me * atom_dev, atom_dev, axis=0)
    ham_bound = PHI_MAX_SQ * 2048 * 0.05 * groups * bound[0, 0] * 1.01 + 1e-20

    scale_beside = lax.ppermute(scale, "grid", swap)
    dense = ham_call(
        order,
        slots,
        core_place,
        chunks + beside,
        scale.reshape(2, 1, 4 * HALF),
        scale_beside.reshape(2, 1, 4 * HALF),
    )

    factor = F16_TOP / ham_bound
    dense = [d.reshape(4, 2 * tile_dev, 128, BLK) for d in dense]
    chip = direct_sum(list(ring_sum(dense, factor)))
    chip = chip.reshape(2, tile_dev, 128, BLK)
    keep = jnp.where(first_core, chip[0], chip[1])
    give = jnp.where(first_core, chip[1], chip[0])
    came = wide(lax.ppermute(cast(give), "grid", swap))
    hamiltonian = jnp.concatenate(
        [jnp.where(first_core, keep, came), jnp.where(first_core, came, keep)], axis=1
    ) * (ham_bound / F16_TOP)
    return (hamiltonian[None], own_coeffs[None], pot.reshape(1, -1))


def solution(mesh):
    placed = (
        P(("grid", "pert"), None),
        P(None, "grid"),
        P("grid"),
        P("grid"),
        P(),
        P(),
        P("pert", "grid", None, None),
        P("grid", None),
        P(),
        P("grid", None),
        P(),
    )
    return jax.shard_map(
        per_device,
        mesh=mesh,
        in_specs=placed,
        out_specs=(P("pert", "grid", None, None), P("pert", "grid", None), P("pert", "grid")),
        check_vma=False,
    )
```

```python
import jax
import jax.numpy as jnp
from jax import lax
from jax.experimental import pallas as pl
from jax.experimental.pallas import tpu as pltpu
from jax.sharding import PartitionSpec as P


SOFTEN = 0.25
ROOT_TWO = 1.4142135623730951
HALF = 512
PIECES = 8
CHUNKS = 8
SOURCES = 5
EARLY = 6
BLK = 256
NB = 4
PHI_MAX_SQ = 36.0
KERNEL_MAX = 2.0
F16_TOP = 32000.0
PAY_ROWS = 24


def ring(shift):
    return [(i, (i + shift) % 4) for i in range(4)]


def grid_perm(dz, dx, dc):
    def at(z, x, c):
        return ((z % 4) * 4 + x % 4) * 2 + c

    return [
        (at(z, x, c), at(z + dz, x + dx, c ^ dc))
        for z in range(4)
        for x in range(4)
        for c in range(2)
    ]


def core_perm(shift, second):
    def at(z, x, c):
        return ((z % 4) * 4 + x % 4) * 2 + c

    pairs = []
    for z in range(4):
        for x in range(4):
            for c in range(2):
                along_z = (c == 0) != second
                there = at(z + shift, x, c) if along_z else at(z, x + shift, c)
                pairs.append((at(z, x, c), there))
    return pairs


def split3(x):
    first = x.astype(jnp.bfloat16)
    rest = x - first.astype(jnp.float32)
    second = rest.astype(jnp.bfloat16)
    third = (rest - second.astype(jnp.float32)).astype(jnp.bfloat16)
    return first, second, third


def fetch_tiles(core, which, where, sources, dmat, sem):
    for side in range(2):
        half = (1 - core) if side else core

        def fetch(n, _, side=side, half=half):
            b, row, col = n // 16, (n // 4) % 4, n % 4
            target = dmat.at[
                b,
                pl.ds(pl.multiple_of(row * BLK + half * 128, 128), 128),
                pl.ds(pl.multiple_of(col * BLK, BLK), BLK),
            ]
            for k in range(SOURCES):

                @pl.when(which[side * 32 + n] == k)
                def _(k=k):
                    pltpu.make_async_copy(
                        sources[side * SOURCES + k].at[where[side * 32 + n]], target, sem
                    ).start()

            return 0

        lax.fori_loop(0, 32, fetch, 0)


def density_steps(order, first, count, chunks, dmat, table, weights, xc, rho, pacc, bufs, top):
    held, tbuf, psem, tsem = bufs
    for i in range(count):
        pltpu.make_async_copy(chunks[i], held.at[i], psem.at[i]).start()
    pltpu.make_async_copy(table.at[order[first]], tbuf.at[0], tsem.at[0]).start()

    def step(i, top):
        slot = lax.rem(i, 2)

        @pl.when(i + 1 < count)
        def _():
            pltpu.make_async_copy(
                table.at[order[first + i + 1]], tbuf.at[1 - slot], tsem.at[1 - slot]
            ).start()

        pi = order[first + i]
        b = pi // 4
        pltpu.make_async_copy(held.at[i], held.at[i], psem.at[i]).wait()
        piece = held[i]
        total = jnp.zeros((1, HALF), jnp.float32)
        for block in range(NB):
            rows = pl.ds(block * BLK, BLK)
            mixed = jnp.dot(dmat[b, rows, :], piece, preferred_element_type=jnp.float32)
            total = total + jnp.sum(
                mixed * held[i, rows, :].astype(jnp.float32), axis=0, keepdims=True
            )
        rho[pi] = total
        weighted = weights[pi] * total
        pltpu.make_async_copy(table.at[pi], tbuf.at[slot], tsem.at[slot]).wait()
        for block in range(8):
            rows = pl.ds(block * 128, 128)
            part = pacc[b, rows, :]
            for lane in range(HALF // 128):
                cols = slice(lane * 128, (lane + 1) * 128)
                part = part + tbuf[slot, rows, cols] * weighted[:, cols]
            pacc[b, rows, :] = part
        return jnp.maximum(top, jnp.abs(xc[pi] * total))

    return lax.fori_loop(0, count, step, top)


def density_first_body(order, place, which, where, *refs):
    chunks = refs[:EARLY]
    sources = refs[EARLY : EARLY + 2 * SOURCES]
    table, weights, xc, rho, pacc, top, dmat, sem, *bufs = refs[EARLY + 2 * SOURCES :]
    fetch_tiles(place[0], which, where, sources, dmat, sem)
    pacc[...] = jnp.zeros_like(pacc)
    rho[...] = jnp.zeros_like(rho)
    pltpu.make_async_copy(dmat, dmat, sem).wait()
    top[...] = density_steps(
        order, 0, EARLY, chunks, dmat, table, weights, xc, rho, pacc, bufs,
        jnp.zeros((1, HALF), jnp.float32),
    )


def density_last_body(order, *refs):
    count = PIECES - EARLY
    chunks = refs[:count]
    (table, dmat, weights, xc, rho_in, pacc_in, top_in, rho, sent, pacc, block_out, *bufs) = (
        refs[count:]
    )
    pacc[...] = pacc_in[...]
    rho[...] = rho_in[...]
    block_out[...] = jnp.zeros_like(block_out)
    top = density_steps(
        order, EARLY, count, chunks, dmat, table, weights, xc, rho, pacc, bufs, top_in[...]
    )
    ones = jnp.ones((8, 128), jnp.bfloat16)
    for b in range(2):
        total = jnp.zeros((8, NB * BLK), jnp.float32)
        for term in split3(pacc[b]):
            total = total + lax.dot_general(
                ones, term, (((1,), (1,)), ((), ())), preferred_element_type=jnp.float32
            )
        for r in range(8):
            block_out[pl.ds(b * 8 + r, 1), :] = total[0:1, r * 128 : (r + 1) * 128]
    block_out[pl.ds(16, 1), :] = jnp.broadcast_to(jnp.max(top, axis=1, keepdims=True), (1, 128))
    for dest in range(32):
        sent[dest] = block_out[...]


def potential_body(table, got, even, odd, weights, xc, rho, coeffs, pot, scale, bound, *scratch):
    tbuf, column, tsem = scratch
    for i in range(2):
        pltpu.make_async_copy(table.at[i], tbuf.at[i], tsem.at[i]).start()
    first = jnp.zeros((even.shape[0], 128), jnp.float32)
    second = jnp.zeros((even.shape[0], 128), jnp.float32)
    for term in split3(got[...]):
        first = first + jnp.dot(even[...], term, preferred_element_type=jnp.float32)
        second = second + jnp.dot(odd[...], term, preferred_element_type=jnp.float32)
    summed = first[:, :64] + second[:, 64:]
    natoms = coeffs.shape[0]
    coeffs[...] = summed[:natoms]
    turned = summed[natoms:].T
    for k in range(32):
        column[pl.ds(k * 64, 64), :] = jnp.broadcast_to(turned[:, k : k + 1], (64, 128))
    top = jnp.zeros((1, 128), jnp.float32)
    for k in range(32):
        top = jnp.maximum(top, got[pl.ds(k * PAY_ROWS + 16, 1), :])
    heavy = jnp.max(jnp.sum(jnp.abs(summed[:natoms]), axis=1, keepdims=True), axis=0, keepdims=True)
    bound[...] = top + jnp.broadcast_to(heavy, (1, 128)) * (KERNEL_MAX * 16)

    def step(i, _):
        slot = lax.rem(i, 3)

        @pl.when(i + 2 < PIECES)
        def _():
            ahead = lax.rem(i + 2, 3)
            pltpu.make_async_copy(table.at[i + 2], tbuf.at[ahead], tsem.at[ahead]).start()

        base = (i // 4) * 1024
        pltpu.make_async_copy(table.at[i], tbuf.at[slot], tsem.at[slot]).wait()
        parts = [jnp.zeros((8, 128), jnp.float32) for _ in range(HALF // 128)]
        for block in range(16):
            factor = column[pl.ds(base + block * 64, 64), :]
            for lane in range(HALF // 128):
                prod = tbuf[slot, block * 64 : (block + 1) * 64, lane * 128 : (lane + 1) * 128]
                parts[lane] = parts[lane] + jnp.sum((prod * factor).reshape(8, 8, 128), axis=0)
        hartree = jnp.concatenate([jnp.sum(p, axis=0, keepdims=True) for p in parts], axis=1)
        potential = hartree + xc[i] * rho[i]
        pot[i] = potential
        scale[i] = weights[i] * potential
        return 0

    lax.fori_loop(0, PIECES, step, 0)


def ham_body(order, slots, place, *refs):
    chunks = refs[: 2 * CHUNKS]
    scale_mine, scale_beside, *rest = refs[2 * CHUNKS :]
    outs, (dense, held, rows_of, psem, osem) = rest[:4], rest[4:]
    core = place[0]
    for side in range(2):
        i = 0
        for ref in chunks[side * CHUNKS : (side + 1) * CHUNKS]:
            width = ref.shape[-1]
            pi = order[i]
            lanes = pl.ds(pl.multiple_of((pi % 4) * HALF, HALF), width)
            for half in range(2):
                at = (1 - core) if half else core
                pltpu.make_async_copy(
                    ref.at[:, half], held.at[side, pi // 4, at, :, :, lanes], psem
                ).start()
            i += width // HALF
    for b in range(2):
        rows_of[0, b] = scale_mine[b]
        rows_of[1, b] = scale_beside[b]

    def clear(s, _):
        dense[s] = jnp.zeros(dense.shape[1:], jnp.float32)
        return 0

    lax.fori_loop(0, dense.shape[0], clear, 0)
    pltpu.make_async_copy(held, held, psem).wait()

    def product(side, b, col):
        left = held[side, b, 0].reshape(2 * BLK, 4 * HALF)
        right = jnp.concatenate([held[side, b, core, col], held[side, b, 1 - core, col]], axis=0)
        right = (right.astype(jnp.float32) * rows_of[side, b]).astype(jnp.bfloat16)
        return lax.dot_general(
            left, right, (((1,), (1,)), ((), ())), preferred_element_type=jnp.float32
        )

    def step(n, _):
        side, b, cols = n // 4, (n // 2) % 2, (n % 2) * 2
        parts = [product(side, b, cols + k) for k in range(2)]
        for k in range(2):
            for row in range(NB):
                slot = slots[side * 32 + b * 16 + row * NB + cols + k]
                dense[slot] += parts[k][row * 128 : (row + 1) * 128]
        return 0

    lax.fori_loop(0, 8, step, 0)
    for d in range(4):
        pltpu.make_async_copy(dense.at[pl.ds(d * 32, 32)], outs[d], osem.at[d]).start()
    for d in range(4):
        pltpu.make_async_copy(dense.at[pl.ds(d * 32, 32)], outs[d], osem.at[d]).wait()


def any_spec():
    return pl.BlockSpec(memory_space=pltpu.HBM)


def vmem_spec():
    return pl.BlockSpec(memory_space=pltpu.VMEM)


def smem_spec():
    return pl.BlockSpec(memory_space=pltpu.SMEM)


def density_buffers(count):
    nbasis = NB * BLK
    return [
        pltpu.VMEM((count, nbasis, HALF), jnp.bfloat16),
        pltpu.VMEM((2, nbasis, HALF), jnp.float32),
        pltpu.SemaphoreType.DMA((count,)),
        pltpu.SemaphoreType.DMA((2,)),
    ]


def density_cost(count):
    return pl.CostEstimate(
        flops=2 * count * HALF * 1024 * 1024, bytes_accessed=count * (3 << 20), transcendentals=0
    )


def density_first(order, place, which, where, chunks, sources, table, weights, xc):
    nbasis = NB * BLK
    return pl.pallas_call(
        density_first_body,
        out_shape=(
            jax.ShapeDtypeStruct((PIECES, 1, HALF), jnp.float32),
            jax.ShapeDtypeStruct((2, nbasis, 128), jnp.float32),
            jax.ShapeDtypeStruct((1, HALF), jnp.float32),
            jax.ShapeDtypeStruct((2, nbasis, nbasis), jnp.bfloat16),
        ),
        in_specs=[smem_spec()] * 4
        + [any_spec()] * (EARLY + 2 * SOURCES + 1)
        + [vmem_spec()] * 2,
        out_specs=(vmem_spec(),) * 4,
        scratch_shapes=[pltpu.SemaphoreType.DMA] + density_buffers(EARLY),
        compiler_params=pltpu.CompilerParams(vmem_limit_bytes=30 << 20),
        cost_estimate=density_cost(EARLY),
        name="density_first",
    )(order, place, which, where, *chunks, *sources, table, weights, xc)


def density_last(order, chunks, table, dmat, weights, xc, rho, pacc, top):
    count = PIECES - EARLY
    return pl.pallas_call(
        density_last_body,
        out_shape=(
            jax.ShapeDtypeStruct((PIECES, 1, HALF), jnp.float32),
            jax.ShapeDtypeStruct((32, PAY_ROWS, 128), jnp.float32),
        ),
        in_specs=[smem_spec()] + [any_spec()] * (count + 1) + [vmem_spec()] * 6,
        out_specs=(vmem_spec(),) * 2,
        scratch_shapes=[
            pltpu.VMEM((2, NB * BLK, 128), jnp.float32),
            pltpu.VMEM((PAY_ROWS, 128), jnp.float32),
        ]
        + density_buffers(count),
        compiler_params=pltpu.CompilerParams(vmem_limit_bytes=24 << 20),
        cost_estimate=density_cost(count),
        name="density_last",
    )(order, *chunks, table, dmat, weights, xc, rho, pacc, top)


def potential_call(table, got, even, odd, weights, xc, rho, natoms):
    row = jax.ShapeDtypeStruct((PIECES, 1, HALF), jnp.float32)
    return pl.pallas_call(
        potential_body,
        out_shape=(
            jax.ShapeDtypeStruct((natoms, 64), jnp.float32),
            row,
            row,
            jax.ShapeDtypeStruct((1, 128), jnp.float32),
        ),
        in_specs=[any_spec()] + [vmem_spec()] * 6,
        out_specs=(vmem_spec(),) * 4,
        scratch_shapes=[
            pltpu.VMEM((3, NB * BLK, HALF), jnp.float32),
            pltpu.VMEM((2048, 128), jnp.float32),
            pltpu.SemaphoreType.DMA((3,)),
        ],
        compiler_params=pltpu.CompilerParams(vmem_limit_bytes=16 << 20),
        cost_estimate=pl.CostEstimate(
            flops=16 << 20, bytes_accessed=16 << 20, transcendentals=0
        ),
        name="potential",
    )(table, got, even, odd, weights, xc, rho)


def ham_call(order, slots, place, chunks, scale_mine, scale_beside):
    return pl.pallas_call(
        ham_body,
        out_shape=(jax.ShapeDtypeStruct((32, 128, BLK), jnp.float32),) * 4,
        in_specs=[smem_spec()] * 3 + [any_spec()] * (2 * CHUNKS) + [vmem_spec()] * 2,
        out_specs=(any_spec(),) * 4,
        scratch_shapes=[
            pltpu.VMEM((128, 128, BLK), jnp.float32),
            pltpu.VMEM((2, 2, 2, NB, 128, 4 * HALF), jnp.bfloat16),
            pltpu.VMEM((2, 2, 1, 4 * HALF), jnp.float32),
            pltpu.SemaphoreType.DMA,
            pltpu.SemaphoreType.DMA((4,)),
        ],
        compiler_params=pltpu.CompilerParams(vmem_limit_bytes=38 << 20),
        cost_estimate=pl.CostEstimate(
            flops=2 * 4096 * 1024 * 1024, bytes_accessed=32 << 20, transcendentals=0
        ),
        name="ham",
    )(
        order,
        slots,
        place,
        *[c.reshape(NB, 2, 128, c.shape[-1]) for c in chunks],
        scale_mine,
        scale_beside,
    )


def cast(x):
    return x.astype(jnp.float16)


def wide(x):
    return x.astype(jnp.float32)


def ring_sum(parts, factor):
    half = parts[2].shape[0] // 2
    from_below = lax.ppermute(cast(parts[2][:half] * factor), "grid", core_perm(1, False))
    from_above = lax.ppermute(cast(parts[2][half:] * factor), "grid", core_perm(-1, False))
    zero = jnp.zeros_like(from_below)
    up = cast(parts[1] * factor + wide(jnp.concatenate([from_below, zero])))
    down = cast(parts[3] * factor + wide(jnp.concatenate([zero, from_above])))
    got_below = lax.ppermute(up, "grid", core_perm(1, False))
    got_above = lax.ppermute(down, "grid", core_perm(-1, False))
    return parts[0] * factor + wide(got_below) + wide(got_above)


def direct_sum(parts):
    total = parts[0]
    got = [lax.ppermute(cast(parts[d]), "grid", core_perm(d, True)) for d in (2, 1, 3)]
    for g in got:
        total = total + wide(g)
    return total


def one_device(
    basis_values,
    point_coords,
    point_weights,
    xc_kernel,
    gauss_widths,
    atom_coords,
    resp_density,
    tile_list,
    tile_home,
    atom_list,
    atom_home,
):
    groups = lax.axis_size("grid")
    me = lax.axis_index("grid")
    plane = lax.axis_index("pert")
    my_z, my_x, my_c = me // 8, (me // 2) % 4, me % 2
    tile_dev = resp_density.shape[1]
    neighbors = atom_list.shape[1]
    moments = gauss_widths.shape[0]
    natoms = atom_home.shape[0]
    ntiles = tile_home.shape[0]
    slots_here = 2 * neighbors

    own0, own1 = basis_values[:HALF].T, basis_values[HALF:].T
    below0 = lax.ppermute(own0, "pert", ring(1))
    above1 = lax.ppermute(own1, "pert", ring(3))
    below1 = lax.ppermute(own1, "pert", ring(1))
    above0 = lax.ppermute(own0, "pert", ring(3))
    steps = jnp.array([0, 0, 3, 3, 1, 1, 2, 2], jnp.int32)
    halves = jnp.array([0, 1] * 4, jnp.int32)
    order = ((plane + steps) % 4) * 2 + halves

    swap = grid_perm(0, 0, 1)
    first_core = my_c == 0
    top_half, low_half = resp_density[0, :, :128], resp_density[0, :, 128:]
    kept = jnp.where(first_core, top_half, low_half)
    came = lax.ppermute(jnp.where(first_core, low_half, top_half), "grid", swap)
    base = jnp.concatenate(
        [jnp.where(first_core, kept, came), jnp.where(first_core, came, kept)], axis=0
    )
    ring_tiles = [lax.ppermute(base, "grid", core_perm(-d, False)) for d in (1, 2, 3)]

    wanted = tile_list.reshape(-1)
    tile_match = wanted[:, None] == jnp.arange(ntiles, dtype=jnp.int32)[None, :]
    homes = jnp.sum(jnp.where(tile_match, tile_home[None, :], 0), axis=1)
    homes_beside = lax.ppermute(homes, "grid", grid_perm(0, 0, 1))

    every_home = jnp.concatenate([homes, homes_beside])
    owner = every_home // tile_dev
    off_z = (owner // 8 - my_z) % 4
    off_x = ((owner // 2) % 4 - my_x) % 4
    ahead = jnp.where(my_c == 0, off_z * 4 + off_x, off_x * 4 + off_z)
    slots = ahead * (2 * tile_dev) + every_home % (2 * tile_dev)
    core_place = my_c.reshape(1).astype(jnp.int32)

    my_owner = homes // tile_dev
    to_z = (my_owner // 8 - my_z) % 4
    to_x = ((my_owner // 2) % 4 - my_x) % 4
    in_chip = homes % (2 * tile_dev)

    def found(one, two):
        source = jnp.where(two == 2, 2 + one // 2, jnp.where(two == 3, 4, two))
        return source, jnp.where(two == 2, one % 2, one) * (2 * tile_dev) + in_chip

    own_first = jnp.where(first_core, to_z, to_x)
    own_second = jnp.where(first_core, to_x, to_z)
    which_own, where_own = found(own_first, own_second)
    which_other, where_other = found(own_second, own_first)
    which = jnp.concatenate([which_own, which_other])
    where = jnp.concatenate([where_own, where_other])

    atom_match = atom_list[:, :, None] == jnp.arange(natoms, dtype=jnp.int32)
    atom_pos = jnp.sum(jnp.where(atom_match[None], atom_coords[:, None, None, :], 0.0), axis=3)
    atom_homes = jnp.sum(jnp.where(atom_match, atom_home, 0), axis=2).reshape(-1)
    delta = point_coords.reshape(3, 2, 4, 1, HALF) - atom_pos[:, :, None, :, None]
    dist_sq = (jnp.sum(delta * delta, axis=0) + SOFTEN).reshape(PIECES, neighbors, 1, HALF)
    spread = (2.0 * gauss_widths * gauss_widths)[None, None, :, None]
    erf_scale = (ROOT_TWO * gauss_widths)[None, None, :, None]
    gauss = jnp.exp(-dist_sq / spread).reshape(PIECES, neighbors * moments, HALF)
    distance = jnp.sqrt(dist_sq)
    hart = (lax.erf(distance / erf_scale) / distance).reshape(
        PIECES, neighbors * moments, HALF
    )
    weights = point_weights.reshape(PIECES, 1, HALF)
    xc = xc_kernel.reshape(PIECES, 1, HALF)

    ring_tiles, gauss = lax.optimization_barrier((ring_tiles, gauss))
    stored = jnp.concatenate([base] + ring_tiles, axis=0)
    ahead_tiles = lax.ppermute(stored, "grid", core_perm(-1, True))
    behind_tiles = lax.ppermute(stored, "grid", core_perm(1, True))

    row = jnp.pad(atom_homes.astype(jnp.float32), (0, 128 - slots_here))
    home_rows = lax.all_to_all(
        jnp.broadcast_to(row[None, None], (groups, 8, 128)), "grid", 0, 0, tiled=True
    )[:, 0, :slots_here]
    wanted_rows = jnp.concatenate(
        [jnp.arange(natoms, dtype=jnp.float32), atom_homes.astype(jnp.float32)]
    )

    def chooser(which):
        held = jnp.pad(
            home_rows.reshape(groups, slots_here // 2, 2)[:, :, which],
            ((0, 0), (0, PAY_ROWS - slots_here // 2)),
            constant_values=-1.0,
        ).reshape(-1)
        return (wanted_rows[:, None] == held[None, :]).astype(jnp.bfloat16)

    even, odd = chooser(0), chooser(1)
    below0, above1, hart = lax.optimization_barrier((below0, above1, hart))
    far0 = lax.ppermute(below0, "pert", ring(1))
    far1 = lax.ppermute(above1, "pert", ring(3))
    chunks = [own0, own1, below0, below1, above0, above1, far0, far1]
    beside = [lax.ppermute(chunk, "grid", swap) for chunk in chunks]

    ahead_tiles, behind_tiles, even, odd, slots = lax.optimization_barrier(
        (ahead_tiles, behind_tiles, even, odd, slots)
    )
    rows2 = 4 * tile_dev
    far_tiles0 = lax.ppermute(ahead_tiles[:rows2], "grid", core_perm(-1, True))
    far_tiles1 = lax.ppermute(behind_tiles[rows2:], "grid", core_perm(1, True))
    sources = [stored, ahead_tiles, far_tiles0, far_tiles1, behind_tiles]
    sources = sources + [lax.ppermute(s, "grid", swap) for s in sources]
    rho, pacc, top, dmat = density_first(
        order, core_place, which, where, chunks[:EARLY], sources, gauss, weights, xc
    )
    rho, sent = density_last(order, chunks[EARLY:], gauss, dmat, weights, xc, rho, pacc, top)
    got = lax.all_to_all(sent, "grid", split_axis=0, concat_axis=0, tiled=True)
    all_coeffs, pot, scale, bound = potential_call(
        hart, got.reshape(groups * PAY_ROWS, 128), even, odd, weights, xc, rho, natoms
    )
    atom_dev = natoms // groups
    own_coeffs = lax.dynamic_slice_in_dim(all_coeffs, me * atom_dev, atom_dev, axis=0)
    ham_bound = PHI_MAX_SQ * 2048 * 0.05 * groups * bound[0, 0] * 1.01 + 1e-20

    scale_beside = lax.ppermute(scale, "grid", swap)
    dense = ham_call(
        order,
        slots,
        core_place,
        chunks + beside,
        scale.reshape(2, 1, 4 * HALF),
        scale_beside.reshape(2, 1, 4 * HALF),
    )

    factor = F16_TOP / ham_bound
    dense = [d.reshape(4, 2 * tile_dev, 128, BLK) for d in dense]
    chip = direct_sum(list(ring_sum(dense, factor)))
    chip = chip.reshape(2, tile_dev, 128, BLK)
    keep = jnp.where(first_core, chip[0], chip[1])
    give = jnp.where(first_core, chip[1], chip[0])
    came = wide(lax.ppermute(cast(give), "grid", swap))
    hamiltonian = jnp.concatenate(
        [jnp.where(first_core, keep, came), jnp.where(first_core, came, keep)], axis=1
    ) * (ham_bound / F16_TOP)
    return (hamiltonian[None], own_coeffs[None], pot.reshape(1, -1))


def solution(mesh):
    placed = (
        P(("grid", "pert"), None),
        P(None, "grid"),
        P("grid"),
        P("grid"),
        P(),
        P(),
        P("pert", "grid", None, None),
        P("grid", None),
        P(),
        P("grid", None),
        P(),
    )
    return jax.shard_map(
        one_device,
        mesh=mesh,
        in_specs=placed,
        out_specs=(P("pert", "grid", None, None), P("pert", "grid", None), P("pert", "grid")),
        check_vma=False,
    )
```

```python
import functools

import jax
import jax.numpy as jnp
from jax import lax
from jax.experimental import pallas as pl
from jax.experimental.pallas import tpu as pltpu
from jax.sharding import PartitionSpec as P


SOFTEN = 0.25
ROOT_TWO = 1.4142135623730951
HALF = 512
PIECES = 8
CHUNKS = 8
SOURCES = 5
EARLY = 6
BLK = 256
NB = 4
PHI_MAX_SQ = 36.0
KERNEL_MAX = 2.0
F16_TOP = 32000.0
PAY_ROWS = 24


def ring(shift):
    return [(i, (i + shift) % 4) for i in range(4)]


def grid_perm(dz, dx, dc):
    def at(z, x, c):
        return ((z % 4) * 4 + x % 4) * 2 + c

    return [
        (at(z, x, c), at(z + dz, x + dx, c ^ dc))
        for z in range(4)
        for x in range(4)
        for c in range(2)
    ]


def core_perm(shift, second):
    def at(z, x, c):
        return ((z % 4) * 4 + x % 4) * 2 + c

    pairs = []
    for z in range(4):
        for x in range(4):
            for c in range(2):
                along_z = (c == 0) != second
                there = at(z + shift, x, c) if along_z else at(z, x + shift, c)
                pairs.append((at(z, x, c), there))
    return pairs


def split3(x):
    first = x.astype(jnp.bfloat16)
    rest = x - first.astype(jnp.float32)
    second = rest.astype(jnp.bfloat16)
    third = (rest - second.astype(jnp.float32)).astype(jnp.bfloat16)
    return first, second, third


def fetch_tiles(core, which, where, sources, dmat, sem):
    for side in range(2):
        half = (1 - core) if side else core

        def fetch(n, _, side=side, half=half):
            b, row, col = n // 16, (n // 4) % 4, n % 4
            target = dmat.at[
                b,
                pl.ds(pl.multiple_of(row * BLK + half * 128, 128), 128),
                pl.ds(pl.multiple_of(col * BLK, BLK), BLK),
            ]
            for k in range(SOURCES):

                @pl.when(which[side * 32 + n] == k)
                def _(k=k):
                    pltpu.make_async_copy(
                        sources[side * SOURCES + k].at[where[side * 32 + n]], target, sem
                    ).start()

            return 0

        lax.fori_loop(0, 32, fetch, 0)


def density_steps(order, first, count, chunks, dmat, table, weights, xc, rho, pacc, bufs, top):
    held, tbuf, psem, tsem = bufs
    for i in range(count):
        pltpu.make_async_copy(chunks[i], held.at[i], psem.at[i]).start()
    pltpu.make_async_copy(table.at[order[first]], tbuf.at[0], tsem.at[0]).start()

    def step(i, top):
        slot = lax.rem(i, 2)

        @pl.when(i + 1 < count)
        def _():
            pltpu.make_async_copy(
                table.at[order[first + i + 1]], tbuf.at[1 - slot], tsem.at[1 - slot]
            ).start()

        pi = order[first + i]
        b = pi // 4
        pltpu.make_async_copy(held.at[i], held.at[i], psem.at[i]).wait()
        piece = held[i]
        total = jnp.zeros((1, HALF), jnp.float32)
        for block in range(NB):
            rows = pl.ds(block * BLK, BLK)
            mixed = jnp.dot(dmat[b, rows, :], piece, preferred_element_type=jnp.float32)
            total = total + jnp.sum(
                mixed * held[i, rows, :].astype(jnp.float32), axis=0, keepdims=True
            )
        rho[pi] = total
        weighted = weights[pi] * total
        pltpu.make_async_copy(table.at[pi], tbuf.at[slot], tsem.at[slot]).wait()
        for block in range(8):
            rows = pl.ds(block * 128, 128)
            part = pacc[b, rows, :]
            for lane in range(HALF // 128):
                cols = slice(lane * 128, (lane + 1) * 128)
                part = part + tbuf[slot, rows, cols] * weighted[:, cols]
            pacc[b, rows, :] = part
        return jnp.maximum(top, jnp.abs(xc[pi] * total))

    return lax.fori_loop(0, count, step, top)


def density_first_body(order, place, which, where, *refs):
    chunks = refs[:EARLY]
    sources = refs[EARLY : EARLY + 2 * SOURCES]
    table, weights, xc, rho, pacc, top, dmat, sem, *bufs = refs[EARLY + 2 * SOURCES :]
    fetch_tiles(place[0], which, where, sources, dmat, sem)
    pacc[...] = jnp.zeros_like(pacc)
    rho[...] = jnp.zeros_like(rho)
    pltpu.make_async_copy(dmat, dmat, sem).wait()
    top[...] = density_steps(
        order, 0, EARLY, chunks, dmat, table, weights, xc, rho, pacc, bufs,
        jnp.zeros((1, HALF), jnp.float32),
    )


def density_last_body(order, *refs):
    count = PIECES - EARLY
    chunks = refs[:count]
    (table, dmat_in, pacc_in, weights, xc, home_rows, rho_in, top_in, rho, sent, *rest) = refs[count:]
    pacc, dmat, block_out, lsem, *bufs = rest
    batch = order[EARLY] // 4
    pltpu.make_async_copy(dmat_in.at[pl.ds(batch, 1)], dmat.at[pl.ds(batch, 1)], lsem.at[0]).start()
    pltpu.make_async_copy(pacc_in, pacc, lsem.at[1]).start()
    rho[...] = rho_in[...]
    block_out[...] = jnp.zeros_like(block_out)
    block_out[pl.ds(17, 2), :] = home_rows[...]
    pltpu.make_async_copy(dmat_in.at[pl.ds(batch, 1)], dmat.at[pl.ds(batch, 1)], lsem.at[0]).wait()
    pltpu.make_async_copy(pacc_in, pacc, lsem.at[1]).wait()
    top = density_steps(
        order, EARLY, count, chunks, dmat, table, weights, xc, rho, pacc, bufs, top_in[...]
    )
    ones = jnp.ones((8, 128), jnp.bfloat16)
    for b in range(2):
        total = jnp.zeros((8, NB * BLK), jnp.float32)
        for term in split3(pacc[b]):
            total = total + lax.dot_general(
                ones, term, (((1,), (1,)), ((), ())), preferred_element_type=jnp.float32
            )
        for r in range(8):
            block_out[pl.ds(b * 8 + r, 1), :] = total[0:1, r * 128 : (r + 1) * 128]
    block_out[pl.ds(16, 1), :] = jnp.broadcast_to(jnp.max(top, axis=1, keepdims=True), (1, 128))
    for dest in range(32):
        sent[dest] = block_out[...]


def potential_body(table, got, mine, weights, xc, rho, coeffs, pot, scale, bound, *scratch):
    tbuf, column, data, tsem = scratch
    for i in range(2):
        pltpu.make_async_copy(table.at[i], tbuf.at[i], tsem.at[i]).start()
    natoms = coeffs.shape[0]
    homes = []
    for which in range(2):
        segments = []
        for group in range(4):
            row = jnp.zeros((1, 128), jnp.float32)
            for k in range(8):
                row = row + got[pl.ds((group * 8 + k) * PAY_ROWS + 17 + which, 1), :]
            segments.append(row)
        homes.append(jnp.concatenate(segments, axis=1))
    for k in range(32):
        data[pl.ds(k * 16, 16), :] = got[pl.ds(k * PAY_ROWS, 16), :]
    stored = lax.broadcasted_iota(jnp.int32, (natoms, 128), 0).astype(jnp.float32)
    wanted = jnp.concatenate([stored, mine[...]], axis=0)
    wanted = jnp.concatenate([wanted] * 4, axis=1)
    even, odd = [
        jnp.where(wanted == row, 1.0, 0.0).astype(jnp.bfloat16)
        for row in homes
    ]
    first = jnp.zeros((natoms + 32, 128), jnp.float32)
    second = jnp.zeros((natoms + 32, 128), jnp.float32)
    for term in split3(data[...]):
        first = first + jnp.dot(even, term, preferred_element_type=jnp.float32)
        second = second + jnp.dot(odd, term, preferred_element_type=jnp.float32)
    summed = first[:, :64] + second[:, 64:]
    coeffs[...] = summed[:natoms]
    turned = summed[natoms:].T
    for k in range(32):
        column[pl.ds(k * 64, 64), :] = jnp.broadcast_to(turned[:, k : k + 1], (64, 128))
    top = jnp.zeros((1, 128), jnp.float32)
    for k in range(32):
        top = jnp.maximum(top, got[pl.ds(k * PAY_ROWS + 16, 1), :])
    heavy = jnp.max(jnp.sum(jnp.abs(summed[:natoms]), axis=1, keepdims=True), axis=0, keepdims=True)
    bound[...] = top + jnp.broadcast_to(heavy, (1, 128)) * (KERNEL_MAX * 16)

    def step(i, _):
        slot = lax.rem(i, 3)

        @pl.when(i + 2 < PIECES)
        def _():
            ahead = lax.rem(i + 2, 3)
            pltpu.make_async_copy(table.at[i + 2], tbuf.at[ahead], tsem.at[ahead]).start()

        base = (i // 4) * 1024
        pltpu.make_async_copy(table.at[i], tbuf.at[slot], tsem.at[slot]).wait()
        parts = [jnp.zeros((8, 128), jnp.float32) for _ in range(HALF // 128)]
        for block in range(16):
            factor = column[pl.ds(base + block * 64, 64), :]
            for lane in range(HALF // 128):
                prod = tbuf[slot, block * 64 : (block + 1) * 64, lane * 128 : (lane + 1) * 128]
                parts[lane] = parts[lane] + jnp.sum((prod * factor).reshape(8, 8, 128), axis=0)
        hartree = jnp.concatenate([jnp.sum(p, axis=0, keepdims=True) for p in parts], axis=1)
        potential = hartree + xc[i] * rho[i]
        pot[i] = potential
        scale[i] = weights[i] * potential
        return 0

    lax.fori_loop(0, PIECES, step, 0)


def ham_body(quarter, order, slots, place, *refs):
    chunks = refs[: 2 * CHUNKS]
    scale_mine, scale_beside, *rest = refs[2 * CHUNKS :]
    outs, (dense, held, rows_of, psem, osem) = rest[:4], rest[4:]
    core = place[0]
    for side in range(2):
        i = 0
        for ref in chunks[side * CHUNKS : (side + 1) * CHUNKS]:
            width = ref.shape[-1]
            pi = order[i]
            lanes = pl.ds(pl.multiple_of((pi % 4) * HALF, HALF), width)
            for half in range(2):
                at = (1 - core) if half else core
                pltpu.make_async_copy(
                    ref.at[:, half], held.at[side, pi // 4, at, :, :, lanes], psem
                ).start()
            i += width // HALF
    for b in range(2):
        rows_of[0, b] = scale_mine[b]
        rows_of[1, b] = scale_beside[b]

    def clear(s, _):
        dense[s] = jnp.zeros(dense.shape[1:], jnp.float32)
        return 0

    lax.fori_loop(0, dense.shape[0], clear, 0)
    pltpu.make_async_copy(held, held, psem).wait()

    def product(side, b, col):
        left = held[side, b, 0, :, quarter * 64 : (quarter + 1) * 64].reshape(BLK, 4 * HALF)
        right = jnp.concatenate([held[side, b, core, col], held[side, b, 1 - core, col]], axis=0)
        right = (right.astype(jnp.float32) * rows_of[side, b]).astype(jnp.bfloat16)
        return lax.dot_general(
            left, right, (((1,), (1,)), ((), ())), preferred_element_type=jnp.float32
        )

    def step(n, _):
        side, b, cols = n // 4, (n // 2) % 2, (n % 2) * 2
        parts = [product(side, b, cols + k) for k in range(2)]
        for k in range(2):
            for row in range(NB):
                slot = slots[side * 32 + b * 16 + row * NB + cols + k]
                dense[slot] += parts[k][row * 64 : (row + 1) * 64]
        return 0

    lax.fori_loop(0, 8, step, 0)
    for d in range(4):
        pltpu.make_async_copy(dense.at[pl.ds(d * 32, 32)], outs[d], osem.at[d]).start()
    for d in range(4):
        pltpu.make_async_copy(dense.at[pl.ds(d * 32, 32)], outs[d], osem.at[d]).wait()


def any_spec():
    return pl.BlockSpec(memory_space=pltpu.HBM)


def vmem_spec():
    return pl.BlockSpec(memory_space=pltpu.VMEM)


def smem_spec():
    return pl.BlockSpec(memory_space=pltpu.SMEM)


def density_buffers(count):
    nbasis = NB * BLK
    return [
        pltpu.VMEM((count, nbasis, HALF), jnp.bfloat16),
        pltpu.VMEM((2, nbasis, HALF), jnp.float32),
        pltpu.SemaphoreType.DMA((count,)),
        pltpu.SemaphoreType.DMA((2,)),
    ]


def density_cost(count):
    return pl.CostEstimate(
        flops=2 * count * HALF * 1024 * 1024, bytes_accessed=count * (3 << 20), transcendentals=0
    )


def density_first(order, place, which, where, chunks, sources, table, weights, xc):
    nbasis = NB * BLK
    return pl.pallas_call(
        density_first_body,
        out_shape=(
            jax.ShapeDtypeStruct((PIECES, 1, HALF), jnp.float32),
            jax.ShapeDtypeStruct((2, nbasis, 128), jnp.float32),
            jax.ShapeDtypeStruct((1, HALF), jnp.float32),
            jax.ShapeDtypeStruct((2, nbasis, nbasis), jnp.bfloat16),
        ),
        in_specs=[smem_spec()] * 4
        + [any_spec()] * (EARLY + 2 * SOURCES + 1)
        + [vmem_spec()] * 2,
        out_specs=(vmem_spec(),) * 4,
        scratch_shapes=[pltpu.SemaphoreType.DMA] + density_buffers(EARLY),
        compiler_params=pltpu.CompilerParams(vmem_limit_bytes=30 << 20),
        cost_estimate=density_cost(EARLY),
        name="density_first",
    )(order, place, which, where, *chunks, *sources, table, weights, xc)


def density_last(order, chunks, table, dmat, pacc, weights, xc, home_rows, rho, top):
    count = PIECES - EARLY
    nbasis = NB * BLK
    return pl.pallas_call(
        density_last_body,
        out_shape=(
            jax.ShapeDtypeStruct((PIECES, 1, HALF), jnp.float32),
            jax.ShapeDtypeStruct((32, PAY_ROWS, 128), jnp.float32),
        ),
        in_specs=[smem_spec()] + [any_spec()] * (count + 3) + [vmem_spec()] * 5,
        out_specs=(vmem_spec(),) * 2,
        scratch_shapes=[
            pltpu.VMEM((2, nbasis, 128), jnp.float32),
            pltpu.VMEM((2, nbasis, nbasis), jnp.bfloat16),
            pltpu.VMEM((PAY_ROWS, 128), jnp.float32),
            pltpu.SemaphoreType.DMA((2,)),
        ]
        + density_buffers(count),
        compiler_params=pltpu.CompilerParams(vmem_limit_bytes=24 << 20),
        cost_estimate=density_cost(count),
        name="density_last",
    )(order, *chunks, table, dmat, pacc, weights, xc, home_rows, rho, top)


def potential_call(table, got, mine, weights, xc, rho, natoms):
    row = jax.ShapeDtypeStruct((PIECES, 1, HALF), jnp.float32)
    return pl.pallas_call(
        potential_body,
        out_shape=(
            jax.ShapeDtypeStruct((natoms, 64), jnp.float32),
            row,
            row,
            jax.ShapeDtypeStruct((1, 128), jnp.float32),
        ),
        in_specs=[any_spec()] + [vmem_spec()] * 5,
        out_specs=(vmem_spec(),) * 4,
        scratch_shapes=[
            pltpu.VMEM((3, NB * BLK, HALF), jnp.float32),
            pltpu.VMEM((2048, 128), jnp.float32),
            pltpu.VMEM((512, 128), jnp.float32),
            pltpu.SemaphoreType.DMA((3,)),
        ],
        compiler_params=pltpu.CompilerParams(vmem_limit_bytes=16 << 20),
        cost_estimate=pl.CostEstimate(
            flops=16 << 20, bytes_accessed=16 << 20, transcendentals=0
        ),
        name="potential",
    )(table, got, mine, weights, xc, rho)


def ham_call(quarter, order, slots, place, chunks, scale_mine, scale_beside):
    return pl.pallas_call(
        functools.partial(ham_body, quarter),
        out_shape=(jax.ShapeDtypeStruct((32, 64, BLK), jnp.float32),) * 4,
        in_specs=[smem_spec()] * 3 + [any_spec()] * (2 * CHUNKS) + [vmem_spec()] * 2,
        out_specs=(any_spec(),) * 4,
        scratch_shapes=[
            pltpu.VMEM((128, 64, BLK), jnp.float32),
            pltpu.VMEM((2, 2, 2, NB, 128, 4 * HALF), jnp.bfloat16),
            pltpu.VMEM((2, 2, 1, 4 * HALF), jnp.float32),
            pltpu.SemaphoreType.DMA,
            pltpu.SemaphoreType.DMA((4,)),
        ],
        compiler_params=pltpu.CompilerParams(vmem_limit_bytes=38 << 20),
        cost_estimate=pl.CostEstimate(
            flops=4096 * 1024 * 1024, bytes_accessed=24 << 20, transcendentals=0
        ),
        name="ham",
    )(
        order,
        slots,
        place,
        *[c.reshape(NB, 2, 128, c.shape[-1]) for c in chunks],
        scale_mine,
        scale_beside,
    )


def cast(x):
    return x.astype(jnp.float16)


def wide(x):
    return x.astype(jnp.float32)


def ring_sum(parts, factor):
    half = parts[2].shape[0] // 2
    from_below = lax.ppermute(cast(parts[2][:half] * factor), "grid", core_perm(1, False))
    from_above = lax.ppermute(cast(parts[2][half:] * factor), "grid", core_perm(-1, False))
    zero = jnp.zeros_like(from_below)
    up = cast(parts[1] * factor + wide(jnp.concatenate([from_below, zero])))
    down = cast(parts[3] * factor + wide(jnp.concatenate([zero, from_above])))
    got_below = lax.ppermute(up, "grid", core_perm(1, False))
    got_above = lax.ppermute(down, "grid", core_perm(-1, False))
    return parts[0] * factor + wide(got_below) + wide(got_above)


def direct_sum(parts):
    total = parts[0]
    got = [lax.ppermute(cast(parts[d]), "grid", core_perm(d, True)) for d in (2, 1, 3)]
    for g in got:
        total = total + wide(g)
    return total


def one_device(
    basis_values,
    point_coords,
    point_weights,
    xc_kernel,
    gauss_widths,
    atom_coords,
    resp_density,
    tile_list,
    tile_home,
    atom_list,
    atom_home,
):
    groups = lax.axis_size("grid")
    me = lax.axis_index("grid")
    plane = lax.axis_index("pert")
    my_z, my_x, my_c = me // 8, (me // 2) % 4, me % 2
    tile_dev = resp_density.shape[1]
    neighbors = atom_list.shape[1]
    moments = gauss_widths.shape[0]
    natoms = atom_home.shape[0]
    ntiles = tile_home.shape[0]
    slots_here = 2 * neighbors

    own0, own1 = basis_values[:HALF].T, basis_values[HALF:].T
    below0 = lax.ppermute(own0, "pert", ring(1))
    above1 = lax.ppermute(own1, "pert", ring(3))
    below1 = lax.ppermute(own1, "pert", ring(1))
    above0 = lax.ppermute(own0, "pert", ring(3))
    steps = jnp.array([0, 0, 3, 3, 1, 1, 2, 2], jnp.int32)
    halves = jnp.array([0, 1] * 4, jnp.int32)
    order = ((plane + steps) % 4) * 2 + halves

    swap = grid_perm(0, 0, 1)
    first_core = my_c == 0
    top_half, low_half = resp_density[0, :, :128], resp_density[0, :, 128:]
    kept = jnp.where(first_core, top_half, low_half)
    came = lax.ppermute(jnp.where(first_core, low_half, top_half), "grid", swap)
    base = jnp.concatenate(
        [jnp.where(first_core, kept, came), jnp.where(first_core, came, kept)], axis=0
    )
    ring_tiles = [lax.ppermute(base, "grid", core_perm(-d, False)) for d in (1, 2, 3)]

    wanted = tile_list.reshape(-1)
    tile_match = wanted[:, None] == jnp.arange(ntiles, dtype=jnp.int32)[None, :]
    homes = jnp.sum(jnp.where(tile_match, tile_home[None, :], 0), axis=1)
    homes_beside = lax.ppermute(homes, "grid", grid_perm(0, 0, 1))

    every_home = jnp.concatenate([homes, homes_beside])
    owner = every_home // tile_dev
    off_z = (owner // 8 - my_z) % 4
    off_x = ((owner // 2) % 4 - my_x) % 4
    ahead = jnp.where(my_c == 0, off_z * 4 + off_x, off_x * 4 + off_z)
    slots = ahead * (2 * tile_dev) + every_home % (2 * tile_dev)
    core_place = my_c.reshape(1).astype(jnp.int32)

    my_owner = homes // tile_dev
    to_z = (my_owner // 8 - my_z) % 4
    to_x = ((my_owner // 2) % 4 - my_x) % 4
    in_chip = homes % (2 * tile_dev)

    def found(one, two):
        source = jnp.where(two == 2, 2 + one // 2, jnp.where(two == 3, 4, two))
        return source, jnp.where(two == 2, one % 2, one) * (2 * tile_dev) + in_chip

    own_first = jnp.where(first_core, to_z, to_x)
    own_second = jnp.where(first_core, to_x, to_z)
    which_own, where_own = found(own_first, own_second)
    which_other, where_other = found(own_second, own_first)
    which = jnp.concatenate([which_own, which_other])
    where = jnp.concatenate([where_own, where_other])

    atom_match = atom_list[:, :, None] == jnp.arange(natoms, dtype=jnp.int32)
    atom_pos = jnp.sum(jnp.where(atom_match[None], atom_coords[:, None, None, :], 0.0), axis=3)
    atom_homes = jnp.sum(jnp.where(atom_match, atom_home, 0), axis=2).reshape(-1)
    delta = point_coords.reshape(3, 2, 4, 1, HALF) - atom_pos[:, :, None, :, None]
    dist_sq = (jnp.sum(delta * delta, axis=0) + SOFTEN).reshape(PIECES, neighbors, 1, HALF)
    spread = (2.0 * gauss_widths * gauss_widths)[None, None, :, None]
    erf_scale = (ROOT_TWO * gauss_widths)[None, None, :, None]
    gauss = jnp.exp(-dist_sq / spread).reshape(PIECES, neighbors * moments, HALF)
    distance = jnp.sqrt(dist_sq)
    hart = (lax.erf(distance / erf_scale) / distance).reshape(
        PIECES, neighbors * moments, HALF
    )
    weights = point_weights.reshape(PIECES, 1, HALF)
    xc = xc_kernel.reshape(PIECES, 1, HALF)

    ring_tiles, gauss = lax.optimization_barrier((ring_tiles, gauss))
    stored = jnp.concatenate([base] + ring_tiles, axis=0)
    ahead_tiles = lax.ppermute(stored, "grid", core_perm(-1, True))
    behind_tiles = lax.ppermute(stored, "grid", core_perm(1, True))

    lane = jnp.arange(128, dtype=jnp.int32)
    here = (lane // 16) == (me % 8)
    home_floats = atom_homes.astype(jnp.float32)
    home_rows = jnp.where(here[None, :], jnp.tile(home_floats.reshape(16, 2).T, (1, 8)), 0.0)
    my_homes = jnp.broadcast_to(home_floats[:, None], (slots_here, 128))
    below0, above1, hart = lax.optimization_barrier((below0, above1, hart))
    far0 = lax.ppermute(below0, "pert", ring(1))
    far1 = lax.ppermute(above1, "pert", ring(3))
    chunks = [own0, own1, below0, below1, above0, above1, far0, far1]
    beside = [lax.ppermute(chunk, "grid", swap) for chunk in chunks]

    ahead_tiles, behind_tiles, slots, home_rows, my_homes = lax.optimization_barrier(
        (ahead_tiles, behind_tiles, slots, home_rows, my_homes)
    )
    rows2 = 4 * tile_dev
    far_tiles0 = lax.ppermute(ahead_tiles[:rows2], "grid", core_perm(-1, True))
    far_tiles1 = lax.ppermute(behind_tiles[rows2:], "grid", core_perm(1, True))
    sources = [stored, ahead_tiles, far_tiles0, far_tiles1, behind_tiles]
    sources = sources + [lax.ppermute(s, "grid", swap) for s in sources]
    rho, pacc, top, dmat = density_first(
        order, core_place, which, where, chunks[:EARLY], sources, gauss, weights, xc
    )
    rho, sent = density_last(
        order, chunks[EARLY:], gauss, dmat, pacc, weights, xc, home_rows, rho, top
    )
    got = lax.all_to_all(sent, "grid", split_axis=0, concat_axis=0, tiled=True)
    all_coeffs, pot, scale, bound = potential_call(
        hart, got.reshape(groups * PAY_ROWS, 128), my_homes, weights, xc, rho, natoms
    )
    atom_dev = natoms // groups
    own_coeffs = lax.dynamic_slice_in_dim(all_coeffs, me * atom_dev, atom_dev, axis=0)
    ham_bound = PHI_MAX_SQ * 2048 * 0.05 * groups * bound[0, 0] * 1.01 + 1e-20

    scale_beside = lax.ppermute(scale, "grid", swap)
    factor = F16_TOP / ham_bound
    sums = []
    for quarter in range(2):
        dense = ham_call(
            quarter,
            order,
            slots,
            core_place,
            chunks + beside,
            scale.reshape(2, 1, 4 * HALF),
            scale_beside.reshape(2, 1, 4 * HALF),
        )
        dense = [d.reshape(4, 2 * tile_dev, 64, BLK) for d in dense]
        chip = direct_sum(list(ring_sum(dense, factor)))
        chip = chip.reshape(2, tile_dev, 64, BLK)
        keep = jnp.where(first_core, chip[0], chip[1])
        give = jnp.where(first_core, chip[1], chip[0])
        came = wide(lax.ppermute(cast(give), "grid", swap))
        sums.append((jnp.where(first_core, keep, came), jnp.where(first_core, came, keep)))
    hamiltonian = jnp.concatenate(
        [sums[0][0], sums[1][0], sums[0][1], sums[1][1]], axis=1
    ) * (ham_bound / F16_TOP)
    return (hamiltonian[None], own_coeffs[None], pot.reshape(1, -1))


def solution(mesh):
    placed = (
        P(("grid", "pert"), None),
        P(None, "grid"),
        P("grid"),
        P("grid"),
        P(),
        P(),
        P("pert", "grid", None, None),
        P("grid", None),
        P(),
        P("grid", None),
        P(),
    )
    return jax.shard_map(
        one_device,
        mesh=mesh,
        in_specs=placed,
        out_specs=(P("pert", "grid", None, None), P("pert", "grid", None), P("pert", "grid")),
        check_vma=False,
    )
```

```python
import jax
import jax.numpy as jnp
from jax import lax
from jax.experimental import pallas as pl
from jax.experimental.pallas import tpu as pltpu
from jax.sharding import PartitionSpec as P


SOFTEN = 0.25
ROOT_TWO = 1.4142135623730951
HALF = 512
PIECES = 8
CHUNKS = 8
VMEM_GRANT = 60 << 20
SOURCES = 5
EARLY = 6
BLK = 256
NB = 4
PHI_MAX_SQ = 36.0
KERNEL_MAX = 2.0
F16_TOP = 32000.0
PAY_ROWS = 24


def ring(shift):
    return [(i, (i + shift) % 4) for i in range(4)]


def grid_perm(dz, dx, dc):
    def at(z, x, c):
        return ((z % 4) * 4 + x % 4) * 2 + c

    return [
        (at(z, x, c), at(z + dz, x + dx, c ^ dc))
        for z in range(4)
        for x in range(4)
        for c in range(2)
    ]


def core_perm(shift, second):
    def at(z, x, c):
        return ((z % 4) * 4 + x % 4) * 2 + c

    pairs = []
    for z in range(4):
        for x in range(4):
            for c in range(2):
                along_z = (c == 0) != second
                there = at(z + shift, x, c) if along_z else at(z, x + shift, c)
                pairs.append((at(z, x, c), there))
    return pairs


def split3(x):
    first = x.astype(jnp.bfloat16)
    rest = x - first.astype(jnp.float32)
    second = rest.astype(jnp.bfloat16)
    third = (rest - second.astype(jnp.float32)).astype(jnp.bfloat16)
    return first, second, third


def fetch_tiles(core, which, where, sources, dmat, sem):
    for side in range(2):
        half = (1 - core) if side else core

        def fetch(n, _, side=side, half=half):
            b, row, col = n // 16, (n // 4) % 4, n % 4
            target = dmat.at[
                b,
                pl.ds(pl.multiple_of(row * BLK + half * 128, 128), 128),
                pl.ds(pl.multiple_of(col * BLK, BLK), BLK),
            ]
            for k in range(SOURCES):

                @pl.when(which[side * 32 + n] == k)
                def _(k=k):
                    pltpu.make_async_copy(
                        sources[side * SOURCES + k].at[where[side * 32 + n]], target, sem
                    ).start()

            return 0

        lax.fori_loop(0, 32, fetch, 0)


def density_steps(order, first, count, chunks, dmat, table, weights, xc, rho, pacc, bufs, top):
    held, tbuf, psem, tsem = bufs
    for i in range(count):
        pltpu.make_async_copy(chunks[i], held.at[i], psem.at[i]).start()
    pltpu.make_async_copy(table.at[order[first]], tbuf.at[0], tsem.at[0]).start()

    def step(i, top):
        slot = lax.rem(i, 2)

        @pl.when(i + 1 < count)
        def _():
            pltpu.make_async_copy(
                table.at[order[first + i + 1]], tbuf.at[1 - slot], tsem.at[1 - slot]
            ).start()

        pi = order[first + i]
        b = pi // 4
        pltpu.make_async_copy(held.at[i], held.at[i], psem.at[i]).wait()
        piece = held[i]
        total = jnp.zeros((1, HALF), jnp.float32)
        for block in range(NB):
            rows = pl.ds(block * BLK, BLK)
            mixed = jnp.dot(dmat[b, rows, :], piece, preferred_element_type=jnp.float32)
            total = total + jnp.sum(
                mixed * held[i, rows, :].astype(jnp.float32), axis=0, keepdims=True
            )
        rho[pi] = total
        weighted = weights[pi] * total
        pltpu.make_async_copy(table.at[pi], tbuf.at[slot], tsem.at[slot]).wait()
        for block in range(8):
            rows = pl.ds(block * 128, 128)
            part = pacc[b, rows, :]
            for lane in range(HALF // 128):
                cols = slice(lane * 128, (lane + 1) * 128)
                part = part + tbuf[slot, rows, cols] * weighted[:, cols]
            pacc[b, rows, :] = part
        return jnp.maximum(top, jnp.abs(xc[pi] * total))

    return lax.fori_loop(0, count, step, top)


def density_first_body(order, place, which, where, *refs):
    chunks = refs[:EARLY]
    sources = refs[EARLY : EARLY + 2 * SOURCES]
    table, weights, xc, rho, pacc, top, dmat, sem, *bufs = refs[EARLY + 2 * SOURCES :]
    fetch_tiles(place[0], which, where, sources, dmat, sem)
    pacc[...] = jnp.zeros_like(pacc)
    rho[...] = jnp.zeros_like(rho)
    pltpu.make_async_copy(dmat, dmat, sem).wait()
    top[...] = density_steps(
        order, 0, EARLY, chunks, dmat, table, weights, xc, rho, pacc, bufs,
        jnp.zeros((1, HALF), jnp.float32),
    )


def density_last_body(order, *refs):
    count = PIECES - EARLY
    chunks = refs[:count]
    (table, dmat_in, pacc_in, weights, xc, home_rows, rho_in, top_in, rho, sent, *rest) = refs[count:]
    pacc, dmat, block_out, lsem, *bufs = rest
    batch = order[EARLY] // 4
    pltpu.make_async_copy(dmat_in.at[pl.ds(batch, 1)], dmat.at[pl.ds(batch, 1)], lsem.at[0]).start()
    pltpu.make_async_copy(pacc_in, pacc, lsem.at[1]).start()
    rho[...] = rho_in[...]
    block_out[...] = jnp.zeros_like(block_out)
    block_out[pl.ds(17, 2), :] = home_rows[...]
    pltpu.make_async_copy(dmat_in.at[pl.ds(batch, 1)], dmat.at[pl.ds(batch, 1)], lsem.at[0]).wait()
    pltpu.make_async_copy(pacc_in, pacc, lsem.at[1]).wait()
    top = density_steps(
        order, EARLY, count, chunks, dmat, table, weights, xc, rho, pacc, bufs, top_in[...]
    )
    ones = jnp.ones((8, 128), jnp.bfloat16)
    for b in range(2):
        total = jnp.zeros((8, NB * BLK), jnp.float32)
        for term in split3(pacc[b]):
            total = total + lax.dot_general(
                ones, term, (((1,), (1,)), ((), ())), preferred_element_type=jnp.float32
            )
        for r in range(8):
            block_out[pl.ds(b * 8 + r, 1), :] = total[0:1, r * 128 : (r + 1) * 128]
    block_out[pl.ds(16, 1), :] = jnp.broadcast_to(jnp.max(top, axis=1, keepdims=True), (1, 128))
    for dest in range(32):
        sent[dest] = block_out[...]


def potential_body(table, got, mine, weights, xc, rho, coeffs, pot, scale, bound, *scratch):
    tbuf, column, data, tsem = scratch
    for i in range(2):
        pltpu.make_async_copy(table.at[i], tbuf.at[i], tsem.at[i]).start()
    natoms = coeffs.shape[0]
    homes = []
    for which in range(2):
        segments = []
        for group in range(4):
            row = jnp.zeros((1, 128), jnp.float32)
            for k in range(8):
                row = row + got[pl.ds((group * 8 + k) * PAY_ROWS + 17 + which, 1), :]
            segments.append(row)
        homes.append(jnp.concatenate(segments, axis=1))
    for k in range(32):
        data[pl.ds(k * 16, 16), :] = got[pl.ds(k * PAY_ROWS, 16), :]
    stored = lax.broadcasted_iota(jnp.int32, (natoms, 128), 0).astype(jnp.float32)
    wanted = jnp.concatenate([stored, mine[...]], axis=0)
    wanted = jnp.concatenate([wanted] * 4, axis=1)
    even, odd = [
        jnp.where(wanted == row, 1.0, 0.0).astype(jnp.bfloat16)
        for row in homes
    ]
    first = jnp.zeros((natoms + 32, 128), jnp.float32)
    second = jnp.zeros((natoms + 32, 128), jnp.float32)
    for term in split3(data[...]):
        first = first + jnp.dot(even, term, preferred_element_type=jnp.float32)
        second = second + jnp.dot(odd, term, preferred_element_type=jnp.float32)
    summed = first[:, :64] + second[:, 64:]
    coeffs[...] = summed[:natoms]
    turned = summed[natoms:].T
    for k in range(32):
        column[pl.ds(k * 64, 64), :] = jnp.broadcast_to(turned[:, k : k + 1], (64, 128))
    top = jnp.zeros((1, 128), jnp.float32)
    for k in range(32):
        top = jnp.maximum(top, got[pl.ds(k * PAY_ROWS + 16, 1), :])
    heavy = jnp.max(jnp.sum(jnp.abs(summed[:natoms]), axis=1, keepdims=True), axis=0, keepdims=True)
    bound[...] = top + jnp.broadcast_to(heavy, (1, 128)) * (KERNEL_MAX * 16)

    def step(i, _):
        slot = lax.rem(i, 3)

        @pl.when(i + 2 < PIECES)
        def _():
            ahead = lax.rem(i + 2, 3)
            pltpu.make_async_copy(table.at[i + 2], tbuf.at[ahead], tsem.at[ahead]).start()

        base = (i // 4) * 1024
        pltpu.make_async_copy(table.at[i], tbuf.at[slot], tsem.at[slot]).wait()
        parts = [jnp.zeros((8, 128), jnp.float32) for _ in range(HALF // 128)]
        for block in range(16):
            factor = column[pl.ds(base + block * 64, 64), :]
            for lane in range(HALF // 128):
                prod = tbuf[slot, block * 64 : (block + 1) * 64, lane * 128 : (lane + 1) * 128]
                parts[lane] = parts[lane] + jnp.sum((prod * factor).reshape(8, 8, 128), axis=0)
        hartree = jnp.concatenate([jnp.sum(p, axis=0, keepdims=True) for p in parts], axis=1)
        potential = hartree + xc[i] * rho[i]
        pot[i] = potential
        scale[i] = weights[i] * potential
        return 0

    lax.fori_loop(0, PIECES, step, 0)


def ham_body(order, slots, place, *refs):
    chunks = refs[: 2 * CHUNKS]
    scale_mine, scale_beside, *rest = refs[2 * CHUNKS :]
    outs, (dense, held, rows_of, psem, osem) = rest[:4], rest[4:]
    core = place[0]
    for side in range(2):
        i = 0
        for ref in chunks[side * CHUNKS : (side + 1) * CHUNKS]:
            width = ref.shape[-1]
            pi = order[i]
            lanes = pl.ds(pl.multiple_of((pi % 4) * HALF, HALF), width)
            for half in range(2):
                at = (1 - core) if half else core
                pltpu.make_async_copy(
                    ref.at[:, half], held.at[side, pi // 4, at, :, :, lanes], psem
                ).start()
            i += width // HALF
    for b in range(2):
        rows_of[0, b] = scale_mine[b]
        rows_of[1, b] = scale_beside[b]

    def clear(s, _):
        dense[s] = jnp.zeros(dense.shape[1:], jnp.float32)
        return 0

    lax.fori_loop(0, dense.shape[0], clear, 0)
    pltpu.make_async_copy(held, held, psem).wait()

    def product(side, b, col):
        left = held[side, b, 0].reshape(2 * BLK, 4 * HALF)
        right = jnp.concatenate([held[side, b, core, col], held[side, b, 1 - core, col]], axis=0)
        right = (right.astype(jnp.float32) * rows_of[side, b]).astype(jnp.bfloat16)
        return lax.dot_general(
            left, right, (((1,), (1,)), ((), ())), preferred_element_type=jnp.float32
        )

    def step(n, _):
        side, b, cols = n // 4, (n // 2) % 2, (n % 2) * 2
        parts = [product(side, b, cols + k) for k in range(2)]
        for k in range(2):
            for row in range(NB):
                slot = slots[side * 32 + b * 16 + row * NB + cols + k]
                dense[slot] += parts[k][row * 128 : (row + 1) * 128]
        return 0

    lax.fori_loop(0, 8, step, 0)
    for d in range(4):
        pltpu.make_async_copy(dense.at[pl.ds(d * 32, 32)], outs[d], osem.at[d]).start()
    for d in range(4):
        pltpu.make_async_copy(dense.at[pl.ds(d * 32, 32)], outs[d], osem.at[d]).wait()


def any_spec():
    return pl.BlockSpec(memory_space=pltpu.HBM)


def vmem_spec():
    return pl.BlockSpec(memory_space=pltpu.VMEM)


def smem_spec():
    return pl.BlockSpec(memory_space=pltpu.SMEM)


def density_buffers(count):
    nbasis = NB * BLK
    return [
        pltpu.VMEM((count, nbasis, HALF), jnp.bfloat16),
        pltpu.VMEM((2, nbasis, HALF), jnp.float32),
        pltpu.SemaphoreType.DMA((count,)),
        pltpu.SemaphoreType.DMA((2,)),
    ]


def density_cost(count):
    return pl.CostEstimate(
        flops=2 * count * HALF * 1024 * 1024, bytes_accessed=count * (3 << 20), transcendentals=0
    )


def density_first(order, place, which, where, chunks, sources, table, weights, xc):
    nbasis = NB * BLK
    return pl.pallas_call(
        density_first_body,
        out_shape=(
            jax.ShapeDtypeStruct((PIECES, 1, HALF), jnp.float32),
            jax.ShapeDtypeStruct((2, nbasis, 128), jnp.float32),
            jax.ShapeDtypeStruct((1, HALF), jnp.float32),
            jax.ShapeDtypeStruct((2, nbasis, nbasis), jnp.bfloat16),
        ),
        in_specs=[smem_spec()] * 4
        + [any_spec()] * (EARLY + 2 * SOURCES + 1)
        + [vmem_spec()] * 2,
        out_specs=(vmem_spec(),) * 4,
        scratch_shapes=[pltpu.SemaphoreType.DMA] + density_buffers(EARLY),
        compiler_params=pltpu.CompilerParams(vmem_limit_bytes=VMEM_GRANT),
        cost_estimate=density_cost(EARLY),
        name="density_first",
    )(order, place, which, where, *chunks, *sources, table, weights, xc)


def density_last(order, chunks, table, dmat, pacc, weights, xc, home_rows, rho, top):
    count = PIECES - EARLY
    nbasis = NB * BLK
    return pl.pallas_call(
        density_last_body,
        out_shape=(
            jax.ShapeDtypeStruct((PIECES, 1, HALF), jnp.float32),
            jax.ShapeDtypeStruct((32, PAY_ROWS, 128), jnp.float32),
        ),
        in_specs=[smem_spec()] + [any_spec()] * (count + 3) + [vmem_spec()] * 5,
        out_specs=(vmem_spec(),) * 2,
        scratch_shapes=[
            pltpu.VMEM((2, nbasis, 128), jnp.float32),
            pltpu.VMEM((2, nbasis, nbasis), jnp.bfloat16),
            pltpu.VMEM((PAY_ROWS, 128), jnp.float32),
            pltpu.SemaphoreType.DMA((2,)),
        ]
        + density_buffers(count),
        compiler_params=pltpu.CompilerParams(vmem_limit_bytes=VMEM_GRANT),
        cost_estimate=density_cost(count),
        name="density_last",
    )(order, *chunks, table, dmat, pacc, weights, xc, home_rows, rho, top)


def potential_call(table, got, mine, weights, xc, rho, natoms):
    row = jax.ShapeDtypeStruct((PIECES, 1, HALF), jnp.float32)
    return pl.pallas_call(
        potential_body,
        out_shape=(
            jax.ShapeDtypeStruct((natoms, 64), jnp.float32),
            row,
            row,
            jax.ShapeDtypeStruct((1, 128), jnp.float32),
        ),
        in_specs=[any_spec()] + [vmem_spec()] * 5,
        out_specs=(vmem_spec(),) * 4,
        scratch_shapes=[
            pltpu.VMEM((3, NB * BLK, HALF), jnp.float32),
            pltpu.VMEM((2048, 128), jnp.float32),
            pltpu.VMEM((512, 128), jnp.float32),
            pltpu.SemaphoreType.DMA((3,)),
        ],
        compiler_params=pltpu.CompilerParams(vmem_limit_bytes=VMEM_GRANT),
        cost_estimate=pl.CostEstimate(
            flops=16 << 20, bytes_accessed=16 << 20, transcendentals=0
        ),
        name="potential",
    )(table, got, mine, weights, xc, rho)


def ham_call(order, slots, place, chunks, scale_mine, scale_beside):
    return pl.pallas_call(
        ham_body,
        out_shape=(jax.ShapeDtypeStruct((32, 128, BLK), jnp.float32),) * 4,
        in_specs=[smem_spec()] * 3 + [any_spec()] * (2 * CHUNKS) + [vmem_spec()] * 2,
        out_specs=(any_spec(),) * 4,
        scratch_shapes=[
            pltpu.VMEM((128, 128, BLK), jnp.float32),
            pltpu.VMEM((2, 2, 2, NB, 128, 4 * HALF), jnp.bfloat16),
            pltpu.VMEM((2, 2, 1, 4 * HALF), jnp.float32),
            pltpu.SemaphoreType.DMA,
            pltpu.SemaphoreType.DMA((4,)),
        ],
        compiler_params=pltpu.CompilerParams(vmem_limit_bytes=VMEM_GRANT),
        cost_estimate=pl.CostEstimate(
            flops=4096 * 1024 * 1024, bytes_accessed=24 << 20, transcendentals=0
        ),
        name="ham",
    )(
        order,
        slots,
        place,
        *[c.reshape(NB, 2, 128, c.shape[-1]) for c in chunks],
        scale_mine,
        scale_beside,
    )


def cast(x):
    return x.astype(jnp.float16)


def wide(x):
    return x.astype(jnp.float32)


def ring_sum(parts, factor):
    half = parts[2].shape[0] // 2
    up, down = core_perm(1, False), core_perm(-1, False)
    from_below = lax.ppermute(cast(parts[2][:half] * factor), "grid", up)
    from_above = lax.ppermute(cast(parts[2][half:] * factor), "grid", down)
    below_high = lax.ppermute(cast(parts[1][half:] * factor), "grid", up)
    above_low = lax.ppermute(cast(parts[3][:half] * factor), "grid", down)
    below_low = lax.ppermute(cast(parts[1][:half] * factor + wide(from_below)), "grid", up)
    above_high = lax.ppermute(cast(parts[3][half:] * factor + wide(from_above)), "grid", down)
    low = parts[0][:half] * factor + wide(below_low) + wide(above_low)
    high = parts[0][half:] * factor + wide(below_high) + wide(above_high)
    return [low[0], low[1], high[0], high[1]]


def direct_sum(parts):
    total = parts[0]
    got = [lax.ppermute(cast(parts[d]), "grid", core_perm(d, True)) for d in (2, 1, 3)]
    for g in got:
        total = total + wide(g)
    return total


def one_device(
    basis_values,
    point_coords,
    point_weights,
    xc_kernel,
    gauss_widths,
    atom_coords,
    resp_density,
    tile_list,
    tile_home,
    atom_list,
    atom_home,
):
    groups = lax.axis_size("grid")
    me = lax.axis_index("grid")
    plane = lax.axis_index("pert")
    my_z, my_x, my_c = me // 8, (me // 2) % 4, me % 2
    tile_dev = resp_density.shape[1]
    neighbors = atom_list.shape[1]
    moments = gauss_widths.shape[0]
    natoms = atom_home.shape[0]
    ntiles = tile_home.shape[0]
    slots_here = 2 * neighbors

    own0, own1 = basis_values[:HALF].T, basis_values[HALF:].T
    below0 = lax.ppermute(own0, "pert", ring(1))
    above1 = lax.ppermute(own1, "pert", ring(3))
    below1 = lax.ppermute(own1, "pert", ring(1))
    above0 = lax.ppermute(own0, "pert", ring(3))
    steps = jnp.array([0, 0, 3, 3, 1, 1, 2, 2], jnp.int32)
    halves = jnp.array([0, 1] * 4, jnp.int32)
    order = ((plane + steps) % 4) * 2 + halves

    swap = grid_perm(0, 0, 1)
    first_core = my_c == 0
    top_half, low_half = resp_density[0, :, :128], resp_density[0, :, 128:]
    kept = jnp.where(first_core, top_half, low_half)
    came = lax.ppermute(jnp.where(first_core, low_half, top_half), "grid", swap)
    base = jnp.concatenate(
        [jnp.where(first_core, kept, came), jnp.where(first_core, came, kept)], axis=0
    )
    ring_tiles = [lax.ppermute(base, "grid", core_perm(-d, False)) for d in (1, 2, 3)]

    wanted = tile_list.reshape(-1)
    tile_match = wanted[:, None] == jnp.arange(ntiles, dtype=jnp.int32)[None, :]
    homes = jnp.sum(jnp.where(tile_match, tile_home[None, :], 0), axis=1)
    homes_beside = lax.ppermute(homes, "grid", grid_perm(0, 0, 1))

    every_home = jnp.concatenate([homes, homes_beside])
    owner = every_home // tile_dev
    off_z = (owner // 8 - my_z) % 4
    off_x = ((owner // 2) % 4 - my_x) % 4
    ahead = jnp.where(my_c == 0, off_z * 4 + off_x, off_x * 4 + off_z)
    slots = ahead * (2 * tile_dev) + every_home % (2 * tile_dev)
    core_place = my_c.reshape(1).astype(jnp.int32)

    my_owner = homes // tile_dev
    to_z = (my_owner // 8 - my_z) % 4
    to_x = ((my_owner // 2) % 4 - my_x) % 4
    in_chip = homes % (2 * tile_dev)

    def found(one, two):
        source = jnp.where(two == 2, 2 + one // 2, jnp.where(two == 3, 4, two))
        return source, jnp.where(two == 2, one % 2, one) * (2 * tile_dev) + in_chip

    own_first = jnp.where(first_core, to_z, to_x)
    own_second = jnp.where(first_core, to_x, to_z)
    which_own, where_own = found(own_first, own_second)
    which_other, where_other = found(own_second, own_first)
    which = jnp.concatenate([which_own, which_other])
    where = jnp.concatenate([where_own, where_other])

    atom_match = atom_list[:, :, None] == jnp.arange(natoms, dtype=jnp.int32)
    atom_pos = jnp.sum(jnp.where(atom_match[None], atom_coords[:, None, None, :], 0.0), axis=3)
    atom_homes = jnp.sum(jnp.where(atom_match, atom_home, 0), axis=2).reshape(-1)
    delta = point_coords.reshape(3, 2, 4, 1, HALF) - atom_pos[:, :, None, :, None]
    dist_sq = (jnp.sum(delta * delta, axis=0) + SOFTEN).reshape(PIECES, neighbors, 1, HALF)
    spread = (2.0 * gauss_widths * gauss_widths)[None, None, :, None]
    erf_scale = (ROOT_TWO * gauss_widths)[None, None, :, None]
    gauss = jnp.exp(-dist_sq / spread).reshape(PIECES, neighbors * moments, HALF)
    distance = jnp.sqrt(dist_sq)
    hart = (lax.erf(distance / erf_scale) / distance).reshape(
        PIECES, neighbors * moments, HALF
    )
    weights = point_weights.reshape(PIECES, 1, HALF)
    xc = xc_kernel.reshape(PIECES, 1, HALF)

    ring_tiles, gauss = lax.optimization_barrier((ring_tiles, gauss))
    stored = jnp.concatenate([base] + ring_tiles, axis=0)
    ahead_tiles = lax.ppermute(stored, "grid", core_perm(-1, True))
    behind_tiles = lax.ppermute(stored, "grid", core_perm(1, True))

    lane = jnp.arange(128, dtype=jnp.int32)
    here = (lane // 16) == (me % 8)
    home_floats = atom_homes.astype(jnp.float32)
    home_rows = jnp.where(here[None, :], jnp.tile(home_floats.reshape(16, 2).T, (1, 8)), 0.0)
    my_homes = jnp.broadcast_to(home_floats[:, None], (slots_here, 128))
    below0, above1, hart = lax.optimization_barrier((below0, above1, hart))
    far0 = lax.ppermute(below0, "pert", ring(1))
    far1 = lax.ppermute(above1, "pert", ring(3))
    chunks = [own0, own1, below0, below1, above0, above1, far0, far1]
    beside = [lax.ppermute(chunk, "grid", swap) for chunk in chunks]

    ahead_tiles, behind_tiles, slots, home_rows, my_homes = lax.optimization_barrier(
        (ahead_tiles, behind_tiles, slots, home_rows, my_homes)
    )
    rows2 = 4 * tile_dev
    far_tiles0 = lax.ppermute(ahead_tiles[:rows2], "grid", core_perm(-1, True))
    far_tiles1 = lax.ppermute(behind_tiles[rows2:], "grid", core_perm(1, True))
    sources = [stored, ahead_tiles, far_tiles0, far_tiles1, behind_tiles]
    sources = sources + [lax.ppermute(s, "grid", swap) for s in sources]
    rho, pacc, top, dmat = density_first(
        order, core_place, which, where, chunks[:EARLY], sources, gauss, weights, xc
    )
    rho, sent = density_last(
        order, chunks[EARLY:], gauss, dmat, pacc, weights, xc, home_rows, rho, top
    )
    got = lax.all_to_all(sent, "grid", split_axis=0, concat_axis=0, tiled=True)
    all_coeffs, pot, scale, bound = potential_call(
        hart, got.reshape(groups * PAY_ROWS, 128), my_homes, weights, xc, rho, natoms
    )
    atom_dev = natoms // groups
    own_coeffs = lax.dynamic_slice_in_dim(all_coeffs, me * atom_dev, atom_dev, axis=0)
    ham_bound = PHI_MAX_SQ * 2048 * 0.05 * groups * bound[0, 0] * 1.01 + 1e-20

    scale_beside = lax.ppermute(scale, "grid", swap)
    factor = F16_TOP / ham_bound
    dense = ham_call(
        order,
        slots,
        core_place,
        chunks + beside,
        scale.reshape(2, 1, 4 * HALF),
        scale_beside.reshape(2, 1, 4 * HALF),
    )
    dense = [d.reshape(4, 2 * tile_dev, 128, BLK) for d in dense]
    chip = direct_sum(ring_sum(dense, factor))
    chip = chip.reshape(2, tile_dev, 128, BLK)
    keep = jnp.where(first_core, chip[0], chip[1])
    give = jnp.where(first_core, chip[1], chip[0])
    came = wide(lax.ppermute(cast(give), "grid", swap))
    hamiltonian = jnp.concatenate(
        [jnp.where(first_core, keep, came), jnp.where(first_core, came, keep)], axis=1
    ) * (ham_bound / F16_TOP)
    return (hamiltonian[None], own_coeffs[None], pot.reshape(1, -1))


def solution(mesh):
    placed = (
        P(("grid", "pert"), None),
        P(None, "grid"),
        P("grid"),
        P("grid"),
        P(),
        P(),
        P("pert", "grid", None, None),
        P("grid", None),
        P(),
        P("grid", None),
        P(),
    )
    return jax.shard_map(
        one_device,
        mesh=mesh,
        in_specs=placed,
        out_specs=(P("pert", "grid", None, None), P("pert", "grid", None), P("pert", "grid")),
        check_vma=False,
    )
```

```python
import jax
import jax.numpy as jnp
from jax import lax
from jax.experimental import pallas as pl
from jax.experimental.pallas import tpu as pltpu
from jax.sharding import PartitionSpec as P


SOFTEN = 0.25
ROOT_TWO = 1.4142135623730951
HALF = 512
PIECES = 8
CHUNKS = 8
VMEM_GRANT = 60 << 20
SOURCES = 8
BLK = 256
NB = 4
PHI_MAX_SQ = 36.0
KERNEL_MAX = 2.0
F16_TOP = 32000.0
PAY_ROWS = 24


def ring(shift):
    return [(i, (i + shift) % 4) for i in range(4)]


def grid_perm(dz, dx, dc):
    def at(z, x, c):
        return ((z % 4) * 4 + x % 4) * 2 + c

    return [
        (at(z, x, c), at(z + dz, x + dx, c ^ dc))
        for z in range(4)
        for x in range(4)
        for c in range(2)
    ]


def core_perm(shift, second):
    def at(z, x, c):
        return ((z % 4) * 4 + x % 4) * 2 + c

    pairs = []
    for z in range(4):
        for x in range(4):
            for c in range(2):
                along_z = (c == 0) != second
                there = at(z + shift, x, c) if along_z else at(z, x + shift, c)
                pairs.append((at(z, x, c), there))
    return pairs


def split3(x):
    first = x.astype(jnp.bfloat16)
    rest = x - first.astype(jnp.float32)
    second = rest.astype(jnp.bfloat16)
    third = (rest - second.astype(jnp.float32)).astype(jnp.bfloat16)
    return first, second, third


def fetch_tiles(core, which, where, sources, dmat, sem):
    for side in range(2):
        half = (1 - core) if side else core

        def fetch(n, _, side=side, half=half):
            b, row, col = n // 16, (n // 4) % 4, n % 4
            target = dmat.at[
                b,
                pl.ds(pl.multiple_of(row * BLK + half * 128, 128), 128),
                pl.ds(pl.multiple_of(col * BLK, BLK), BLK),
            ]
            at = side * 32 + n

            def pick(low, high):
                if high - low == 1:
                    pltpu.make_async_copy(
                        sources[side * SOURCES + low].at[where[at]], target, sem
                    ).start()
                    return
                middle = (low + high) // 2
                pl.when(which[at] < middle)(lambda: pick(low, middle))
                pl.when(which[at] >= middle)(lambda: pick(middle, high))

            pick(0, SOURCES)
            return 0

        lax.fori_loop(0, 32, fetch, 0)


def density_steps(order, chunks, dmat, sem, table, weights, xc, rho, pacc, bufs, top):
    held, tbuf, psem, tsem = bufs
    for i in range(CHUNKS):
        pltpu.make_async_copy(chunks[i], held.at[i], psem.at[i]).start()
    pltpu.make_async_copy(table.at[order[0]], tbuf.at[0], tsem.at[0]).start()
    pltpu.make_async_copy(dmat, dmat, sem).wait()

    def step(i, top):
        slot = lax.rem(i, 2)

        @pl.when(i + 1 < CHUNKS)
        def _():
            pltpu.make_async_copy(
                table.at[order[i + 1]], tbuf.at[1 - slot], tsem.at[1 - slot]
            ).start()

        pi = order[i]
        b = pi // 4
        pltpu.make_async_copy(held.at[i], held.at[i], psem.at[i]).wait()
        piece = held[i]
        total = jnp.zeros((1, HALF), jnp.float32)
        for block in range(NB):
            rows = pl.ds(block * BLK, BLK)
            mixed = jnp.dot(dmat[b, rows, :], piece, preferred_element_type=jnp.float32)
            total = total + jnp.sum(
                mixed * held[i, rows, :].astype(jnp.float32), axis=0, keepdims=True
            )
        rho[pi] = total
        weighted = weights[pi] * total
        pltpu.make_async_copy(table.at[pi], tbuf.at[slot], tsem.at[slot]).wait()
        for block in range(8):
            rows = pl.ds(block * 128, 128)
            part = pacc[b, rows, :]
            for lane in range(HALF // 128):
                cols = slice(lane * 128, (lane + 1) * 128)
                part = part + tbuf[slot, rows, cols] * weighted[:, cols]
            pacc[b, rows, :] = part
        return jnp.maximum(top, jnp.abs(xc[pi] * total))

    return lax.fori_loop(0, CHUNKS, step, top)


def density_body(order, place, which, where, *refs):
    chunks = refs[:CHUNKS]
    sources = refs[CHUNKS : CHUNKS + 2 * SOURCES]
    table, weights, xc, home_rows, rho, sent, *rest = refs[CHUNKS + 2 * SOURCES :]
    pacc, dmat, block_out, sem, *bufs = rest
    fetch_tiles(place[0], which, where, sources, dmat, sem)
    pacc[...] = jnp.zeros_like(pacc)
    block_out[...] = jnp.zeros_like(block_out)
    block_out[pl.ds(17, 2), :] = home_rows[...]
    top = density_steps(
        order, chunks, dmat, sem, table, weights, xc, rho, pacc, bufs,
        jnp.zeros((1, HALF), jnp.float32),
    )
    ones = jnp.ones((8, 128), jnp.bfloat16)
    for b in range(2):
        total = jnp.zeros((8, NB * BLK), jnp.float32)
        for term in split3(pacc[b]):
            total = total + lax.dot_general(
                ones, term, (((1,), (1,)), ((), ())), preferred_element_type=jnp.float32
            )
        for r in range(8):
            block_out[pl.ds(b * 8 + r, 1), :] = total[0:1, r * 128 : (r + 1) * 128]
    block_out[pl.ds(16, 1), :] = jnp.broadcast_to(jnp.max(top, axis=1, keepdims=True), (1, 128))
    for dest in range(32):
        sent[dest] = block_out[...]


def potential_body(table, got, mine, weights, xc, rho, coeffs, pot, scale, bound, *scratch):
    tbuf, column, data, tsem = scratch
    for i in range(2):
        pltpu.make_async_copy(table.at[i], tbuf.at[i], tsem.at[i]).start()
    natoms = coeffs.shape[0]
    homes = []
    for which in range(2):
        segments = []
        for group in range(4):
            row = jnp.zeros((1, 128), jnp.float32)
            for k in range(8):
                row = row + got[pl.ds((group * 8 + k) * PAY_ROWS + 17 + which, 1), :]
            segments.append(row)
        homes.append(jnp.concatenate(segments, axis=1))
    for k in range(32):
        data[pl.ds(k * 16, 16), :] = got[pl.ds(k * PAY_ROWS, 16), :]
    stored = lax.broadcasted_iota(jnp.int32, (natoms, 128), 0).astype(jnp.float32)
    wanted = jnp.concatenate([stored, mine[...]], axis=0)
    wanted = jnp.concatenate([wanted] * 4, axis=1)
    even, odd = [
        jnp.where(wanted == row, 1.0, 0.0).astype(jnp.bfloat16)
        for row in homes
    ]
    first = jnp.zeros((natoms + 32, 128), jnp.float32)
    second = jnp.zeros((natoms + 32, 128), jnp.float32)
    for term in split3(data[...]):
        first = first + jnp.dot(even, term, preferred_element_type=jnp.float32)
        second = second + jnp.dot(odd, term, preferred_element_type=jnp.float32)
    summed = first[:, :64] + second[:, 64:]
    coeffs[...] = summed[:natoms]
    turned = summed[natoms:].T
    for k in range(32):
        column[pl.ds(k * 64, 64), :] = jnp.broadcast_to(turned[:, k : k + 1], (64, 128))
    top = jnp.zeros((1, 128), jnp.float32)
    for k in range(32):
        top = jnp.maximum(top, got[pl.ds(k * PAY_ROWS + 16, 1), :])
    heavy = jnp.max(jnp.sum(jnp.abs(summed[:natoms]), axis=1, keepdims=True), axis=0, keepdims=True)
    bound[...] = top + jnp.broadcast_to(heavy, (1, 128)) * (KERNEL_MAX * 16)

    def step(i, _):
        slot = lax.rem(i, 3)

        @pl.when(i + 2 < PIECES)
        def _():
            ahead = lax.rem(i + 2, 3)
            pltpu.make_async_copy(table.at[i + 2], tbuf.at[ahead], tsem.at[ahead]).start()

        base = (i // 4) * 1024
        pltpu.make_async_copy(table.at[i], tbuf.at[slot], tsem.at[slot]).wait()
        parts = [jnp.zeros((8, 128), jnp.float32) for _ in range(HALF // 128)]
        for block in range(16):
            factor = column[pl.ds(base + block * 64, 64), :]
            for lane in range(HALF // 128):
                prod = tbuf[slot, block * 64 : (block + 1) * 64, lane * 128 : (lane + 1) * 128]
                parts[lane] = parts[lane] + jnp.sum((prod * factor).reshape(8, 8, 128), axis=0)
        hartree = jnp.concatenate([jnp.sum(p, axis=0, keepdims=True) for p in parts], axis=1)
        potential = hartree + xc[i] * rho[i]
        pot[i] = potential
        scale[i] = weights[i] * potential
        return 0

    lax.fori_loop(0, PIECES, step, 0)


def ham_body(order, slots, place, *refs):
    chunks = refs[: 2 * CHUNKS]
    scale_mine, scale_beside, *rest = refs[2 * CHUNKS :]
    outs, (dense, held, rows_of, psem, osem) = rest[:4], rest[4:]
    core = place[0]
    for side in range(2):
        i = 0
        for ref in chunks[side * CHUNKS : (side + 1) * CHUNKS]:
            width = ref.shape[-1]
            pi = order[i]
            lanes = pl.ds(pl.multiple_of((pi % 4) * HALF, HALF), width)
            for half in range(2):
                at = (1 - core) if half else core
                pltpu.make_async_copy(
                    ref.at[:, half], held.at[side, pi // 4, at, :, :, lanes], psem
                ).start()
            i += width // HALF
    for b in range(2):
        rows_of[0, b] = scale_mine[b]
        rows_of[1, b] = scale_beside[b]

    def clear(s, _):
        dense[s] = jnp.zeros(dense.shape[1:], jnp.float32)
        return 0

    lax.fori_loop(0, dense.shape[0], clear, 0)
    pltpu.make_async_copy(held, held, psem).wait()

    def product(side, b, col):
        left = held[side, b, 0].reshape(2 * BLK, 4 * HALF)
        right = jnp.concatenate([held[side, b, core, col], held[side, b, 1 - core, col]], axis=0)
        right = (right.astype(jnp.float32) * rows_of[side, b]).astype(jnp.bfloat16)
        return lax.dot_general(
            left, right, (((1,), (1,)), ((), ())), preferred_element_type=jnp.float32
        )

    def step(n, _):
        side, b, cols = n // 4, (n // 2) % 2, (n % 2) * 2
        parts = [product(side, b, cols + k) for k in range(2)]
        for k in range(2):
            for row in range(NB):
                slot = slots[side * 32 + b * 16 + row * NB + cols + k]
                dense[slot] += parts[k][row * 128 : (row + 1) * 128]
        return 0

    lax.fori_loop(0, 8, step, 0)
    for d in range(4):
        pltpu.make_async_copy(dense.at[pl.ds(d * 32, 32)], outs[d], osem.at[d]).start()
    for d in range(4):
        pltpu.make_async_copy(dense.at[pl.ds(d * 32, 32)], outs[d], osem.at[d]).wait()


def any_spec():
    return pl.BlockSpec(memory_space=pltpu.HBM)


def vmem_spec():
    return pl.BlockSpec(memory_space=pltpu.VMEM)


def smem_spec():
    return pl.BlockSpec(memory_space=pltpu.SMEM)


def density_call(order, place, which, where, chunks, sources, table, weights, xc, home_rows):
    nbasis = NB * BLK
    return pl.pallas_call(
        density_body,
        out_shape=(
            jax.ShapeDtypeStruct((PIECES, 1, HALF), jnp.float32),
            jax.ShapeDtypeStruct((32, PAY_ROWS, 128), jnp.float32),
        ),
        in_specs=[smem_spec()] * 4
        + [any_spec()] * (CHUNKS + 2 * SOURCES + 1)
        + [vmem_spec()] * 3,
        out_specs=(vmem_spec(),) * 2,
        scratch_shapes=[
            pltpu.VMEM((2, nbasis, 128), jnp.float32),
            pltpu.VMEM((2, nbasis, nbasis), jnp.bfloat16),
            pltpu.VMEM((PAY_ROWS, 128), jnp.float32),
            pltpu.SemaphoreType.DMA,
            pltpu.VMEM((CHUNKS, nbasis, HALF), jnp.bfloat16),
            pltpu.VMEM((2, nbasis, HALF), jnp.float32),
            pltpu.SemaphoreType.DMA((CHUNKS,)),
            pltpu.SemaphoreType.DMA((2,)),
        ],
        compiler_params=pltpu.CompilerParams(vmem_limit_bytes=VMEM_GRANT),
        cost_estimate=pl.CostEstimate(
            flops=2 * 4096 * 1024 * 1024, bytes_accessed=32 << 20, transcendentals=0
        ),
        name="density",
    )(order, place, which, where, *chunks, *sources, table, weights, xc, home_rows)


def potential_call(table, got, mine, weights, xc, rho, natoms):
    row = jax.ShapeDtypeStruct((PIECES, 1, HALF), jnp.float32)
    return pl.pallas_call(
        potential_body,
        out_shape=(
            jax.ShapeDtypeStruct((natoms, 64), jnp.float32),
            row,
            row,
            jax.ShapeDtypeStruct((1, 128), jnp.float32),
        ),
        in_specs=[any_spec()] + [vmem_spec()] * 5,
        out_specs=(vmem_spec(),) * 4,
        scratch_shapes=[
            pltpu.VMEM((3, NB * BLK, HALF), jnp.float32),
            pltpu.VMEM((2048, 128), jnp.float32),
            pltpu.VMEM((512, 128), jnp.float32),
            pltpu.SemaphoreType.DMA((3,)),
        ],
        compiler_params=pltpu.CompilerParams(vmem_limit_bytes=VMEM_GRANT),
        cost_estimate=pl.CostEstimate(
            flops=16 << 20, bytes_accessed=16 << 20, transcendentals=0
        ),
        name="potential",
    )(table, got, mine, weights, xc, rho)


def ham_call(order, slots, place, chunks, scale_mine, scale_beside):
    return pl.pallas_call(
        ham_body,
        out_shape=(jax.ShapeDtypeStruct((32, 128, BLK), jnp.float32),) * 4,
        in_specs=[smem_spec()] * 3 + [any_spec()] * (2 * CHUNKS) + [vmem_spec()] * 2,
        out_specs=(any_spec(),) * 4,
        scratch_shapes=[
            pltpu.VMEM((128, 128, BLK), jnp.float32),
            pltpu.VMEM((2, 2, 2, NB, 128, 4 * HALF), jnp.bfloat16),
            pltpu.VMEM((2, 2, 1, 4 * HALF), jnp.float32),
            pltpu.SemaphoreType.DMA,
            pltpu.SemaphoreType.DMA((4,)),
        ],
        compiler_params=pltpu.CompilerParams(vmem_limit_bytes=VMEM_GRANT),
        cost_estimate=pl.CostEstimate(
            flops=4096 * 1024 * 1024, bytes_accessed=24 << 20, transcendentals=0
        ),
        name="ham",
    )(
        order,
        slots,
        place,
        *[c.reshape(NB, 2, 128, c.shape[-1]) for c in chunks],
        scale_mine,
        scale_beside,
    )


def cast(x):
    return x.astype(jnp.float16)


def wide(x):
    return x.astype(jnp.float32)


def ring_sum(parts, factor):
    half = parts[2].shape[0] // 2
    up, down = core_perm(1, False), core_perm(-1, False)
    from_below = lax.ppermute(cast(parts[2][:half] * factor), "grid", up)
    from_above = lax.ppermute(cast(parts[2][half:] * factor), "grid", down)
    below_high = lax.ppermute(cast(parts[1][half:] * factor), "grid", up)
    above_low = lax.ppermute(cast(parts[3][:half] * factor), "grid", down)
    below_low = lax.ppermute(cast(parts[1][:half] * factor + wide(from_below)), "grid", up)
    above_high = lax.ppermute(cast(parts[3][half:] * factor + wide(from_above)), "grid", down)
    low = parts[0][:half] * factor + wide(below_low) + wide(above_low)
    high = parts[0][half:] * factor + wide(below_high) + wide(above_high)
    return [low[0], low[1], high[0], high[1]]


def direct_sum(parts):
    total = parts[0]
    got = [lax.ppermute(cast(parts[d]), "grid", core_perm(d, True)) for d in (2, 1, 3)]
    for g in got:
        total = total + wide(g)
    return total


def one_device(
    basis_values,
    point_coords,
    point_weights,
    xc_kernel,
    gauss_widths,
    atom_coords,
    resp_density,
    tile_list,
    tile_home,
    atom_list,
    atom_home,
):
    groups = lax.axis_size("grid")
    me = lax.axis_index("grid")
    plane = lax.axis_index("pert")
    my_z, my_x, my_c = me // 8, (me // 2) % 4, me % 2
    tile_dev = resp_density.shape[1]
    neighbors = atom_list.shape[1]
    moments = gauss_widths.shape[0]
    natoms = atom_home.shape[0]
    ntiles = tile_home.shape[0]
    slots_here = 2 * neighbors

    own0, own1 = basis_values[:HALF].T, basis_values[HALF:].T
    below0 = lax.ppermute(own0, "pert", ring(1))
    above1 = lax.ppermute(own1, "pert", ring(3))
    below1 = lax.ppermute(own1, "pert", ring(1))
    above0 = lax.ppermute(own0, "pert", ring(3))
    steps = jnp.array([0, 0, 3, 3, 1, 1, 2, 2], jnp.int32)
    halves = jnp.array([0, 1] * 4, jnp.int32)
    order = ((plane + steps) % 4) * 2 + halves

    swap = grid_perm(0, 0, 1)
    first_core = my_c == 0
    top_half, low_half = resp_density[0, :, :128], resp_density[0, :, 128:]
    kept = jnp.where(first_core, top_half, low_half)
    came = lax.ppermute(jnp.where(first_core, low_half, top_half), "grid", swap)
    base = jnp.concatenate(
        [jnp.where(first_core, kept, came), jnp.where(first_core, came, kept)], axis=0
    )
    ring_tiles = [lax.ppermute(base, "grid", core_perm(-d, False)) for d in (1, 2, 3)]

    wanted = tile_list.reshape(-1)
    tile_match = wanted[:, None] == jnp.arange(ntiles, dtype=jnp.int32)[None, :]
    homes = jnp.sum(jnp.where(tile_match, tile_home[None, :], 0), axis=1)
    homes_beside = lax.ppermute(homes, "grid", grid_perm(0, 0, 1))

    every_home = jnp.concatenate([homes, homes_beside])
    owner = every_home // tile_dev
    off_z = (owner // 8 - my_z) % 4
    off_x = ((owner // 2) % 4 - my_x) % 4
    ahead = jnp.where(my_c == 0, off_z * 4 + off_x, off_x * 4 + off_z)
    slots = ahead * (2 * tile_dev) + every_home % (2 * tile_dev)
    core_place = my_c.reshape(1).astype(jnp.int32)

    my_owner = homes // tile_dev
    to_z = (my_owner // 8 - my_z) % 4
    to_x = ((my_owner // 2) % 4 - my_x) % 4
    in_chip = homes % (2 * tile_dev)

    def found(one, two):
        return two * 2 + one // 2, (one % 2) * (2 * tile_dev) + in_chip

    own_first = jnp.where(first_core, to_z, to_x)
    own_second = jnp.where(first_core, to_x, to_z)
    which_own, where_own = found(own_first, own_second)
    which_other, where_other = found(own_second, own_first)
    which = jnp.concatenate([which_own, which_other])
    where = jnp.concatenate([where_own, where_other])

    atom_match = atom_list[:, :, None] == jnp.arange(natoms, dtype=jnp.int32)
    atom_pos = jnp.sum(jnp.where(atom_match[None], atom_coords[:, None, None, :], 0.0), axis=3)
    atom_homes = jnp.sum(jnp.where(atom_match, atom_home, 0), axis=2).reshape(-1)
    delta = point_coords.reshape(3, 2, 4, 1, HALF) - atom_pos[:, :, None, :, None]
    dist_sq = (jnp.sum(delta * delta, axis=0) + SOFTEN).reshape(PIECES, neighbors, 1, HALF)
    spread = (2.0 * gauss_widths * gauss_widths)[None, None, :, None]
    erf_scale = (ROOT_TWO * gauss_widths)[None, None, :, None]
    gauss = jnp.exp(-dist_sq / spread).reshape(PIECES, neighbors * moments, HALF)
    distance = jnp.sqrt(dist_sq)
    hart = (lax.erf(distance / erf_scale) / distance).reshape(
        PIECES, neighbors * moments, HALF
    )
    weights = point_weights.reshape(PIECES, 1, HALF)
    xc = xc_kernel.reshape(PIECES, 1, HALF)

    lane = jnp.arange(128, dtype=jnp.int32)
    here = (lane // 16) == (me % 8)
    home_floats = atom_homes.astype(jnp.float32)
    home_rows = jnp.where(here[None, :], jnp.tile(home_floats.reshape(16, 2).T, (1, 8)), 0.0)
    my_homes = jnp.broadcast_to(home_floats[:, None], (slots_here, 128))

    back, forth = core_perm(-1, True), core_perm(1, True)
    near = jnp.concatenate([base, ring_tiles[0]], axis=0)
    other = jnp.concatenate([ring_tiles[1], ring_tiles[2]], axis=0)
    near_ahead = lax.ppermute(near, "grid", back)
    other_behind = lax.ppermute(other, "grid", forth)
    near_behind = lax.ppermute(near, "grid", forth)
    other_ahead = lax.ppermute(other, "grid", back)
    near_ahead, slots, home_rows, my_homes, which, where = lax.optimization_barrier(
        (near_ahead, slots, home_rows, my_homes, which, where)
    )
    near_far = lax.ppermute(near_ahead, "grid", back)
    other_far = lax.ppermute(other_behind, "grid", forth)
    sources = [
        near, other, near_ahead, other_ahead, near_far, other_far, near_behind, other_behind,
    ]
    sources = sources + [lax.ppermute(s, "grid", swap) for s in sources]

    far0 = lax.ppermute(below0, "pert", ring(1))
    far1 = lax.ppermute(above1, "pert", ring(3))
    chunks = [own0, own1, below0, below1, above0, above1, far0, far1]
    beside = [lax.ppermute(chunk, "grid", swap) for chunk in chunks]

    rho, sent = density_call(
        order, core_place, which, where, chunks, sources, gauss, weights, xc, home_rows
    )
    got = lax.all_to_all(sent, "grid", split_axis=0, concat_axis=0, tiled=True)
    all_coeffs, pot, scale, bound = potential_call(
        hart, got.reshape(groups * PAY_ROWS, 128), my_homes, weights, xc, rho, natoms
    )
    atom_dev = natoms // groups
    own_coeffs = lax.dynamic_slice_in_dim(all_coeffs, me * atom_dev, atom_dev, axis=0)
    ham_bound = PHI_MAX_SQ * 2048 * 0.05 * groups * bound[0, 0] * 1.01 + 1e-20

    scale_beside = lax.ppermute(scale, "grid", swap)
    factor = F16_TOP / ham_bound
    dense = ham_call(
        order,
        slots,
        core_place,
        chunks + beside,
        scale.reshape(2, 1, 4 * HALF),
        scale_beside.reshape(2, 1, 4 * HALF),
    )
    dense = [d.reshape(4, 2 * tile_dev, 128, BLK) for d in dense]
    chip = direct_sum(ring_sum(dense, factor))
    chip = chip.reshape(2, tile_dev, 128, BLK)
    keep = jnp.where(first_core, chip[0], chip[1])
    give = jnp.where(first_core, chip[1], chip[0])
    came = wide(lax.ppermute(cast(give), "grid", swap))
    hamiltonian = jnp.concatenate(
        [jnp.where(first_core, keep, came), jnp.where(first_core, came, keep)], axis=1
    ) * (ham_bound / F16_TOP)
    return (hamiltonian[None], own_coeffs[None], pot.reshape(1, -1))


def solution(mesh):
    placed = (
        P(("grid", "pert"), None),
        P(None, "grid"),
        P("grid"),
        P("grid"),
        P(),
        P(),
        P("pert", "grid", None, None),
        P("grid", None),
        P(),
        P("grid", None),
        P(),
    )
    return jax.shard_map(
        one_device,
        mesh=mesh,
        in_specs=placed,
        out_specs=(P("pert", "grid", None, None), P("pert", "grid", None), P("pert", "grid")),
        check_vma=False,
    )
```

```python
import jax
import jax.numpy as jnp
from jax import lax
from jax.experimental import pallas as pl
from jax.experimental.pallas import tpu as pltpu
from jax.sharding import PartitionSpec as P


SOFTEN = 0.25
ROOT_TWO = 1.4142135623730951
HALF = 512
PIECES = 8
CHUNKS = 8
VMEM_GRANT = 60 << 20
SOURCES = 8
BLK = 256
NB = 4
PHI_MAX_SQ = 36.0
KERNEL_MAX = 2.0
F16_TOP = 32000.0
PAY_ROWS = 24


def ring(shift):
    return [(i, (i + shift) % 4) for i in range(4)]


def grid_perm(dz, dx, dc):
    def at(z, x, c):
        return ((z % 4) * 4 + x % 4) * 2 + c

    return [
        (at(z, x, c), at(z + dz, x + dx, c ^ dc))
        for z in range(4)
        for x in range(4)
        for c in range(2)
    ]


def core_perm(shift, second):
    def at(z, x, c):
        return ((z % 4) * 4 + x % 4) * 2 + c

    pairs = []
    for z in range(4):
        for x in range(4):
            for c in range(2):
                along_z = (c == 0) != second
                there = at(z + shift, x, c) if along_z else at(z, x + shift, c)
                pairs.append((at(z, x, c), there))
    return pairs


def split3(x):
    first = x.astype(jnp.bfloat16)
    rest = x - first.astype(jnp.float32)
    second = rest.astype(jnp.bfloat16)
    third = (rest - second.astype(jnp.float32)).astype(jnp.bfloat16)
    return first, second, third


def fetch_tiles(core, which, where, sources, dmat, sem):
    for side in range(2):
        half = (1 - core) if side else core

        def fetch(n, _, side=side, half=half):
            b, row, col = n // 16, (n // 4) % 4, n % 4
            target = dmat.at[
                b,
                pl.ds(pl.multiple_of(row * BLK + half * 128, 128), 128),
                pl.ds(pl.multiple_of(col * BLK, BLK), BLK),
            ]
            at = side * 32 + n

            def pick(low, high):
                if high - low == 1:
                    pltpu.make_async_copy(
                        sources[side * SOURCES + low].at[where[at]], target, sem
                    ).start()
                    return
                middle = (low + high) // 2
                pl.when(which[at] < middle)(lambda: pick(low, middle))
                pl.when(which[at] >= middle)(lambda: pick(middle, high))

            pick(0, SOURCES)
            return 0

        lax.fori_loop(0, 32, fetch, 0)


def density_steps(order, dmat, sem, table, weights, xc, rho, pacc, bufs, top):
    held, tbuf, psem, tsem = bufs
    pltpu.make_async_copy(dmat, dmat, sem).wait()

    def step(i, top):
        pi = order[i]
        b = pi // 4
        pltpu.make_async_copy(held.at[i], held.at[i], psem.at[i]).wait()
        piece = held[i]
        total = jnp.zeros((1, HALF), jnp.float32)
        for block in range(NB):
            rows = pl.ds(block * BLK, BLK)
            mixed = jnp.dot(dmat[b, rows, :], piece, preferred_element_type=jnp.float32)
            total = total + jnp.sum(
                mixed * held[i, rows, :].astype(jnp.float32), axis=0, keepdims=True
            )
        rho[pi] = total
        weighted = weights[pi] * total
        pltpu.make_async_copy(table.at[pi], tbuf.at[i], tsem.at[i]).wait()
        for block in range(8):
            rows = pl.ds(block * 128, 128)
            part = pacc[b, rows, :]
            for lane in range(HALF // 128):
                cols = slice(lane * 128, (lane + 1) * 128)
                part = part + tbuf[i, rows, cols] * weighted[:, cols]
            pacc[b, rows, :] = part
        return jnp.maximum(top, jnp.abs(xc[pi] * total))

    return lax.fori_loop(0, CHUNKS, step, top)


def assemble_body(place, which, where, *refs):
    *sources, dmat, sem = refs
    fetch_tiles(place[0], which, where, sources, dmat, sem)
    pltpu.make_async_copy(dmat, dmat, sem).wait()


def density_body(order, *refs):
    chunks = refs[:CHUNKS]
    table, dmat_in, weights, xc, home_rows, rho, sent, *rest = refs[CHUNKS:]
    pacc, dmat, block_out, sem, *bufs = rest
    held, tbuf, psem, tsem = bufs

    def load(i):
        pltpu.make_async_copy(chunks[i], held.at[i], psem.at[i]).start()
        pltpu.make_async_copy(table.at[order[i]], tbuf.at[i], tsem.at[i]).start()

    pltpu.make_async_copy(dmat_in, dmat, sem).start()
    for i in range(CHUNKS):
        load(i)
    pacc[...] = jnp.zeros_like(pacc)
    block_out[...] = jnp.zeros_like(block_out)
    block_out[pl.ds(17, 2), :] = home_rows[...]
    top = density_steps(
        order, dmat, sem, table, weights, xc, rho, pacc, bufs, jnp.zeros((1, HALF), jnp.float32)
    )
    ones = jnp.ones((8, 128), jnp.bfloat16)
    for b in range(2):
        total = jnp.zeros((8, NB * BLK), jnp.float32)
        for term in split3(pacc[b]):
            total = total + lax.dot_general(
                ones, term, (((1,), (1,)), ((), ())), preferred_element_type=jnp.float32
            )
        for r in range(8):
            block_out[pl.ds(b * 8 + r, 1), :] = total[0:1, r * 128 : (r + 1) * 128]
    block_out[pl.ds(16, 1), :] = jnp.broadcast_to(jnp.max(top, axis=1, keepdims=True), (1, 128))
    for dest in range(32):
        sent[dest] = block_out[...]


def potential_body(table, got, mine, weights, xc, rho, coeffs, pot, scale, bound, *scratch):
    tbuf, column, data, tsem = scratch
    for i in range(PIECES):
        pltpu.make_async_copy(table.at[i], tbuf.at[i], tsem.at[i]).start()
    natoms = coeffs.shape[0]
    homes = []
    for which in range(2):
        segments = []
        for group in range(4):
            row = jnp.zeros((1, 128), jnp.float32)
            for k in range(8):
                row = row + got[pl.ds((group * 8 + k) * PAY_ROWS + 17 + which, 1), :]
            segments.append(row)
        homes.append(jnp.concatenate(segments, axis=1))
    for k in range(32):
        data[pl.ds(k * 16, 16), :] = got[pl.ds(k * PAY_ROWS, 16), :]
    stored = lax.broadcasted_iota(jnp.int32, (natoms, 128), 0).astype(jnp.float32)
    wanted = jnp.concatenate([stored, mine[...]], axis=0)
    wanted = jnp.concatenate([wanted] * 4, axis=1)
    even, odd = [
        jnp.where(wanted == row, 1.0, 0.0).astype(jnp.bfloat16)
        for row in homes
    ]
    first = jnp.zeros((natoms + 32, 128), jnp.float32)
    second = jnp.zeros((natoms + 32, 128), jnp.float32)
    for term in split3(data[...]):
        first = first + jnp.dot(even, term, preferred_element_type=jnp.float32)
        second = second + jnp.dot(odd, term, preferred_element_type=jnp.float32)
    summed = first[:, :64] + second[:, 64:]
    coeffs[...] = summed[:natoms]
    turned = summed[natoms:].T
    for k in range(32):
        column[pl.ds(k * 64, 64), :] = jnp.broadcast_to(turned[:, k : k + 1], (64, 128))
    top = jnp.zeros((1, 128), jnp.float32)
    for k in range(32):
        top = jnp.maximum(top, got[pl.ds(k * PAY_ROWS + 16, 1), :])
    heavy = jnp.max(jnp.sum(jnp.abs(summed[:natoms]), axis=1, keepdims=True), axis=0, keepdims=True)
    bound[...] = top + jnp.broadcast_to(heavy, (1, 128)) * (KERNEL_MAX * 16)

    def step(i, _):
        base = (i // 4) * 1024
        pltpu.make_async_copy(table.at[i], tbuf.at[i], tsem.at[i]).wait()
        parts = [jnp.zeros((8, 128), jnp.float32) for _ in range(HALF // 128)]
        for block in range(16):
            factor = column[pl.ds(base + block * 64, 64), :]
            for lane in range(HALF // 128):
                prod = tbuf[i, block * 64 : (block + 1) * 64, lane * 128 : (lane + 1) * 128]
                parts[lane] = parts[lane] + jnp.sum((prod * factor).reshape(8, 8, 128), axis=0)
        hartree = jnp.concatenate([jnp.sum(p, axis=0, keepdims=True) for p in parts], axis=1)
        potential = hartree + xc[i] * rho[i]
        pot[i] = potential
        scale[i] = weights[i] * potential
        return 0

    lax.fori_loop(0, PIECES, step, 0)


def ham_body(order, slots, place, *refs):
    chunks = refs[: 2 * CHUNKS]
    scale_mine, scale_beside, *rest = refs[2 * CHUNKS :]
    outs, (dense, held, rows_of, psem, osem) = rest[:4], rest[4:]
    core = place[0]
    for side in range(2):
        i = 0
        for ref in chunks[side * CHUNKS : (side + 1) * CHUNKS]:
            width = ref.shape[-1]
            pi = order[i]
            lanes = pl.ds(pl.multiple_of((pi % 4) * HALF, HALF), width)
            for half in range(2):
                at = (1 - core) if half else core
                pltpu.make_async_copy(
                    ref.at[:, half],
                    held.at[side, pi // 4, at, :, :, lanes],
                    psem.at[side * 2 + pi // 4],
                ).start()
            i += width // HALF
    for b in range(2):
        rows_of[0, b] = scale_mine[b]
        rows_of[1, b] = scale_beside[b]

    def clear(s, _):
        dense[s] = jnp.zeros(dense.shape[1:], jnp.float32)
        return 0

    lax.fori_loop(0, dense.shape[0], clear, 0)

    def product(side, b, col):
        left = held[side, b, 0].reshape(2 * BLK, 4 * HALF)
        right = jnp.concatenate([held[side, b, core, col], held[side, b, 1 - core, col]], axis=0)
        right = (right.astype(jnp.float32) * rows_of[side, b]).astype(jnp.bfloat16)
        return lax.dot_general(
            left, right, (((1,), (1,)), ((), ())), preferred_element_type=jnp.float32
        )

    def step(n, _):
        side, b, cols = n // 4, (n // 2) % 2, (n % 2) * 2

        @pl.when(cols == 0)
        def _():
            batch = held.at[side, b]
            pltpu.make_async_copy(batch, batch, psem.at[side * 2 + b]).wait()

        parts = [product(side, b, cols + k) for k in range(2)]
        for k in range(2):
            for row in range(NB):
                slot = slots[side * 32 + b * 16 + row * NB + cols + k]
                dense[slot] += parts[k][row * 128 : (row + 1) * 128]
        return 0

    lax.fori_loop(0, 8, step, 0)
    for d in range(4):
        pltpu.make_async_copy(dense.at[pl.ds(d * 32, 32)], outs[d], osem.at[d]).start()
    for d in range(4):
        pltpu.make_async_copy(dense.at[pl.ds(d * 32, 32)], outs[d], osem.at[d]).wait()


def any_spec():
    return pl.BlockSpec(memory_space=pltpu.HBM)


def vmem_spec():
    return pl.BlockSpec(memory_space=pltpu.VMEM)


def smem_spec():
    return pl.BlockSpec(memory_space=pltpu.SMEM)


def assemble_call(place, which, where, sources):
    nbasis = NB * BLK
    return pl.pallas_call(
        assemble_body,
        out_shape=jax.ShapeDtypeStruct((2, nbasis, nbasis), jnp.bfloat16),
        in_specs=[smem_spec()] * 3 + [any_spec()] * (2 * SOURCES),
        out_specs=vmem_spec(),
        scratch_shapes=[pltpu.SemaphoreType.DMA],
        compiler_params=pltpu.CompilerParams(vmem_limit_bytes=VMEM_GRANT),
        cost_estimate=pl.CostEstimate(flops=0, bytes_accessed=8 << 20, transcendentals=0),
        name="assemble",
    )(place, which, where, *sources)


def density_call(order, chunks, table, dmat, weights, xc, home_rows):
    nbasis = NB * BLK
    return pl.pallas_call(
        density_body,
        out_shape=(
            jax.ShapeDtypeStruct((PIECES, 1, HALF), jnp.float32),
            jax.ShapeDtypeStruct((32, PAY_ROWS, 128), jnp.float32),
        ),
        in_specs=[smem_spec()] + [any_spec()] * (CHUNKS + 2) + [vmem_spec()] * 3,
        out_specs=(vmem_spec(),) * 2,
        scratch_shapes=[
            pltpu.VMEM((2, nbasis, 128), jnp.float32),
            pltpu.VMEM((2, nbasis, nbasis), jnp.bfloat16),
            pltpu.VMEM((PAY_ROWS, 128), jnp.float32),
            pltpu.SemaphoreType.DMA,
            pltpu.VMEM((CHUNKS, nbasis, HALF), jnp.bfloat16),
            pltpu.VMEM((CHUNKS, nbasis, HALF), jnp.float32),
            pltpu.SemaphoreType.DMA((CHUNKS,)),
            pltpu.SemaphoreType.DMA((CHUNKS,)),
        ],
        compiler_params=pltpu.CompilerParams(vmem_limit_bytes=VMEM_GRANT),
        cost_estimate=pl.CostEstimate(
            flops=2 * 4096 * 1024 * 1024, bytes_accessed=32 << 20, transcendentals=0
        ),
        name="density",
    )(order, *chunks, table, dmat, weights, xc, home_rows)


def potential_call(table, got, mine, weights, xc, rho, natoms):
    row = jax.ShapeDtypeStruct((PIECES, 1, HALF), jnp.float32)
    return pl.pallas_call(
        potential_body,
        out_shape=(
            jax.ShapeDtypeStruct((natoms, 64), jnp.float32),
            row,
            row,
            jax.ShapeDtypeStruct((1, 128), jnp.float32),
        ),
        in_specs=[any_spec()] + [vmem_spec()] * 5,
        out_specs=(vmem_spec(),) * 4,
        scratch_shapes=[
            pltpu.VMEM((PIECES, NB * BLK, HALF), jnp.float32),
            pltpu.VMEM((2048, 128), jnp.float32),
            pltpu.VMEM((512, 128), jnp.float32),
            pltpu.SemaphoreType.DMA((PIECES,)),
        ],
        compiler_params=pltpu.CompilerParams(vmem_limit_bytes=VMEM_GRANT),
        cost_estimate=pl.CostEstimate(
            flops=16 << 20, bytes_accessed=16 << 20, transcendentals=0
        ),
        name="potential",
    )(table, got, mine, weights, xc, rho)


def ham_call(order, slots, place, chunks, scale_mine, scale_beside):
    return pl.pallas_call(
        ham_body,
        out_shape=(jax.ShapeDtypeStruct((32, 128, BLK), jnp.float32),) * 4,
        in_specs=[smem_spec()] * 3 + [any_spec()] * (2 * CHUNKS) + [vmem_spec()] * 2,
        out_specs=(any_spec(),) * 4,
        scratch_shapes=[
            pltpu.VMEM((128, 128, BLK), jnp.float32),
            pltpu.VMEM((2, 2, 2, NB, 128, 4 * HALF), jnp.bfloat16),
            pltpu.VMEM((2, 2, 1, 4 * HALF), jnp.float32),
            pltpu.SemaphoreType.DMA((4,)),
            pltpu.SemaphoreType.DMA((4,)),
        ],
        compiler_params=pltpu.CompilerParams(vmem_limit_bytes=VMEM_GRANT),
        cost_estimate=pl.CostEstimate(
            flops=4096 * 1024 * 1024, bytes_accessed=24 << 20, transcendentals=0
        ),
        name="ham",
    )(
        order,
        slots,
        place,
        *[c.reshape(NB, 2, 128, c.shape[-1]) for c in chunks],
        scale_mine,
        scale_beside,
    )


def cast(x):
    return x.astype(jnp.float16)


def wide(x):
    return x.astype(jnp.float32)


def ring_sum(parts, factor):
    half = parts[2].shape[0] // 2
    up, down = core_perm(1, False), core_perm(-1, False)
    from_below = lax.ppermute(cast(parts[2][:half] * factor), "grid", up)
    from_above = lax.ppermute(cast(parts[2][half:] * factor), "grid", down)
    below_high = lax.ppermute(cast(parts[1][half:] * factor), "grid", up)
    above_low = lax.ppermute(cast(parts[3][:half] * factor), "grid", down)
    below_low = lax.ppermute(cast(parts[1][:half] * factor + wide(from_below)), "grid", up)
    above_high = lax.ppermute(cast(parts[3][half:] * factor + wide(from_above)), "grid", down)
    low = parts[0][:half] * factor + wide(below_low) + wide(above_low)
    high = parts[0][half:] * factor + wide(below_high) + wide(above_high)
    return [low[0], low[1], high[0], high[1]]


def direct_sum(parts):
    total = parts[0]
    got = [lax.ppermute(cast(parts[d]), "grid", core_perm(d, True)) for d in (2, 1, 3)]
    for g in got:
        total = total + wide(g)
    return total


def one_device(
    basis_values,
    point_coords,
    point_weights,
    xc_kernel,
    gauss_widths,
    atom_coords,
    resp_density,
    tile_list,
    tile_home,
    atom_list,
    atom_home,
):
    groups = lax.axis_size("grid")
    me = lax.axis_index("grid")
    plane = lax.axis_index("pert")
    my_z, my_x, my_c = me // 8, (me // 2) % 4, me % 2
    tile_dev = resp_density.shape[1]
    neighbors = atom_list.shape[1]
    moments = gauss_widths.shape[0]
    natoms = atom_home.shape[0]
    ntiles = tile_home.shape[0]
    slots_here = 2 * neighbors

    own0, own1 = basis_values[:HALF].T, basis_values[HALF:].T
    below0 = lax.ppermute(own0, "pert", ring(1))
    above1 = lax.ppermute(own1, "pert", ring(3))
    below1 = lax.ppermute(own1, "pert", ring(1))
    above0 = lax.ppermute(own0, "pert", ring(3))
    steps = jnp.array([0, 0, 3, 3, 1, 1, 2, 2], jnp.int32)
    halves = jnp.array([0, 1] * 4, jnp.int32)
    order = ((plane + steps) % 4) * 2 + halves

    swap = grid_perm(0, 0, 1)
    first_core = my_c == 0
    top_half, low_half = resp_density[0, :, :128], resp_density[0, :, 128:]
    kept = jnp.where(first_core, top_half, low_half)
    came = lax.ppermute(jnp.where(first_core, low_half, top_half), "grid", swap)
    base = jnp.concatenate(
        [jnp.where(first_core, kept, came), jnp.where(first_core, came, kept)], axis=0
    )
    ring_tiles = [lax.ppermute(base, "grid", core_perm(-d, False)) for d in (1, 2, 3)]

    wanted = tile_list.reshape(-1)
    tile_match = wanted[:, None] == jnp.arange(ntiles, dtype=jnp.int32)[None, :]
    homes = jnp.sum(jnp.where(tile_match, tile_home[None, :], 0), axis=1)
    homes_beside = lax.ppermute(homes, "grid", grid_perm(0, 0, 1))

    every_home = jnp.concatenate([homes, homes_beside])
    owner = every_home // tile_dev
    off_z = (owner // 8 - my_z) % 4
    off_x = ((owner // 2) % 4 - my_x) % 4
    ahead = jnp.where(my_c == 0, off_z * 4 + off_x, off_x * 4 + off_z)
    slots = ahead * (2 * tile_dev) + every_home % (2 * tile_dev)
    core_place = my_c.reshape(1).astype(jnp.int32)

    my_owner = homes // tile_dev
    to_z = (my_owner // 8 - my_z) % 4
    to_x = ((my_owner // 2) % 4 - my_x) % 4
    in_chip = homes % (2 * tile_dev)

    def found(one, two):
        return two * 2 + one // 2, (one % 2) * (2 * tile_dev) + in_chip

    own_first = jnp.where(first_core, to_z, to_x)
    own_second = jnp.where(first_core, to_x, to_z)
    which_own, where_own = found(own_first, own_second)
    which_other, where_other = found(own_second, own_first)
    which = jnp.concatenate([which_own, which_other])
    where = jnp.concatenate([where_own, where_other])

    atom_match = atom_list[:, :, None] == jnp.arange(natoms, dtype=jnp.int32)
    atom_pos = jnp.sum(jnp.where(atom_match[None], atom_coords[:, None, None, :], 0.0), axis=3)
    atom_homes = jnp.sum(jnp.where(atom_match, atom_home, 0), axis=2).reshape(-1)
    delta = point_coords.reshape(3, 2, 4, 1, HALF) - atom_pos[:, :, None, :, None]
    dist_sq = (jnp.sum(delta * delta, axis=0) + SOFTEN).reshape(PIECES, neighbors, 1, HALF)
    spread = (2.0 * gauss_widths * gauss_widths)[None, None, :, None]
    erf_scale = (ROOT_TWO * gauss_widths)[None, None, :, None]
    gauss = jnp.exp(-dist_sq / spread).reshape(PIECES, neighbors * moments, HALF)
    distance = jnp.sqrt(dist_sq)
    hart = (lax.erf(distance / erf_scale) / distance).reshape(
        PIECES, neighbors * moments, HALF
    )
    weights = point_weights.reshape(PIECES, 1, HALF)
    xc = xc_kernel.reshape(PIECES, 1, HALF)

    lane = jnp.arange(128, dtype=jnp.int32)
    here = (lane // 16) == (me % 8)
    home_floats = atom_homes.astype(jnp.float32)
    home_rows = jnp.where(here[None, :], jnp.tile(home_floats.reshape(16, 2).T, (1, 8)), 0.0)
    my_homes = jnp.broadcast_to(home_floats[:, None], (slots_here, 128))

    back, forth = core_perm(-1, True), core_perm(1, True)
    near = jnp.concatenate([base, ring_tiles[0]], axis=0)
    other = jnp.concatenate([ring_tiles[1], ring_tiles[2]], axis=0)
    near_ahead = lax.ppermute(near, "grid", back)
    other_behind = lax.ppermute(other, "grid", forth)
    near_behind = lax.ppermute(near, "grid", forth)
    other_ahead = lax.ppermute(other, "grid", back)
    near_ahead, slots, home_rows, my_homes, which, where = lax.optimization_barrier(
        (near_ahead, slots, home_rows, my_homes, which, where)
    )
    near_far = lax.ppermute(near_ahead, "grid", back)
    other_far = lax.ppermute(other_behind, "grid", forth)
    sources = [
        near, other, near_ahead, other_ahead, near_far, other_far, near_behind, other_behind,
    ]
    sources = sources + [lax.ppermute(s, "grid", swap) for s in sources]

    far0 = lax.ppermute(below0, "pert", ring(1))
    far1 = lax.ppermute(above1, "pert", ring(3))
    chunks = [own0, own1, below0, below1, above0, above1, far0, far1]
    beside = [lax.ppermute(chunk, "grid", swap) for chunk in chunks]

    dmat = assemble_call(core_place, which, where, sources)
    rho, sent = density_call(order, chunks, gauss, dmat, weights, xc, home_rows)
    got = lax.all_to_all(sent, "grid", split_axis=0, concat_axis=0, tiled=True)
    all_coeffs, pot, scale, bound = potential_call(
        hart, got.reshape(groups * PAY_ROWS, 128), my_homes, weights, xc, rho, natoms
    )
    atom_dev = natoms // groups
    own_coeffs = lax.dynamic_slice_in_dim(all_coeffs, me * atom_dev, atom_dev, axis=0)
    ham_bound = PHI_MAX_SQ * 2048 * 0.05 * groups * bound[0, 0] * 1.01 + 1e-20

    scale_beside = lax.ppermute(scale, "grid", swap)
    factor = F16_TOP / ham_bound
    dense = ham_call(
        order,
        slots,
        core_place,
        chunks + beside,
        scale.reshape(2, 1, 4 * HALF),
        scale_beside.reshape(2, 1, 4 * HALF),
    )
    dense = [d.reshape(4, 2 * tile_dev, 128, BLK) for d in dense]
    chip = direct_sum(ring_sum(dense, factor))
    chip = chip.reshape(2, tile_dev, 128, BLK)
    keep = jnp.where(first_core, chip[0], chip[1])
    give = jnp.where(first_core, chip[1], chip[0])
    came = wide(lax.ppermute(cast(give), "grid", swap))
    hamiltonian = jnp.concatenate(
        [jnp.where(first_core, keep, came), jnp.where(first_core, came, keep)], axis=1
    ) * (ham_bound / F16_TOP)
    return (hamiltonian[None], own_coeffs[None], pot.reshape(1, -1))


def solution(mesh):
    placed = (
        P(("grid", "pert"), None),
        P(None, "grid"),
        P("grid"),
        P("grid"),
        P(),
        P(),
        P("pert", "grid", None, None),
        P("grid", None),
        P(),
        P("grid", None),
        P(),
    )
    return jax.shard_map(
        one_device,
        mesh=mesh,
        in_specs=placed,
        out_specs=(P("pert", "grid", None, None), P("pert", "grid", None), P("pert", "grid")),
        check_vma=False,
    )
```

```python
import jax
import jax.numpy as jnp
from jax import lax
from jax.experimental import pallas as pl
from jax.experimental.pallas import tpu as pltpu
from jax.sharding import PartitionSpec as P


SOFTEN = 0.25
ROOT_TWO = 1.4142135623730951
HALF = 512
PIECES = 8
CHUNKS = 8
VMEM_GRANT = 60 << 20
SOURCES = 8
BLK = 256
NB = 4
PHI_MAX_SQ = 36.0
KERNEL_MAX = 2.0
F16_TOP = 32000.0
PAY_ROWS = 24


def ring(shift):
    return [(i, (i + shift) % 4) for i in range(4)]


def grid_perm(dz, dx, dc):
    def at(z, x, c):
        return ((z % 4) * 4 + x % 4) * 2 + c

    return [
        (at(z, x, c), at(z + dz, x + dx, c ^ dc))
        for z in range(4)
        for x in range(4)
        for c in range(2)
    ]


def core_perm(shift, second):
    def at(z, x, c):
        return ((z % 4) * 4 + x % 4) * 2 + c

    pairs = []
    for z in range(4):
        for x in range(4):
            for c in range(2):
                along_z = (c == 0) != second
                there = at(z + shift, x, c) if along_z else at(z, x + shift, c)
                pairs.append((at(z, x, c), there))
    return pairs


def split3(x):
    first = x.astype(jnp.bfloat16)
    rest = x - first.astype(jnp.float32)
    second = rest.astype(jnp.bfloat16)
    third = (rest - second.astype(jnp.float32)).astype(jnp.bfloat16)
    return first, second, third


def fetch_tiles(core, which, where, sources, dmat, sem):
    for side in range(2):
        half = (1 - core) if side else core

        def fetch(n, _, side=side, half=half):
            b, row, col = n // 16, (n // 4) % 4, n % 4
            target = dmat.at[
                b,
                pl.ds(pl.multiple_of(row * BLK + half * 128, 128), 128),
                pl.ds(pl.multiple_of(col * BLK, BLK), BLK),
            ]
            at = side * 32 + n

            def pick(low, high):
                if high - low == 1:
                    pltpu.make_async_copy(
                        sources[side * SOURCES + low].at[where[at]], target, sem
                    ).start()
                    return
                middle = (low + high) // 2
                pl.when(which[at] < middle)(lambda: pick(low, middle))
                pl.when(which[at] >= middle)(lambda: pick(middle, high))

            pick(0, SOURCES)
            return 0

        lax.fori_loop(0, 32, fetch, 0)


def density_steps(order, dmat, sem, table, weights, xc, rho, pacc, bufs, top):
    held, tbuf, psem, tsem = bufs
    pltpu.make_async_copy(dmat, dmat, sem).wait()

    def step(i, top):
        pi = order[i]
        b = pi // 4
        pltpu.make_async_copy(held.at[i], held.at[i], psem.at[i]).wait()
        piece = held[i]
        total = jnp.zeros((1, HALF), jnp.float32)
        for block in range(NB):
            rows = pl.ds(block * BLK, BLK)
            mixed = jnp.dot(dmat[b, rows, :], piece, preferred_element_type=jnp.float32)
            total = total + jnp.sum(
                mixed * held[i, rows, :].astype(jnp.float32), axis=0, keepdims=True
            )
        rho[pi] = total
        weighted = weights[pi] * total
        pltpu.make_async_copy(table.at[pi], tbuf.at[i], tsem.at[i]).wait()
        for block in range(8):
            rows = pl.ds(block * 128, 128)
            part = pacc[b, rows, :]
            for lane in range(HALF // 128):
                cols = slice(lane * 128, (lane + 1) * 128)
                part = part + tbuf[i, rows, cols] * weighted[:, cols]
            pacc[b, rows, :] = part
        return jnp.maximum(top, jnp.abs(xc[pi] * total))

    return lax.fori_loop(0, CHUNKS, step, top)


def density_body(order, place, which, where, *refs):
    chunks = refs[:CHUNKS]
    sources = refs[CHUNKS : CHUNKS + 2 * SOURCES]
    table, weights, xc, home_rows, rho, sent, *rest = refs[CHUNKS + 2 * SOURCES :]
    pacc, dmat, block_out, sem, *bufs = rest
    held, tbuf, psem, tsem = bufs

    def load(i):
        pltpu.make_async_copy(chunks[i], held.at[i], psem.at[i]).start()
        pltpu.make_async_copy(table.at[order[i]], tbuf.at[i], tsem.at[i]).start()

    load(0)
    fetch_tiles(place[0], which, where, sources, dmat, sem)
    for i in range(1, CHUNKS):
        load(i)
    pacc[...] = jnp.zeros_like(pacc)
    block_out[...] = jnp.zeros_like(block_out)
    block_out[pl.ds(17, 2), :] = home_rows[...]
    top = density_steps(
        order, dmat, sem, table, weights, xc, rho, pacc, bufs, jnp.zeros((1, HALF), jnp.float32)
    )
    ones = jnp.ones((8, 128), jnp.bfloat16)
    for b in range(2):
        total = jnp.zeros((8, NB * BLK), jnp.float32)
        for term in split3(pacc[b]):
            total = total + lax.dot_general(
                ones, term, (((1,), (1,)), ((), ())), preferred_element_type=jnp.float32
            )
        for r in range(8):
            block_out[pl.ds(b * 8 + r, 1), :] = total[0:1, r * 128 : (r + 1) * 128]
    block_out[pl.ds(16, 1), :] = jnp.broadcast_to(jnp.max(top, axis=1, keepdims=True), (1, 128))
    for dest in range(32):
        sent[dest] = block_out[...]


def potential_body(table, got, mine, weights, xc, rho, coeffs, pot, scale, bound, *scratch):
    tbuf, column, data, tsem = scratch
    for i in range(PIECES):
        pltpu.make_async_copy(table.at[i], tbuf.at[i], tsem.at[i]).start()
    natoms = coeffs.shape[0]
    homes = []
    for which in range(2):
        segments = []
        for group in range(4):
            row = jnp.zeros((1, 128), jnp.float32)
            for k in range(8):
                row = row + got[pl.ds((group * 8 + k) * PAY_ROWS + 17 + which, 1), :]
            segments.append(row)
        homes.append(jnp.concatenate(segments, axis=1))
    for k in range(32):
        data[pl.ds(k * 16, 16), :] = got[pl.ds(k * PAY_ROWS, 16), :]
    stored = lax.broadcasted_iota(jnp.int32, (natoms, 128), 0).astype(jnp.float32)
    wanted = jnp.concatenate([stored, mine[...]], axis=0)
    wanted = jnp.concatenate([wanted] * 4, axis=1)
    even, odd = [
        jnp.where(wanted == row, 1.0, 0.0).astype(jnp.bfloat16)
        for row in homes
    ]
    first = jnp.zeros((natoms + 32, 128), jnp.float32)
    second = jnp.zeros((natoms + 32, 128), jnp.float32)
    for term in split3(data[...]):
        first = first + jnp.dot(even, term, preferred_element_type=jnp.float32)
        second = second + jnp.dot(odd, term, preferred_element_type=jnp.float32)
    summed = first[:, :64] + second[:, 64:]
    coeffs[...] = summed[:natoms]
    turned = summed[natoms:].T
    for k in range(32):
        column[pl.ds(k * 64, 64), :] = jnp.broadcast_to(turned[:, k : k + 1], (64, 128))
    top = jnp.zeros((1, 128), jnp.float32)
    for k in range(32):
        top = jnp.maximum(top, got[pl.ds(k * PAY_ROWS + 16, 1), :])
    heavy = jnp.max(jnp.sum(jnp.abs(summed[:natoms]), axis=1, keepdims=True), axis=0, keepdims=True)
    bound[...] = top + jnp.broadcast_to(heavy, (1, 128)) * (KERNEL_MAX * 16)

    def step(i, _):
        base = (i // 4) * 1024
        pltpu.make_async_copy(table.at[i], tbuf.at[i], tsem.at[i]).wait()
        parts = [jnp.zeros((8, 128), jnp.float32) for _ in range(HALF // 128)]
        for block in range(16):
            factor = column[pl.ds(base + block * 64, 64), :]
            for lane in range(HALF // 128):
                prod = tbuf[i, block * 64 : (block + 1) * 64, lane * 128 : (lane + 1) * 128]
                parts[lane] = parts[lane] + jnp.sum((prod * factor).reshape(8, 8, 128), axis=0)
        hartree = jnp.concatenate([jnp.sum(p, axis=0, keepdims=True) for p in parts], axis=1)
        potential = hartree + xc[i] * rho[i]
        pot[i] = potential
        scale[i] = weights[i] * potential
        return 0

    lax.fori_loop(0, PIECES, step, 0)


def ham_body(order, slots, place, *refs):
    chunks = refs[: 2 * CHUNKS]
    scale_mine, scale_beside, *rest = refs[2 * CHUNKS :]
    outs, (dense, held, rows_of, psem, osem) = rest[:4], rest[4:]
    core = place[0]
    for side in range(2):
        i = 0
        for ref in chunks[side * CHUNKS : (side + 1) * CHUNKS]:
            width = ref.shape[-1]
            pi = order[i]
            lanes = pl.ds(pl.multiple_of((pi % 4) * HALF, HALF), width)
            for half in range(2):
                at = (1 - core) if half else core
                pltpu.make_async_copy(
                    ref.at[:, half],
                    held.at[side, pi // 4, at, :, :, lanes],
                    psem.at[side * 2 + pi // 4],
                ).start()
            i += width // HALF
    for b in range(2):
        rows_of[0, b] = scale_mine[b]
        rows_of[1, b] = scale_beside[b]

    def clear(s, _):
        dense[s] = jnp.zeros(dense.shape[1:], jnp.float32)
        return 0

    lax.fori_loop(0, dense.shape[0], clear, 0)

    def product(side, b, col):
        left = held[side, b, 0].reshape(2 * BLK, 4 * HALF)
        right = jnp.concatenate([held[side, b, core, col], held[side, b, 1 - core, col]], axis=0)
        right = (right.astype(jnp.float32) * rows_of[side, b]).astype(jnp.bfloat16)
        return lax.dot_general(
            left, right, (((1,), (1,)), ((), ())), preferred_element_type=jnp.float32
        )

    def step(n, _):
        side, b, cols = n // 4, (n // 2) % 2, (n % 2) * 2

        @pl.when(cols == 0)
        def _():
            batch = held.at[side, b]
            pltpu.make_async_copy(batch, batch, psem.at[side * 2 + b]).wait()

        parts = [product(side, b, cols + k) for k in range(2)]
        for k in range(2):
            for row in range(NB):
                slot = slots[side * 32 + b * 16 + row * NB + cols + k]
                dense[slot] += parts[k][row * 128 : (row + 1) * 128]
        return 0

    lax.fori_loop(0, 8, step, 0)
    for d in range(4):
        pltpu.make_async_copy(dense.at[pl.ds(d * 32, 32)], outs[d], osem.at[d]).start()
    for d in range(4):
        pltpu.make_async_copy(dense.at[pl.ds(d * 32, 32)], outs[d], osem.at[d]).wait()


def any_spec():
    return pl.BlockSpec(memory_space=pltpu.HBM)


def vmem_spec():
    return pl.BlockSpec(memory_space=pltpu.VMEM)


def smem_spec():
    return pl.BlockSpec(memory_space=pltpu.SMEM)


def density_call(order, place, which, where, chunks, sources, table, weights, xc, home_rows):
    nbasis = NB * BLK
    return pl.pallas_call(
        density_body,
        out_shape=(
            jax.ShapeDtypeStruct((PIECES, 1, HALF), jnp.float32),
            jax.ShapeDtypeStruct((32, PAY_ROWS, 128), jnp.float32),
        ),
        in_specs=[smem_spec()] * 4
        + [any_spec()] * (CHUNKS + 2 * SOURCES + 1)
        + [vmem_spec()] * 3,
        out_specs=(vmem_spec(),) * 2,
        scratch_shapes=[
            pltpu.VMEM((2, nbasis, 128), jnp.float32),
            pltpu.VMEM((2, nbasis, nbasis), jnp.bfloat16),
            pltpu.VMEM((PAY_ROWS, 128), jnp.float32),
            pltpu.SemaphoreType.DMA,
            pltpu.VMEM((CHUNKS, nbasis, HALF), jnp.bfloat16),
            pltpu.VMEM((CHUNKS, nbasis, HALF), jnp.float32),
            pltpu.SemaphoreType.DMA((CHUNKS,)),
            pltpu.SemaphoreType.DMA((CHUNKS,)),
        ],
        compiler_params=pltpu.CompilerParams(vmem_limit_bytes=VMEM_GRANT),
        cost_estimate=pl.CostEstimate(
            flops=2 * 4096 * 1024 * 1024, bytes_accessed=32 << 20, transcendentals=0
        ),
        name="density",
    )(order, place, which, where, *chunks, *sources, table, weights, xc, home_rows)


def potential_call(table, got, mine, weights, xc, rho, natoms):
    row = jax.ShapeDtypeStruct((PIECES, 1, HALF), jnp.float32)
    return pl.pallas_call(
        potential_body,
        out_shape=(
            jax.ShapeDtypeStruct((natoms, 64), jnp.float32),
            row,
            row,
            jax.ShapeDtypeStruct((1, 128), jnp.float32),
        ),
        in_specs=[any_spec()] + [vmem_spec()] * 5,
        out_specs=(vmem_spec(),) * 4,
        scratch_shapes=[
            pltpu.VMEM((PIECES, NB * BLK, HALF), jnp.float32),
            pltpu.VMEM((2048, 128), jnp.float32),
            pltpu.VMEM((512, 128), jnp.float32),
            pltpu.SemaphoreType.DMA((PIECES,)),
        ],
        compiler_params=pltpu.CompilerParams(vmem_limit_bytes=VMEM_GRANT),
        cost_estimate=pl.CostEstimate(
            flops=16 << 20, bytes_accessed=16 << 20, transcendentals=0
        ),
        name="potential",
    )(table, got, mine, weights, xc, rho)


def ham_call(order, slots, place, chunks, scale_mine, scale_beside):
    return pl.pallas_call(
        ham_body,
        out_shape=(jax.ShapeDtypeStruct((32, 128, BLK), jnp.float32),) * 4,
        in_specs=[smem_spec()] * 3 + [any_spec()] * (2 * CHUNKS) + [vmem_spec()] * 2,
        out_specs=(any_spec(),) * 4,
        scratch_shapes=[
            pltpu.VMEM((128, 128, BLK), jnp.float32),
            pltpu.VMEM((2, 2, 2, NB, 128, 4 * HALF), jnp.bfloat16),
            pltpu.VMEM((2, 2, 1, 4 * HALF), jnp.float32),
            pltpu.SemaphoreType.DMA((4,)),
            pltpu.SemaphoreType.DMA((4,)),
        ],
        compiler_params=pltpu.CompilerParams(vmem_limit_bytes=VMEM_GRANT),
        cost_estimate=pl.CostEstimate(
            flops=4096 * 1024 * 1024, bytes_accessed=24 << 20, transcendentals=0
        ),
        name="ham",
    )(
        order,
        slots,
        place,
        *[c.reshape(NB, 2, 128, c.shape[-1]) for c in chunks],
        scale_mine,
        scale_beside,
    )


def cast(x):
    return x.astype(jnp.float16)


def wide(x):
    return x.astype(jnp.float32)


def ring_sum(parts, factor):
    half = parts[2].shape[0] // 2
    up, down = core_perm(1, False), core_perm(-1, False)
    from_below = lax.ppermute(cast(parts[2][:half] * factor), "grid", up)
    from_above = lax.ppermute(cast(parts[2][half:] * factor), "grid", down)
    below_high = lax.ppermute(cast(parts[1][half:] * factor), "grid", up)
    above_low = lax.ppermute(cast(parts[3][:half] * factor), "grid", down)
    below_low = lax.ppermute(cast(parts[1][:half] * factor + wide(from_below)), "grid", up)
    above_high = lax.ppermute(cast(parts[3][half:] * factor + wide(from_above)), "grid", down)
    low = parts[0][:half] * factor + wide(below_low) + wide(above_low)
    high = parts[0][half:] * factor + wide(below_high) + wide(above_high)
    return [low[0], low[1], high[0], high[1]]


def direct_sum(parts):
    total = parts[0]
    got = [lax.ppermute(cast(parts[d]), "grid", core_perm(d, True)) for d in (2, 1, 3)]
    for g in got:
        total = total + wide(g)
    return total


def one_device(
    basis_values,
    point_coords,
    point_weights,
    xc_kernel,
    gauss_widths,
    atom_coords,
    resp_density,
    tile_list,
    tile_home,
    atom_list,
    atom_home,
):
    groups = lax.axis_size("grid")
    me = lax.axis_index("grid")
    plane = lax.axis_index("pert")
    my_z, my_x, my_c = me // 8, (me // 2) % 4, me % 2
    tile_dev = resp_density.shape[1]
    neighbors = atom_list.shape[1]
    moments = gauss_widths.shape[0]
    natoms = atom_home.shape[0]
    ntiles = tile_home.shape[0]
    slots_here = 2 * neighbors

    own0, own1 = basis_values[:HALF].T, basis_values[HALF:].T
    below0 = lax.ppermute(own0, "pert", ring(1))
    above1 = lax.ppermute(own1, "pert", ring(3))
    below1 = lax.ppermute(own1, "pert", ring(1))
    above0 = lax.ppermute(own0, "pert", ring(3))
    steps = jnp.array([0, 0, 3, 3, 1, 1, 2, 2], jnp.int32)
    halves = jnp.array([0, 1] * 4, jnp.int32)
    order = ((plane + steps) % 4) * 2 + halves

    swap = grid_perm(0, 0, 1)
    first_core = my_c == 0
    top_half, low_half = resp_density[0, :, :128], resp_density[0, :, 128:]
    kept = jnp.where(first_core, top_half, low_half)
    came = lax.ppermute(jnp.where(first_core, low_half, top_half), "grid", swap)
    base = jnp.concatenate(
        [jnp.where(first_core, kept, came), jnp.where(first_core, came, kept)], axis=0
    )
    ring_tiles = [lax.ppermute(base, "grid", core_perm(-d, False)) for d in (1, 2, 3)]

    wanted = tile_list.reshape(-1)
    tile_match = wanted[:, None] == jnp.arange(ntiles, dtype=jnp.int32)[None, :]
    homes = jnp.sum(jnp.where(tile_match, tile_home[None, :], 0), axis=1)
    homes_beside = lax.ppermute(homes, "grid", grid_perm(0, 0, 1))

    every_home = jnp.concatenate([homes, homes_beside])
    owner = every_home // tile_dev
    off_z = (owner // 8 - my_z) % 4
    off_x = ((owner // 2) % 4 - my_x) % 4
    ahead = jnp.where(my_c == 0, off_z * 4 + off_x, off_x * 4 + off_z)
    slots = ahead * (2 * tile_dev) + every_home % (2 * tile_dev)
    core_place = my_c.reshape(1).astype(jnp.int32)

    my_owner = homes // tile_dev
    to_z = (my_owner // 8 - my_z) % 4
    to_x = ((my_owner // 2) % 4 - my_x) % 4
    in_chip = homes % (2 * tile_dev)

    def found(one, two):
        return two * 2 + one // 2, (one % 2) * (2 * tile_dev) + in_chip

    own_first = jnp.where(first_core, to_z, to_x)
    own_second = jnp.where(first_core, to_x, to_z)
    which_own, where_own = found(own_first, own_second)
    which_other, where_other = found(own_second, own_first)
    which = jnp.concatenate([which_own, which_other])
    where = jnp.concatenate([where_own, where_other])

    atom_match = atom_list[:, :, None] == jnp.arange(natoms, dtype=jnp.int32)
    atom_pos = jnp.sum(jnp.where(atom_match[None], atom_coords[:, None, None, :], 0.0), axis=3)
    atom_homes = jnp.sum(jnp.where(atom_match, atom_home, 0), axis=2).reshape(-1)
    delta = point_coords.reshape(3, 2, 4, 1, HALF) - atom_pos[:, :, None, :, None]
    dist_sq = (jnp.sum(delta * delta, axis=0) + SOFTEN).reshape(PIECES, neighbors, 1, HALF)
    spread = (2.0 * gauss_widths * gauss_widths)[None, None, :, None]
    erf_scale = (ROOT_TWO * gauss_widths)[None, None, :, None]
    gauss = jnp.exp(-dist_sq / spread).reshape(PIECES, neighbors * moments, HALF)
    distance = jnp.sqrt(dist_sq)
    weights = point_weights.reshape(PIECES, 1, HALF)
    xc = xc_kernel.reshape(PIECES, 1, HALF)

    lane = jnp.arange(128, dtype=jnp.int32)
    here = (lane // 16) == (me % 8)
    home_floats = atom_homes.astype(jnp.float32)
    home_rows = jnp.where(here[None, :], jnp.tile(home_floats.reshape(16, 2).T, (1, 8)), 0.0)
    my_homes = jnp.broadcast_to(home_floats[:, None], (slots_here, 128))

    back, forth = core_perm(-1, True), core_perm(1, True)
    near = jnp.concatenate([base, ring_tiles[0]], axis=0)
    other = jnp.concatenate([ring_tiles[1], ring_tiles[2]], axis=0)
    near_ahead = lax.ppermute(near, "grid", back)
    other_behind = lax.ppermute(other, "grid", forth)
    near_behind = lax.ppermute(near, "grid", forth)
    other_ahead = lax.ppermute(other, "grid", back)
    near_ahead, slots, home_rows, my_homes, which, where = lax.optimization_barrier(
        (near_ahead, slots, home_rows, my_homes, which, where)
    )
    near_far = lax.ppermute(near_ahead, "grid", back)
    other_far = lax.ppermute(other_behind, "grid", forth)
    sources = [
        near, other, near_ahead, other_ahead, near_far, other_far, near_behind, other_behind,
    ]
    sources = sources + [lax.ppermute(s, "grid", swap) for s in sources]

    far0 = lax.ppermute(below0, "pert", ring(1))
    far1 = lax.ppermute(above1, "pert", ring(3))
    chunks = [own0, own1, below0, below1, above0, above1, far0, far1]

    rho, sent = density_call(
        order, core_place, which, where, chunks, sources, gauss, weights, xc, home_rows
    )
    distance, sent, later = lax.optimization_barrier((distance, sent, chunks))
    beside = [lax.ppermute(chunk, "grid", swap) for chunk in later]
    hart = (lax.erf(distance / erf_scale) / distance).reshape(
        PIECES, neighbors * moments, HALF
    )
    got = lax.all_to_all(sent, "grid", split_axis=0, concat_axis=0, tiled=True)
    all_coeffs, pot, scale, bound = potential_call(
        hart, got.reshape(groups * PAY_ROWS, 128), my_homes, weights, xc, rho, natoms
    )
    atom_dev = natoms // groups
    own_coeffs = lax.dynamic_slice_in_dim(all_coeffs, me * atom_dev, atom_dev, axis=0)
    ham_bound = PHI_MAX_SQ * 2048 * 0.05 * groups * bound[0, 0] * 1.01 + 1e-20

    scale_beside = lax.ppermute(scale, "grid", swap)
    factor = F16_TOP / ham_bound
    dense = ham_call(
        order,
        slots,
        core_place,
        chunks + beside,
        scale.reshape(2, 1, 4 * HALF),
        scale_beside.reshape(2, 1, 4 * HALF),
    )
    dense = [d.reshape(4, 2 * tile_dev, 128, BLK) for d in dense]
    chip = direct_sum(ring_sum(dense, factor))
    chip = chip.reshape(2, tile_dev, 128, BLK)
    keep = jnp.where(first_core, chip[0], chip[1])
    give = jnp.where(first_core, chip[1], chip[0])
    came = wide(lax.ppermute(cast(give), "grid", swap))
    hamiltonian = jnp.concatenate(
        [jnp.where(first_core, keep, came), jnp.where(first_core, came, keep)], axis=1
    ) * (ham_bound / F16_TOP)
    return (hamiltonian[None], own_coeffs[None], pot.reshape(1, -1))


def solution(mesh):
    placed = (
        P(("grid", "pert"), None),
        P(None, "grid"),
        P("grid"),
        P("grid"),
        P(),
        P(),
        P("pert", "grid", None, None),
        P("grid", None),
        P(),
        P("grid", None),
        P(),
    )
    return jax.shard_map(
        one_device,
        mesh=mesh,
        in_specs=placed,
        out_specs=(P("pert", "grid", None, None), P("pert", "grid", None), P("pert", "grid")),
        check_vma=False,
    )
```

```python
import jax
import jax.numpy as jnp
from jax import lax
from jax.experimental import pallas as pl
from jax.experimental.pallas import tpu as pltpu
from jax.sharding import PartitionSpec as P


SOFTEN = 0.25
EARLY_SWAPS = (0, 1, 2, 5)
ROOT_TWO = 1.4142135623730951
HALF = 512
PIECES = 8
CHUNKS = 8
VMEM_GRANT = 60 << 20
SOURCES = 8
BLK = 256
NB = 4
PHI_MAX_SQ = 36.0
KERNEL_MAX = 2.0
F16_TOP = 32000.0
PAY_ROWS = 24


def ring(shift):
    return [(i, (i + shift) % 4) for i in range(4)]


def grid_perm(dz, dx, dc):
    def at(z, x, c):
        return ((z % 4) * 4 + x % 4) * 2 + c

    return [
        (at(z, x, c), at(z + dz, x + dx, c ^ dc))
        for z in range(4)
        for x in range(4)
        for c in range(2)
    ]


def core_perm(shift, second):
    def at(z, x, c):
        return ((z % 4) * 4 + x % 4) * 2 + c

    pairs = []
    for z in range(4):
        for x in range(4):
            for c in range(2):
                along_z = (c == 0) != second
                there = at(z + shift, x, c) if along_z else at(z, x + shift, c)
                pairs.append((at(z, x, c), there))
    return pairs


def split3(x):
    first = x.astype(jnp.bfloat16)
    rest = x - first.astype(jnp.float32)
    second = rest.astype(jnp.bfloat16)
    third = (rest - second.astype(jnp.float32)).astype(jnp.bfloat16)
    return first, second, third


def fetch_tiles(core, which, where, sources, dmat, sem):
    for side in range(2):
        half = (1 - core) if side else core

        def fetch(n, _, side=side, half=half):
            b, row, col = n // 16, (n // 4) % 4, n % 4
            target = dmat.at[
                b,
                pl.ds(pl.multiple_of(row * BLK + half * 128, 128), 128),
                pl.ds(pl.multiple_of(col * BLK, BLK), BLK),
            ]
            at = side * 32 + n

            def pick(low, high):
                if high - low == 1:
                    pltpu.make_async_copy(
                        sources[side * SOURCES + low].at[where[at]], target, sem
                    ).start()
                    return
                middle = (low + high) // 2
                pl.when(which[at] < middle)(lambda: pick(low, middle))
                pl.when(which[at] >= middle)(lambda: pick(middle, high))

            pick(0, SOURCES)
            return 0

        lax.fori_loop(0, 32, fetch, 0)


def density_steps(order, dmat, sem, table, weights, xc, rho, pacc, bufs, top):
    held, tbuf, psem, tsem = bufs
    pltpu.make_async_copy(dmat, dmat, sem).wait()

    def step(i, top):
        pi = order[i]
        b = pi // 4
        pltpu.make_async_copy(held.at[i], held.at[i], psem.at[i]).wait()
        piece = held[i]
        total = jnp.zeros((1, HALF), jnp.float32)
        for block in range(NB):
            rows = pl.ds(block * BLK, BLK)
            mixed = jnp.dot(dmat[b, rows, :], piece, preferred_element_type=jnp.float32)
            total = total + jnp.sum(
                mixed * held[i, rows, :].astype(jnp.float32), axis=0, keepdims=True
            )
        rho[pi] = total
        weighted = weights[pi] * total
        pltpu.make_async_copy(table.at[pi], tbuf.at[i], tsem.at[i]).wait()
        for block in range(8):
            rows = pl.ds(block * 128, 128)
            part = pacc[b, rows, :]
            for lane in range(HALF // 128):
                cols = slice(lane * 128, (lane + 1) * 128)
                part = part + tbuf[i, rows, cols] * weighted[:, cols]
            pacc[b, rows, :] = part
        return jnp.maximum(top, jnp.abs(xc[pi] * total))

    return lax.fori_loop(0, CHUNKS, step, top)


def density_body(order, place, which, where, *refs):
    chunks = refs[:CHUNKS]
    sources = refs[CHUNKS : CHUNKS + 2 * SOURCES]
    table, weights, xc, home_rows, rho, sent, *rest = refs[CHUNKS + 2 * SOURCES :]
    pacc, dmat, block_out, sem, *bufs = rest
    held, tbuf, psem, tsem = bufs

    def load(i):
        pltpu.make_async_copy(chunks[i], held.at[i], psem.at[i]).start()
        pltpu.make_async_copy(table.at[order[i]], tbuf.at[i], tsem.at[i]).start()

    load(0)
    fetch_tiles(place[0], which, where, sources, dmat, sem)
    for i in range(1, CHUNKS):
        load(i)
    pacc[...] = jnp.zeros_like(pacc)
    block_out[...] = jnp.zeros_like(block_out)
    block_out[pl.ds(17, 2), :] = home_rows[...]
    top = density_steps(
        order, dmat, sem, table, weights, xc, rho, pacc, bufs, jnp.zeros((1, HALF), jnp.float32)
    )
    ones = jnp.ones((8, 128), jnp.bfloat16)
    for b in range(2):
        total = jnp.zeros((8, NB * BLK), jnp.float32)
        for term in split3(pacc[b]):
            total = total + lax.dot_general(
                ones, term, (((1,), (1,)), ((), ())), preferred_element_type=jnp.float32
            )
        for r in range(8):
            block_out[pl.ds(b * 8 + r, 1), :] = total[0:1, r * 128 : (r + 1) * 128]
    block_out[pl.ds(16, 1), :] = jnp.broadcast_to(jnp.max(top, axis=1, keepdims=True), (1, 128))
    for dest in range(32):
        sent[dest] = block_out[...]


def potential_body(table, got, mine, weights, xc, rho, coeffs, pot, scale, bound, *scratch):
    tbuf, column, data, tsem = scratch
    for i in range(PIECES):
        pltpu.make_async_copy(table.at[i], tbuf.at[i], tsem.at[i]).start()
    natoms = coeffs.shape[0]
    homes = []
    for which in range(2):
        segments = []
        for group in range(4):
            row = jnp.zeros((1, 128), jnp.float32)
            for k in range(8):
                row = row + got[pl.ds((group * 8 + k) * PAY_ROWS + 17 + which, 1), :]
            segments.append(row)
        homes.append(jnp.concatenate(segments, axis=1))
    for k in range(32):
        data[pl.ds(k * 16, 16), :] = got[pl.ds(k * PAY_ROWS, 16), :]
    stored = lax.broadcasted_iota(jnp.int32, (natoms, 128), 0).astype(jnp.float32)
    wanted = jnp.concatenate([stored, mine[...]], axis=0)
    wanted = jnp.concatenate([wanted] * 4, axis=1)
    even, odd = [
        jnp.where(wanted == row, 1.0, 0.0).astype(jnp.bfloat16)
        for row in homes
    ]
    first = jnp.zeros((natoms + 32, 128), jnp.float32)
    second = jnp.zeros((natoms + 32, 128), jnp.float32)
    for term in split3(data[...]):
        first = first + jnp.dot(even, term, preferred_element_type=jnp.float32)
        second = second + jnp.dot(odd, term, preferred_element_type=jnp.float32)
    summed = first[:, :64] + second[:, 64:]
    coeffs[...] = summed[:natoms]
    turned = summed[natoms:].T
    for k in range(32):
        column[pl.ds(k * 64, 64), :] = jnp.broadcast_to(turned[:, k : k + 1], (64, 128))
    top = jnp.zeros((1, 128), jnp.float32)
    for k in range(32):
        top = jnp.maximum(top, got[pl.ds(k * PAY_ROWS + 16, 1), :])
    heavy = jnp.max(jnp.sum(jnp.abs(summed[:natoms]), axis=1, keepdims=True), axis=0, keepdims=True)
    bound[...] = top + jnp.broadcast_to(heavy, (1, 128)) * (KERNEL_MAX * 16)

    def step(i, _):
        base = (i // 4) * 1024
        pltpu.make_async_copy(table.at[i], tbuf.at[i], tsem.at[i]).wait()
        parts = [jnp.zeros((8, 128), jnp.float32) for _ in range(HALF // 128)]
        for block in range(16):
            factor = column[pl.ds(base + block * 64, 64), :]
            for lane in range(HALF // 128):
                prod = tbuf[i, block * 64 : (block + 1) * 64, lane * 128 : (lane + 1) * 128]
                parts[lane] = parts[lane] + jnp.sum((prod * factor).reshape(8, 8, 128), axis=0)
        hartree = jnp.concatenate([jnp.sum(p, axis=0, keepdims=True) for p in parts], axis=1)
        potential = hartree + xc[i] * rho[i]
        pot[i] = potential
        scale[i] = weights[i] * potential
        return 0

    lax.fori_loop(0, PIECES, step, 0)


def ham_body(order, slots, place, *refs):
    chunks = refs[: 2 * CHUNKS]
    scale_mine, scale_beside, *rest = refs[2 * CHUNKS :]
    outs, (dense, held, rows_of, psem, osem) = rest[:4], rest[4:]
    core = place[0]
    for side in range(2):
        i = 0
        for ref in chunks[side * CHUNKS : (side + 1) * CHUNKS]:
            width = ref.shape[-1]
            pi = order[i]
            lanes = pl.ds(pl.multiple_of((pi % 4) * HALF, HALF), width)
            for half in range(2):
                at = (1 - core) if half else core
                pltpu.make_async_copy(
                    ref.at[:, half],
                    held.at[side, pi // 4, at, :, :, lanes],
                    psem.at[side * 2 + pi // 4],
                ).start()
            i += width // HALF
    for b in range(2):
        rows_of[0, b] = scale_mine[b]
        rows_of[1, b] = scale_beside[b]

    def clear(s, _):
        dense[s] = jnp.zeros(dense.shape[1:], jnp.float32)
        return 0

    lax.fori_loop(0, dense.shape[0], clear, 0)

    def product(side, b, col):
        left = held[side, b, 0].reshape(2 * BLK, 4 * HALF)
        right = jnp.concatenate([held[side, b, core, col], held[side, b, 1 - core, col]], axis=0)
        right = (right.astype(jnp.float32) * rows_of[side, b]).astype(jnp.bfloat16)
        return lax.dot_general(
            left, right, (((1,), (1,)), ((), ())), preferred_element_type=jnp.float32
        )

    def step(n, _):
        side, b, cols = n // 4, (n // 2) % 2, (n % 2) * 2

        @pl.when(cols == 0)
        def _():
            batch = held.at[side, b]
            pltpu.make_async_copy(batch, batch, psem.at[side * 2 + b]).wait()

        parts = [product(side, b, cols + k) for k in range(2)]
        for k in range(2):
            for row in range(NB):
                slot = slots[side * 32 + b * 16 + row * NB + cols + k]
                dense[slot] += parts[k][row * 128 : (row + 1) * 128]
        return 0

    lax.fori_loop(0, 8, step, 0)
    for d in range(4):
        pltpu.make_async_copy(dense.at[pl.ds(d * 32, 32)], outs[d], osem.at[d]).start()
    for d in range(4):
        pltpu.make_async_copy(dense.at[pl.ds(d * 32, 32)], outs[d], osem.at[d]).wait()


def any_spec():
    return pl.BlockSpec(memory_space=pltpu.HBM)


def vmem_spec():
    return pl.BlockSpec(memory_space=pltpu.VMEM)


def smem_spec():
    return pl.BlockSpec(memory_space=pltpu.SMEM)


def density_call(order, place, which, where, chunks, sources, table, weights, xc, home_rows):
    nbasis = NB * BLK
    return pl.pallas_call(
        density_body,
        out_shape=(
            jax.ShapeDtypeStruct((PIECES, 1, HALF), jnp.float32),
            jax.ShapeDtypeStruct((32, PAY_ROWS, 128), jnp.float32),
        ),
        in_specs=[smem_spec()] * 4
        + [any_spec()] * (CHUNKS + 2 * SOURCES + 1)
        + [vmem_spec()] * 3,
        out_specs=(vmem_spec(),) * 2,
        scratch_shapes=[
            pltpu.VMEM((2, nbasis, 128), jnp.float32),
            pltpu.VMEM((2, nbasis, nbasis), jnp.bfloat16),
            pltpu.VMEM((PAY_ROWS, 128), jnp.float32),
            pltpu.SemaphoreType.DMA,
            pltpu.VMEM((CHUNKS, nbasis, HALF), jnp.bfloat16),
            pltpu.VMEM((CHUNKS, nbasis, HALF), jnp.float32),
            pltpu.SemaphoreType.DMA((CHUNKS,)),
            pltpu.SemaphoreType.DMA((CHUNKS,)),
        ],
        compiler_params=pltpu.CompilerParams(vmem_limit_bytes=VMEM_GRANT),
        cost_estimate=pl.CostEstimate(
            flops=2 * 4096 * 1024 * 1024, bytes_accessed=32 << 20, transcendentals=0
        ),
        name="density",
    )(order, place, which, where, *chunks, *sources, table, weights, xc, home_rows)


def potential_call(table, got, mine, weights, xc, rho, natoms):
    row = jax.ShapeDtypeStruct((PIECES, 1, HALF), jnp.float32)
    return pl.pallas_call(
        potential_body,
        out_shape=(
            jax.ShapeDtypeStruct((natoms, 64), jnp.float32),
            row,
            row,
            jax.ShapeDtypeStruct((1, 128), jnp.float32),
        ),
        in_specs=[any_spec()] + [vmem_spec()] * 5,
        out_specs=(vmem_spec(),) * 4,
        scratch_shapes=[
            pltpu.VMEM((PIECES, NB * BLK, HALF), jnp.float32),
            pltpu.VMEM((2048, 128), jnp.float32),
            pltpu.VMEM((512, 128), jnp.float32),
            pltpu.SemaphoreType.DMA((PIECES,)),
        ],
        compiler_params=pltpu.CompilerParams(vmem_limit_bytes=VMEM_GRANT),
        cost_estimate=pl.CostEstimate(
            flops=16 << 20, bytes_accessed=16 << 20, transcendentals=0
        ),
        name="potential",
    )(table, got, mine, weights, xc, rho)


def ham_call(order, slots, place, chunks, scale_mine, scale_beside):
    return pl.pallas_call(
        ham_body,
        out_shape=(jax.ShapeDtypeStruct((32, 128, BLK), jnp.float32),) * 4,
        in_specs=[smem_spec()] * 3 + [any_spec()] * (2 * CHUNKS) + [vmem_spec()] * 2,
        out_specs=(any_spec(),) * 4,
        scratch_shapes=[
            pltpu.VMEM((128, 128, BLK), jnp.float32),
            pltpu.VMEM((2, 2, 2, NB, 128, 4 * HALF), jnp.bfloat16),
            pltpu.VMEM((2, 2, 1, 4 * HALF), jnp.float32),
            pltpu.SemaphoreType.DMA((4,)),
            pltpu.SemaphoreType.DMA((4,)),
        ],
        compiler_params=pltpu.CompilerParams(vmem_limit_bytes=VMEM_GRANT),
        cost_estimate=pl.CostEstimate(
            flops=4096 * 1024 * 1024, bytes_accessed=24 << 20, transcendentals=0
        ),
        name="ham",
    )(
        order,
        slots,
        place,
        *[c.reshape(NB, 2, 128, c.shape[-1]) for c in chunks],
        scale_mine,
        scale_beside,
    )


def cast(x):
    return x.astype(jnp.float16)


def wide(x):
    return x.astype(jnp.float32)


def ring_sum(parts, factor):
    half = parts[2].shape[0] // 2
    up, down = core_perm(1, False), core_perm(-1, False)
    from_below = lax.ppermute(cast(parts[2][:half] * factor), "grid", up)
    from_above = lax.ppermute(cast(parts[2][half:] * factor), "grid", down)
    below_high = lax.ppermute(cast(parts[1][half:] * factor), "grid", up)
    above_low = lax.ppermute(cast(parts[3][:half] * factor), "grid", down)
    below_low = lax.ppermute(cast(parts[1][:half] * factor + wide(from_below)), "grid", up)
    above_high = lax.ppermute(cast(parts[3][half:] * factor + wide(from_above)), "grid", down)
    low = parts[0][:half] * factor + wide(below_low) + wide(above_low)
    high = parts[0][half:] * factor + wide(below_high) + wide(above_high)
    return [low[0], low[1], high[0], high[1]]


def direct_sum(parts):
    total = parts[0]
    got = [lax.ppermute(cast(parts[d]), "grid", core_perm(d, True)) for d in (2, 1, 3)]
    for g in got:
        total = total + wide(g)
    return total


def one_device(
    basis_values,
    point_coords,
    point_weights,
    xc_kernel,
    gauss_widths,
    atom_coords,
    resp_density,
    tile_list,
    tile_home,
    atom_list,
    atom_home,
):
    groups = lax.axis_size("grid")
    me = lax.axis_index("grid")
    plane = lax.axis_index("pert")
    my_z, my_x, my_c = me // 8, (me // 2) % 4, me % 2
    tile_dev = resp_density.shape[1]
    neighbors = atom_list.shape[1]
    moments = gauss_widths.shape[0]
    natoms = atom_home.shape[0]
    ntiles = tile_home.shape[0]
    slots_here = 2 * neighbors

    own0, own1 = basis_values[:HALF].T, basis_values[HALF:].T
    below0 = lax.ppermute(own0, "pert", ring(1))
    above1 = lax.ppermute(own1, "pert", ring(3))
    below1 = lax.ppermute(own1, "pert", ring(1))
    above0 = lax.ppermute(own0, "pert", ring(3))
    steps = jnp.array([0, 0, 3, 3, 1, 1, 2, 2], jnp.int32)
    halves = jnp.array([0, 1] * 4, jnp.int32)
    order = ((plane + steps) % 4) * 2 + halves

    swap = grid_perm(0, 0, 1)
    first_core = my_c == 0
    top_half, low_half = resp_density[0, :, :128], resp_density[0, :, 128:]
    kept = jnp.where(first_core, top_half, low_half)
    came = lax.ppermute(jnp.where(first_core, low_half, top_half), "grid", swap)
    base = jnp.concatenate(
        [jnp.where(first_core, kept, came), jnp.where(first_core, came, kept)], axis=0
    )
    ring_tiles = [lax.ppermute(base, "grid", core_perm(-d, False)) for d in (1, 2, 3)]

    wanted = tile_list.reshape(-1)
    tile_match = wanted[:, None] == jnp.arange(ntiles, dtype=jnp.int32)[None, :]
    homes = jnp.sum(jnp.where(tile_match, tile_home[None, :], 0), axis=1)
    homes_beside = lax.ppermute(homes, "grid", grid_perm(0, 0, 1))

    every_home = jnp.concatenate([homes, homes_beside])
    owner = every_home // tile_dev
    off_z = (owner // 8 - my_z) % 4
    off_x = ((owner // 2) % 4 - my_x) % 4
    ahead = jnp.where(my_c == 0, off_z * 4 + off_x, off_x * 4 + off_z)
    slots = ahead * (2 * tile_dev) + every_home % (2 * tile_dev)
    core_place = my_c.reshape(1).astype(jnp.int32)

    my_owner = homes // tile_dev
    to_z = (my_owner // 8 - my_z) % 4
    to_x = ((my_owner // 2) % 4 - my_x) % 4
    in_chip = homes % (2 * tile_dev)

    def found(one, two):
        return two * 2 + one // 2, (one % 2) * (2 * tile_dev) + in_chip

    own_first = jnp.where(first_core, to_z, to_x)
    own_second = jnp.where(first_core, to_x, to_z)
    which_own, where_own = found(own_first, own_second)
    which_other, where_other = found(own_second, own_first)
    which = jnp.concatenate([which_own, which_other])
    where = jnp.concatenate([where_own, where_other])

    atom_match = atom_list[:, :, None] == jnp.arange(natoms, dtype=jnp.int32)
    atom_pos = jnp.sum(jnp.where(atom_match[None], atom_coords[:, None, None, :], 0.0), axis=3)
    atom_homes = jnp.sum(jnp.where(atom_match, atom_home, 0), axis=2).reshape(-1)
    delta = point_coords.reshape(3, 2, 4, 1, HALF) - atom_pos[:, :, None, :, None]
    dist_sq = (jnp.sum(delta * delta, axis=0) + SOFTEN).reshape(PIECES, neighbors, 1, HALF)
    spread = (2.0 * gauss_widths * gauss_widths)[None, None, :, None]
    erf_scale = (ROOT_TWO * gauss_widths)[None, None, :, None]
    gauss = jnp.exp(-dist_sq / spread).reshape(PIECES, neighbors * moments, HALF)
    distance = jnp.sqrt(dist_sq)
    hart = (lax.erf(distance / erf_scale) / distance).reshape(
        PIECES, neighbors * moments, HALF
    )
    weights = point_weights.reshape(PIECES, 1, HALF)
    xc = xc_kernel.reshape(PIECES, 1, HALF)

    lane = jnp.arange(128, dtype=jnp.int32)
    here = (lane // 16) == (me % 8)
    home_floats = atom_homes.astype(jnp.float32)
    home_rows = jnp.where(here[None, :], jnp.tile(home_floats.reshape(16, 2).T, (1, 8)), 0.0)
    my_homes = jnp.broadcast_to(home_floats[:, None], (slots_here, 128))

    back, forth = core_perm(-1, True), core_perm(1, True)
    near = jnp.concatenate([base, ring_tiles[0]], axis=0)
    other = jnp.concatenate([ring_tiles[1], ring_tiles[2]], axis=0)
    near_ahead = lax.ppermute(near, "grid", back)
    other_behind = lax.ppermute(other, "grid", forth)
    near_behind = lax.ppermute(near, "grid", forth)
    other_ahead = lax.ppermute(other, "grid", back)
    near_ahead, slots, home_rows, my_homes, which, where = lax.optimization_barrier(
        (near_ahead, slots, home_rows, my_homes, which, where)
    )
    near_far = lax.ppermute(near_ahead, "grid", back)
    other_far = lax.ppermute(other_behind, "grid", forth)
    sources = [
        near, other, near_ahead, other_ahead, near_far, other_far, near_behind, other_behind,
    ]
    sources = sources + [lax.ppermute(s, "grid", swap) for s in sources]

    far0 = lax.ppermute(below0, "pert", ring(1))
    far1 = lax.ppermute(above1, "pert", ring(3))
    chunks = [own0, own1, below0, below1, above0, above1, far0, far1]

    rho, sent = density_call(
        order, core_place, which, where, chunks, sources, gauss, weights, xc, home_rows
    )
    sent, later = lax.optimization_barrier((sent, chunks))
    beside = [
        lax.ppermute(chunks[i] if i in EARLY_SWAPS else later[i], "grid", swap)
        for i in range(CHUNKS)
    ]
    got = lax.all_to_all(sent, "grid", split_axis=0, concat_axis=0, tiled=True)
    all_coeffs, pot, scale, bound = potential_call(
        hart, got.reshape(groups * PAY_ROWS, 128), my_homes, weights, xc, rho, natoms
    )
    atom_dev = natoms // groups
    own_coeffs = lax.dynamic_slice_in_dim(all_coeffs, me * atom_dev, atom_dev, axis=0)
    ham_bound = PHI_MAX_SQ * 2048 * 0.05 * groups * bound[0, 0] * 1.01 + 1e-20

    scale_beside = lax.ppermute(scale, "grid", swap)
    factor = F16_TOP / ham_bound
    dense = ham_call(
        order,
        slots,
        core_place,
        chunks + beside,
        scale.reshape(2, 1, 4 * HALF),
        scale_beside.reshape(2, 1, 4 * HALF),
    )
    dense = [d.reshape(4, 2 * tile_dev, 128, BLK) for d in dense]
    chip = direct_sum(ring_sum(dense, factor))
    chip = chip.reshape(2, tile_dev, 128, BLK)
    keep = jnp.where(first_core, chip[0], chip[1])
    give = jnp.where(first_core, chip[1], chip[0])
    came = wide(lax.ppermute(cast(give), "grid", swap))
    hamiltonian = jnp.concatenate(
        [jnp.where(first_core, keep, came), jnp.where(first_core, came, keep)], axis=1
    ) * (ham_bound / F16_TOP)
    return (hamiltonian[None], own_coeffs[None], pot.reshape(1, -1))


def solution(mesh):
    placed = (
        P(("grid", "pert"), None),
        P(None, "grid"),
        P("grid"),
        P("grid"),
        P(),
        P(),
        P("pert", "grid", None, None),
        P("grid", None),
        P(),
        P("grid", None),
        P(),
    )
    return jax.shard_map(
        one_device,
        mesh=mesh,
        in_specs=placed,
        out_specs=(P("pert", "grid", None, None), P("pert", "grid", None), P("pert", "grid")),
        check_vma=False,
    )
```

```python
import jax
import jax.numpy as jnp
from jax import lax
from jax.experimental import pallas as pl
from jax.experimental.pallas import tpu as pltpu
from jax.sharding import PartitionSpec as P


SOFTEN = 0.25
EARLY_SWAPS = (0, 1, 2, 5)
ROOT_TWO = 1.4142135623730951
HALF = 512
PIECES = 8
CHUNKS = 8
VMEM_GRANT = 60 << 20
SOURCES = 8
BLK = 256
NB = 4
PHI_MAX_SQ = 36.0
KERNEL_MAX = 2.0
F16_TOP = 32000.0
PAY_ROWS = 24


def ring(shift):
    return [(i, (i + shift) % 4) for i in range(4)]


def grid_perm(dz, dx, dc):
    def at(z, x, c):
        return ((z % 4) * 4 + x % 4) * 2 + c

    return [
        (at(z, x, c), at(z + dz, x + dx, c ^ dc))
        for z in range(4)
        for x in range(4)
        for c in range(2)
    ]


def core_perm(shift, second):
    def at(z, x, c):
        return ((z % 4) * 4 + x % 4) * 2 + c

    pairs = []
    for z in range(4):
        for x in range(4):
            for c in range(2):
                along_z = (c == 0) != second
                there = at(z + shift, x, c) if along_z else at(z, x + shift, c)
                pairs.append((at(z, x, c), there))
    return pairs


def split3(x):
    first = x.astype(jnp.bfloat16)
    rest = x - first.astype(jnp.float32)
    second = rest.astype(jnp.bfloat16)
    third = (rest - second.astype(jnp.float32)).astype(jnp.bfloat16)
    return first, second, third


def fetch_tiles(core, which, where, sources, dmat, sem):
    for side in range(2):
        half = (1 - core) if side else core

        def fetch(n, _, side=side, half=half):
            b, row, col = n // 16, (n // 4) % 4, n % 4
            target = dmat.at[
                b,
                pl.ds(pl.multiple_of(row * BLK + half * 128, 128), 128),
                pl.ds(pl.multiple_of(col * BLK, BLK), BLK),
            ]
            at = side * 32 + n

            def pick(low, high):
                if high - low == 1:
                    pltpu.make_async_copy(
                        sources[side * SOURCES + low].at[where[at]], target, sem
                    ).start()
                    return
                middle = (low + high) // 2
                pl.when(which[at] < middle)(lambda: pick(low, middle))
                pl.when(which[at] >= middle)(lambda: pick(middle, high))

            pick(0, SOURCES)
            return 0

        lax.fori_loop(0, 32, fetch, 0)


def density_steps(order, dmat, sem, table, weights, xc, rho, pacc, bufs, top):
    held, tbuf, psem, tsem = bufs
    pltpu.make_async_copy(dmat, dmat, sem).wait()

    def step(i, top):
        pi = order[i]
        b = pi // 4
        pltpu.make_async_copy(held.at[i], held.at[i], psem.at[i]).wait()
        piece = held[i]
        total = jnp.zeros((1, HALF), jnp.float32)
        for block in range(NB):
            rows = pl.ds(block * BLK, BLK)
            mixed = jnp.dot(dmat[b, rows, :], piece, preferred_element_type=jnp.float32)
            total = total + jnp.sum(
                mixed * held[i, rows, :].astype(jnp.float32), axis=0, keepdims=True
            )
        rho[pi] = total
        weighted = weights[pi] * total
        pltpu.make_async_copy(table.at[pi], tbuf.at[i], tsem.at[i]).wait()
        for block in range(8):
            rows = pl.ds(block * 128, 128)
            part = pacc[b, rows, :]
            for lane in range(HALF // 128):
                cols = slice(lane * 128, (lane + 1) * 128)
                part = part + tbuf[i, rows, cols] * weighted[:, cols]
            pacc[b, rows, :] = part
        return jnp.maximum(top, jnp.abs(xc[pi] * total))

    return lax.fori_loop(0, CHUNKS, step, top)


def density_body(order, place, which, where, *refs):
    chunks = refs[:CHUNKS]
    sources = refs[CHUNKS : CHUNKS + 2 * SOURCES]
    table, weights, xc, home_rows, rho, sent, *rest = refs[CHUNKS + 2 * SOURCES :]
    pacc, dmat, block_out, sem, *bufs = rest
    held, tbuf, psem, tsem = bufs

    def load(i):
        pltpu.make_async_copy(chunks[i], held.at[i], psem.at[i]).start()
        pltpu.make_async_copy(table.at[order[i]], tbuf.at[i], tsem.at[i]).start()

    load(0)
    fetch_tiles(place[0], which, where, sources, dmat, sem)
    for i in range(1, CHUNKS):
        load(i)
    pacc[...] = jnp.zeros_like(pacc)
    block_out[...] = jnp.zeros_like(block_out)
    block_out[pl.ds(17, 2), :] = home_rows[...]
    top = density_steps(
        order, dmat, sem, table, weights, xc, rho, pacc, bufs, jnp.zeros((1, HALF), jnp.float32)
    )
    ones = jnp.ones((8, 128), jnp.bfloat16)
    for b in range(2):
        total = jnp.zeros((8, NB * BLK), jnp.float32)
        for term in split3(pacc[b]):
            total = total + lax.dot_general(
                ones, term, (((1,), (1,)), ((), ())), preferred_element_type=jnp.float32
            )
        for r in range(8):
            block_out[pl.ds(b * 8 + r, 1), :] = total[0:1, r * 128 : (r + 1) * 128]
    block_out[pl.ds(16, 1), :] = jnp.broadcast_to(jnp.max(top, axis=1, keepdims=True), (1, 128))
    for dest in range(32):
        sent[dest] = block_out[...]


def potential_body(table, got, mine, weights, xc, rho, coeffs, pot, scale, bound, *scratch):
    tbuf, column, data, tsem = scratch
    for i in range(PIECES):
        pltpu.make_async_copy(table.at[i], tbuf.at[i], tsem.at[i]).start()
    natoms = coeffs.shape[0]
    homes = []
    for which in range(2):
        segments = []
        for group in range(4):
            row = jnp.zeros((1, 128), jnp.float32)
            for k in range(8):
                row = row + got[pl.ds((group * 8 + k) * PAY_ROWS + 17 + which, 1), :]
            segments.append(row)
        homes.append(jnp.concatenate(segments, axis=1))
    for k in range(32):
        data[pl.ds(k * 16, 16), :] = got[pl.ds(k * PAY_ROWS, 16), :]
    stored = lax.broadcasted_iota(jnp.int32, (natoms, 128), 0).astype(jnp.float32)
    wanted = jnp.concatenate([stored, mine[...]], axis=0)
    wanted = jnp.concatenate([wanted] * 4, axis=1)
    even, odd = [
        jnp.where(wanted == row, 1.0, 0.0).astype(jnp.bfloat16)
        for row in homes
    ]
    first = jnp.zeros((natoms + 32, 128), jnp.float32)
    second = jnp.zeros((natoms + 32, 128), jnp.float32)
    for term in split3(data[...]):
        first = first + jnp.dot(even, term, preferred_element_type=jnp.float32)
        second = second + jnp.dot(odd, term, preferred_element_type=jnp.float32)
    summed = first[:, :64] + second[:, 64:]
    coeffs[...] = summed[:natoms]
    turned = summed[natoms:].T
    for k in range(32):
        column[pl.ds(k * 64, 64), :] = jnp.broadcast_to(turned[:, k : k + 1], (64, 128))
    top = jnp.zeros((1, 128), jnp.float32)
    for k in range(32):
        top = jnp.maximum(top, got[pl.ds(k * PAY_ROWS + 16, 1), :])
    heavy = jnp.max(jnp.sum(jnp.abs(summed[:natoms]), axis=1, keepdims=True), axis=0, keepdims=True)
    bound[...] = top + jnp.broadcast_to(heavy, (1, 128)) * (KERNEL_MAX * 16)

    def step(i, _):
        base = (i // 4) * 1024
        pltpu.make_async_copy(table.at[i], tbuf.at[i], tsem.at[i]).wait()
        parts = [jnp.zeros((8, 128), jnp.float32) for _ in range(HALF // 128)]
        for block in range(16):
            factor = column[pl.ds(base + block * 64, 64), :]
            for lane in range(HALF // 128):
                prod = tbuf[i, block * 64 : (block + 1) * 64, lane * 128 : (lane + 1) * 128]
                parts[lane] = parts[lane] + jnp.sum((prod * factor).reshape(8, 8, 128), axis=0)
        hartree = jnp.concatenate([jnp.sum(p, axis=0, keepdims=True) for p in parts], axis=1)
        potential = hartree + xc[i] * rho[i]
        pot[i] = potential
        scale[i] = weights[i] * potential
        return 0

    lax.fori_loop(0, PIECES, step, 0)


def ham_body(order, slots, place, *refs):
    chunks = refs[: 2 * CHUNKS]
    scale_mine, scale_beside, *rest = refs[2 * CHUNKS :]
    outs, (dense, held, rows_of, psem, osem) = rest[:8], rest[8:]
    core = place[0]
    for side in range(2):
        i = 0
        for ref in chunks[side * CHUNKS : (side + 1) * CHUNKS]:
            width = ref.shape[-1]
            pi = order[i]
            lanes = pl.ds(pl.multiple_of((pi % 4) * HALF, HALF), width)
            for half in range(2):
                at = (1 - core) if half else core
                pltpu.make_async_copy(
                    ref.at[:, half],
                    held.at[side, pi // 4, at, :, :, lanes],
                    psem.at[side * 2 + pi // 4],
                ).start()
            i += width // HALF
    for b in range(2):
        rows_of[0, b] = scale_mine[b]
        rows_of[1, b] = scale_beside[b]

    def clear(s, _):
        dense[s] = jnp.zeros(dense.shape[1:], jnp.float32)
        return 0

    lax.fori_loop(0, dense.shape[0], clear, 0)

    def product(side, b, col):
        left = held[side, b, 0].reshape(2 * BLK, 4 * HALF)
        right = jnp.concatenate([held[side, b, core, col], held[side, b, 1 - core, col]], axis=0)
        right = (right.astype(jnp.float32) * rows_of[side, b]).astype(jnp.bfloat16)
        return lax.dot_general(
            left, right, (((1,), (1,)), ((), ())), preferred_element_type=jnp.float32
        )

    def step(n, _):
        side, b, cols = n // 4, (n // 2) % 2, (n % 2) * 2

        @pl.when(cols == 0)
        def _():
            batch = held.at[side, b]
            pltpu.make_async_copy(batch, batch, psem.at[side * 2 + b]).wait()

        parts = [product(side, b, cols + k) for k in range(2)]
        for k in range(2):
            for row in range(NB):
                slot = slots[side * 32 + b * 16 + row * NB + cols + k]
                dense[slot] += parts[k][row * 128 : (row + 1) * 128]
        return 0

    lax.fori_loop(0, 8, step, 0)
    for d in range(8):
        pltpu.make_async_copy(dense.at[pl.ds(d * 16, 16)], outs[d], osem.at[d]).start()
    for d in range(8):
        pltpu.make_async_copy(dense.at[pl.ds(d * 16, 16)], outs[d], osem.at[d]).wait()


def any_spec():
    return pl.BlockSpec(memory_space=pltpu.HBM)


def vmem_spec():
    return pl.BlockSpec(memory_space=pltpu.VMEM)


def smem_spec():
    return pl.BlockSpec(memory_space=pltpu.SMEM)


def density_call(order, place, which, where, chunks, sources, table, weights, xc, home_rows):
    nbasis = NB * BLK
    return pl.pallas_call(
        density_body,
        out_shape=(
            jax.ShapeDtypeStruct((PIECES, 1, HALF), jnp.float32),
            jax.ShapeDtypeStruct((32, PAY_ROWS, 128), jnp.float32),
        ),
        in_specs=[smem_spec()] * 4
        + [any_spec()] * (CHUNKS + 2 * SOURCES + 1)
        + [vmem_spec()] * 3,
        out_specs=(vmem_spec(),) * 2,
        scratch_shapes=[
            pltpu.VMEM((2, nbasis, 128), jnp.float32),
            pltpu.VMEM((2, nbasis, nbasis), jnp.bfloat16),
            pltpu.VMEM((PAY_ROWS, 128), jnp.float32),
            pltpu.SemaphoreType.DMA,
            pltpu.VMEM((CHUNKS, nbasis, HALF), jnp.bfloat16),
            pltpu.VMEM((CHUNKS, nbasis, HALF), jnp.float32),
            pltpu.SemaphoreType.DMA((CHUNKS,)),
            pltpu.SemaphoreType.DMA((CHUNKS,)),
        ],
        compiler_params=pltpu.CompilerParams(vmem_limit_bytes=VMEM_GRANT),
        cost_estimate=pl.CostEstimate(
            flops=2 * 4096 * 1024 * 1024, bytes_accessed=32 << 20, transcendentals=0
        ),
        name="density",
    )(order, place, which, where, *chunks, *sources, table, weights, xc, home_rows)


def potential_call(table, got, mine, weights, xc, rho, natoms):
    row = jax.ShapeDtypeStruct((PIECES, 1, HALF), jnp.float32)
    return pl.pallas_call(
        potential_body,
        out_shape=(
            jax.ShapeDtypeStruct((natoms, 64), jnp.float32),
            row,
            row,
            jax.ShapeDtypeStruct((1, 128), jnp.float32),
        ),
        in_specs=[any_spec()] + [vmem_spec()] * 5,
        out_specs=(vmem_spec(),) * 4,
        scratch_shapes=[
            pltpu.VMEM((PIECES, NB * BLK, HALF), jnp.float32),
            pltpu.VMEM((2048, 128), jnp.float32),
            pltpu.VMEM((512, 128), jnp.float32),
            pltpu.SemaphoreType.DMA((PIECES,)),
        ],
        compiler_params=pltpu.CompilerParams(vmem_limit_bytes=VMEM_GRANT),
        cost_estimate=pl.CostEstimate(
            flops=16 << 20, bytes_accessed=16 << 20, transcendentals=0
        ),
        name="potential",
    )(table, got, mine, weights, xc, rho)


def ham_call(order, slots, place, chunks, scale_mine, scale_beside):
    return pl.pallas_call(
        ham_body,
        out_shape=(jax.ShapeDtypeStruct((16, 128, BLK), jnp.float32),) * 8,
        in_specs=[smem_spec()] * 3 + [any_spec()] * (2 * CHUNKS) + [vmem_spec()] * 2,
        out_specs=(any_spec(),) * 8,
        scratch_shapes=[
            pltpu.VMEM((128, 128, BLK), jnp.float32),
            pltpu.VMEM((2, 2, 2, NB, 128, 4 * HALF), jnp.bfloat16),
            pltpu.VMEM((2, 2, 1, 4 * HALF), jnp.float32),
            pltpu.SemaphoreType.DMA((4,)),
            pltpu.SemaphoreType.DMA((8,)),
        ],
        compiler_params=pltpu.CompilerParams(vmem_limit_bytes=VMEM_GRANT),
        cost_estimate=pl.CostEstimate(
            flops=4096 * 1024 * 1024, bytes_accessed=24 << 20, transcendentals=0
        ),
        name="ham",
    )(
        order,
        slots,
        place,
        *[c.reshape(NB, 2, 128, c.shape[-1]) for c in chunks],
        scale_mine,
        scale_beside,
    )


def cast(x):
    return x.astype(jnp.float16)


def wide(x):
    return x.astype(jnp.float32)


def ring_sum(low, high, factor):
    up, down = core_perm(1, False), core_perm(-1, False)
    from_below = lax.ppermute(cast(low[2] * factor), "grid", up)
    from_above = lax.ppermute(cast(high[2] * factor), "grid", down)
    below_high = lax.ppermute(cast(high[1] * factor), "grid", up)
    above_low = lax.ppermute(cast(low[3] * factor), "grid", down)
    below_low = lax.ppermute(cast(low[1] * factor + wide(from_below)), "grid", up)
    above_high = lax.ppermute(cast(high[3] * factor + wide(from_above)), "grid", down)
    low = low[0] * factor + wide(below_low) + wide(above_low)
    high = high[0] * factor + wide(below_high) + wide(above_high)
    return [low[0], low[1], high[0], high[1]]


def direct_sum(parts):
    total = parts[0]
    got = [lax.ppermute(cast(parts[d]), "grid", core_perm(d, True)) for d in (2, 1, 3)]
    for g in got:
        total = total + wide(g)
    return total


def one_device(
    basis_values,
    point_coords,
    point_weights,
    xc_kernel,
    gauss_widths,
    atom_coords,
    resp_density,
    tile_list,
    tile_home,
    atom_list,
    atom_home,
):
    groups = lax.axis_size("grid")
    me = lax.axis_index("grid")
    plane = lax.axis_index("pert")
    my_z, my_x, my_c = me // 8, (me // 2) % 4, me % 2
    tile_dev = resp_density.shape[1]
    neighbors = atom_list.shape[1]
    moments = gauss_widths.shape[0]
    natoms = atom_home.shape[0]
    ntiles = tile_home.shape[0]
    slots_here = 2 * neighbors

    own0, own1 = basis_values[:HALF].T, basis_values[HALF:].T
    below0 = lax.ppermute(own0, "pert", ring(1))
    above1 = lax.ppermute(own1, "pert", ring(3))
    below1 = lax.ppermute(own1, "pert", ring(1))
    above0 = lax.ppermute(own0, "pert", ring(3))
    steps = jnp.array([0, 0, 3, 3, 1, 1, 2, 2], jnp.int32)
    halves = jnp.array([0, 1] * 4, jnp.int32)
    order = ((plane + steps) % 4) * 2 + halves

    swap = grid_perm(0, 0, 1)
    first_core = my_c == 0
    top_half, low_half = resp_density[0, :, :128], resp_density[0, :, 128:]
    kept = jnp.where(first_core, top_half, low_half)
    came = lax.ppermute(jnp.where(first_core, low_half, top_half), "grid", swap)
    base = jnp.concatenate(
        [jnp.where(first_core, kept, came), jnp.where(first_core, came, kept)], axis=0
    )
    ring_tiles = [lax.ppermute(base, "grid", core_perm(-d, False)) for d in (1, 2, 3)]

    wanted = tile_list.reshape(-1)
    tile_match = wanted[:, None] == jnp.arange(ntiles, dtype=jnp.int32)[None, :]
    homes = jnp.sum(jnp.where(tile_match, tile_home[None, :], 0), axis=1)
    homes_beside = lax.ppermute(homes, "grid", grid_perm(0, 0, 1))

    every_home = jnp.concatenate([homes, homes_beside])
    owner = every_home // tile_dev
    off_z = (owner // 8 - my_z) % 4
    off_x = ((owner // 2) % 4 - my_x) % 4
    ahead = jnp.where(my_c == 0, off_z * 4 + off_x, off_x * 4 + off_z)
    slots = ahead * (2 * tile_dev) + every_home % (2 * tile_dev)
    core_place = my_c.reshape(1).astype(jnp.int32)

    my_owner = homes // tile_dev
    to_z = (my_owner // 8 - my_z) % 4
    to_x = ((my_owner // 2) % 4 - my_x) % 4
    in_chip = homes % (2 * tile_dev)

    def found(one, two):
        return two * 2 + one // 2, (one % 2) * (2 * tile_dev) + in_chip

    own_first = jnp.where(first_core, to_z, to_x)
    own_second = jnp.where(first_core, to_x, to_z)
    which_own, where_own = found(own_first, own_second)
    which_other, where_other = found(own_second, own_first)
    which = jnp.concatenate([which_own, which_other])
    where = jnp.concatenate([where_own, where_other])

    atom_match = atom_list[:, :, None] == jnp.arange(natoms, dtype=jnp.int32)
    atom_pos = jnp.sum(jnp.where(atom_match[None], atom_coords[:, None, None, :], 0.0), axis=3)
    atom_homes = jnp.sum(jnp.where(atom_match, atom_home, 0), axis=2).reshape(-1)
    delta = point_coords.reshape(3, 2, 4, 1, HALF) - atom_pos[:, :, None, :, None]
    dist_sq = (jnp.sum(delta * delta, axis=0) + SOFTEN).reshape(PIECES, neighbors, 1, HALF)
    spread = (2.0 * gauss_widths * gauss_widths)[None, None, :, None]
    erf_scale = (ROOT_TWO * gauss_widths)[None, None, :, None]
    gauss = jnp.exp(-dist_sq / spread).reshape(PIECES, neighbors * moments, HALF)
    distance = jnp.sqrt(dist_sq)
    weights = point_weights.reshape(PIECES, 1, HALF)
    xc = xc_kernel.reshape(PIECES, 1, HALF)

    lane = jnp.arange(128, dtype=jnp.int32)
    here = (lane // 16) == (me % 8)
    home_floats = atom_homes.astype(jnp.float32)
    home_rows = jnp.where(here[None, :], jnp.tile(home_floats.reshape(16, 2).T, (1, 8)), 0.0)
    my_homes = jnp.broadcast_to(home_floats[:, None], (slots_here, 128))

    back, forth = core_perm(-1, True), core_perm(1, True)
    first, slots, home_rows, my_homes, which, where = lax.optimization_barrier(
        (ring_tiles[0], slots, home_rows, my_homes, which, where)
    )
    near = jnp.concatenate([base, first], axis=0)
    other = jnp.concatenate([ring_tiles[1], ring_tiles[2]], axis=0)
    near_ahead = lax.ppermute(near, "grid", back)
    other_behind = lax.ppermute(other, "grid", forth)
    near_behind = lax.ppermute(near, "grid", forth)
    other_ahead = lax.ppermute(other, "grid", back)
    near_far = lax.ppermute(near_ahead, "grid", back)
    other_far = lax.ppermute(other_behind, "grid", forth)
    sources = [
        near, other, near_ahead, other_ahead, near_far, other_far, near_behind, other_behind,
    ]
    sources = sources + [lax.ppermute(s, "grid", swap) for s in sources]

    far0 = lax.ppermute(below0, "pert", ring(1))
    far1 = lax.ppermute(above1, "pert", ring(3))
    chunks = [own0, own1, below0, below1, above0, above1, far0, far1]

    rho, sent = density_call(
        order, core_place, which, where, chunks, sources, gauss, weights, xc, home_rows
    )
    distance, sent, later = lax.optimization_barrier((distance, sent, chunks))
    beside = [
        lax.ppermute(chunks[i] if i in EARLY_SWAPS else later[i], "grid", swap)
        for i in range(CHUNKS)
    ]
    hart = (lax.erf(distance / erf_scale) / distance).reshape(
        PIECES, neighbors * moments, HALF
    )
    got = lax.all_to_all(sent, "grid", split_axis=0, concat_axis=0, tiled=True)
    all_coeffs, pot, scale, bound = potential_call(
        hart, got.reshape(groups * PAY_ROWS, 128), my_homes, weights, xc, rho, natoms
    )
    atom_dev = natoms // groups
    own_coeffs = lax.dynamic_slice_in_dim(all_coeffs, me * atom_dev, atom_dev, axis=0)
    ham_bound = PHI_MAX_SQ * 2048 * 0.05 * groups * bound[0, 0] * 1.01 + 1e-20

    scale_beside = lax.ppermute(scale, "grid", swap)
    factor = F16_TOP / ham_bound
    dense = ham_call(
        order,
        slots,
        core_place,
        chunks + beside,
        scale.reshape(2, 1, 4 * HALF),
        scale_beside.reshape(2, 1, 4 * HALF),
    )
    dense = [d.reshape(2, 2 * tile_dev, 128, BLK) for d in dense]
    chip = direct_sum(ring_sum(dense[0::2], dense[1::2], factor))
    chip = chip.reshape(2, tile_dev, 128, BLK)
    keep = jnp.where(first_core, chip[0], chip[1])
    give = jnp.where(first_core, chip[1], chip[0])
    came = wide(lax.ppermute(cast(give), "grid", swap))
    hamiltonian = jnp.concatenate(
        [jnp.where(first_core, keep, came), jnp.where(first_core, came, keep)], axis=1
    ) * (ham_bound / F16_TOP)
    return (hamiltonian[None], own_coeffs[None], pot.reshape(1, -1))


def solution(mesh):
    placed = (
        P(("grid", "pert"), None),
        P(None, "grid"),
        P("grid"),
        P("grid"),
        P(),
        P(),
        P("pert", "grid", None, None),
        P("grid", None),
        P(),
        P("grid", None),
        P(),
    )
    return jax.shard_map(
        one_device,
        mesh=mesh,
        in_specs=placed,
        out_specs=(P("pert", "grid", None, None), P("pert", "grid", None), P("pert", "grid")),
        check_vma=False,
    )
```

```python
import jax
import jax.numpy as jnp
from jax import lax
from jax.experimental import pallas as pl
from jax.experimental.pallas import tpu as pltpu
from jax.sharding import PartitionSpec as P


SOFTEN = 0.25
EARLY_SWAPS = (0, 1, 2, 3, 4, 5)
ROOT_TWO = 1.4142135623730951
HALF = 512
PIECES = 8
CHUNKS = 8
VMEM_GRANT = 60 << 20
SOURCES = 8
BLK = 256
NB = 4
PHI_MAX_SQ = 36.0
KERNEL_MAX = 2.0
F16_TOP = 32000.0
PAY_ROWS = 24


def ring(shift):
    return [(i, (i + shift) % 4) for i in range(4)]


def grid_perm(dz, dx, dc):
    def at(z, x, c):
        return ((z % 4) * 4 + x % 4) * 2 + c

    return [
        (at(z, x, c), at(z + dz, x + dx, c ^ dc))
        for z in range(4)
        for x in range(4)
        for c in range(2)
    ]


def core_perm(shift, second):
    def at(z, x, c):
        return ((z % 4) * 4 + x % 4) * 2 + c

    pairs = []
    for z in range(4):
        for x in range(4):
            for c in range(2):
                along_z = (c == 0) != second
                there = at(z + shift, x, c) if along_z else at(z, x + shift, c)
                pairs.append((at(z, x, c), there))
    return pairs


def split3(x):
    first = x.astype(jnp.bfloat16)
    rest = x - first.astype(jnp.float32)
    second = rest.astype(jnp.bfloat16)
    third = (rest - second.astype(jnp.float32)).astype(jnp.bfloat16)
    return first, second, third


def fetch_tiles(core, which, where, sources, dmat, sem):
    for side in range(2):
        half = (1 - core) if side else core

        def fetch(n, _, side=side, half=half):
            b, row, col = n // 16, (n // 4) % 4, n % 4
            target = dmat.at[
                b,
                pl.ds(pl.multiple_of(row * BLK + half * 128, 128), 128),
                pl.ds(pl.multiple_of(col * BLK, BLK), BLK),
            ]
            kind, block = which[side * 32 + n], where[side * 32 + n]

            def pick(low, high):
                if high - low == 1:
                    pltpu.make_async_copy(
                        sources[side * SOURCES + low].at[block], target, sem
                    ).start()
                    return
                middle = (low + high) // 2
                pl.when(kind < middle)(lambda: pick(low, middle))
                pl.when(kind >= middle)(lambda: pick(middle, high))

            pick(0, SOURCES)
            return 0

        lax.fori_loop(0, 32, fetch, 0)


def density_steps(order, dmat, sem, table, weights, xc, rho, pacc, bufs, top):
    held, tbuf, psem, tsem = bufs
    pltpu.make_async_copy(dmat, dmat, sem).wait()

    def step(i, top):
        pi = order[i]
        b = pi // 4
        pltpu.make_async_copy(held.at[i], held.at[i], psem.at[i]).wait()
        piece = held[i]
        total = jnp.zeros((1, HALF), jnp.float32)
        for block in range(NB):
            rows = pl.ds(block * BLK, BLK)
            mixed = jnp.dot(dmat[b, rows, :], piece, preferred_element_type=jnp.float32)
            total = total + jnp.sum(
                mixed * held[i, rows, :].astype(jnp.float32), axis=0, keepdims=True
            )
        rho[pi] = total
        weighted = weights[pi] * total
        pltpu.make_async_copy(table.at[pi], tbuf.at[i], tsem.at[i]).wait()
        for block in range(8):
            rows = pl.ds(block * 128, 128)
            part = pacc[b, rows, :]
            for lane in range(HALF // 128):
                cols = slice(lane * 128, (lane + 1) * 128)
                part = part + tbuf[i, rows, cols] * weighted[:, cols]
            pacc[b, rows, :] = part
        return jnp.maximum(top, jnp.abs(xc[pi] * total))

    return lax.fori_loop(0, CHUNKS, step, top)


def density_body(order, place, which, where, *refs):
    chunks = refs[:CHUNKS]
    sources = refs[CHUNKS : CHUNKS + 2 * SOURCES]
    table, weights, xc, home_rows, rho, sent, *rest = refs[CHUNKS + 2 * SOURCES :]
    pacc, dmat, block_out, sem, *bufs = rest
    held, tbuf, psem, tsem = bufs

    def load(i):
        pltpu.make_async_copy(chunks[i], held.at[i], psem.at[i]).start()
        pltpu.make_async_copy(table.at[order[i]], tbuf.at[i], tsem.at[i]).start()

    load(0)
    fetch_tiles(place[0], which, where, sources, dmat, sem)
    for i in range(1, CHUNKS):
        load(i)
    pacc[...] = jnp.zeros_like(pacc)
    block_out[...] = jnp.zeros_like(block_out)
    block_out[pl.ds(17, 2), :] = home_rows[...]
    top = density_steps(
        order, dmat, sem, table, weights, xc, rho, pacc, bufs, jnp.zeros((1, HALF), jnp.float32)
    )
    ones = jnp.ones((8, 128), jnp.bfloat16)
    for b in range(2):
        total = jnp.zeros((8, NB * BLK), jnp.float32)
        for term in split3(pacc[b]):
            total = total + lax.dot_general(
                ones, term, (((1,), (1,)), ((), ())), preferred_element_type=jnp.float32
            )
        for r in range(8):
            block_out[pl.ds(b * 8 + r, 1), :] = total[0:1, r * 128 : (r + 1) * 128]
    block_out[pl.ds(16, 1), :] = jnp.broadcast_to(jnp.max(top, axis=1, keepdims=True), (1, 128))
    for dest in range(32):
        sent[dest] = block_out[...]


def potential_body(table0, table1, got, mine, weights, xc, rho, coeffs, pot, scale, bound, *scratch):
    tbuf, column, data, tsem = scratch
    for i in range(PIECES):
        table = table0 if i < PIECES // 2 else table1
        pltpu.make_async_copy(table.at[i % (PIECES // 2)], tbuf.at[i], tsem.at[i]).start()
    natoms = coeffs.shape[0]
    homes = []
    for which in range(2):
        segments = []
        for group in range(4):
            row = jnp.zeros((1, 128), jnp.float32)
            for k in range(8):
                row = row + got[pl.ds((group * 8 + k) * PAY_ROWS + 17 + which, 1), :]
            segments.append(row)
        homes.append(jnp.concatenate(segments, axis=1))
    for k in range(32):
        data[pl.ds(k * 16, 16), :] = got[pl.ds(k * PAY_ROWS, 16), :]
    stored = lax.broadcasted_iota(jnp.int32, (natoms, 128), 0).astype(jnp.float32)
    wanted = jnp.concatenate([stored, mine[...]], axis=0)
    wanted = jnp.concatenate([wanted] * 4, axis=1)
    even, odd = [
        jnp.where(wanted == row, 1.0, 0.0).astype(jnp.bfloat16)
        for row in homes
    ]
    first = jnp.zeros((natoms + 32, 128), jnp.float32)
    second = jnp.zeros((natoms + 32, 128), jnp.float32)
    for term in split3(data[...]):
        first = first + jnp.dot(even, term, preferred_element_type=jnp.float32)
        second = second + jnp.dot(odd, term, preferred_element_type=jnp.float32)
    summed = first[:, :64] + second[:, 64:]
    coeffs[...] = summed[:natoms]
    turned = summed[natoms:].T
    for k in range(32):
        column[pl.ds(k * 64, 64), :] = jnp.broadcast_to(turned[:, k : k + 1], (64, 128))
    top = jnp.zeros((1, 128), jnp.float32)
    for k in range(32):
        top = jnp.maximum(top, got[pl.ds(k * PAY_ROWS + 16, 1), :])
    heavy = jnp.max(jnp.sum(jnp.abs(summed[:natoms]), axis=1, keepdims=True), axis=0, keepdims=True)
    bound[...] = top + jnp.broadcast_to(heavy, (1, 128)) * (KERNEL_MAX * 16)

    def step(i, _):
        base = (i // 4) * 1024
        pltpu.make_async_copy(tbuf.at[i], tbuf.at[i], tsem.at[i]).wait()
        parts = [jnp.zeros((8, 128), jnp.float32) for _ in range(HALF // 128)]
        for block in range(16):
            factor = column[pl.ds(base + block * 64, 64), :]
            for lane in range(HALF // 128):
                prod = tbuf[i, block * 64 : (block + 1) * 64, lane * 128 : (lane + 1) * 128]
                parts[lane] = parts[lane] + jnp.sum((prod * factor).reshape(8, 8, 128), axis=0)
        hartree = jnp.concatenate([jnp.sum(p, axis=0, keepdims=True) for p in parts], axis=1)
        potential = hartree + xc[i] * rho[i]
        pot[i] = potential
        scale[i] = weights[i] * potential
        return 0

    lax.fori_loop(0, PIECES, step, 0)


def ham_body(order, slots, place, *refs):
    chunks = refs[: 2 * CHUNKS]
    scale_mine, scale_beside, *rest = refs[2 * CHUNKS :]
    outs, (dense, held, rows_of, psem, osem) = rest[:8], rest[8:]
    core = place[0]
    for side in range(2):
        i = 0
        for ref in chunks[side * CHUNKS : (side + 1) * CHUNKS]:
            width = ref.shape[-1]
            pi = order[i]
            lanes = pl.ds(pl.multiple_of((pi % 4) * HALF, HALF), width)
            for half in range(2):
                at = (1 - core) if half else core
                pltpu.make_async_copy(
                    ref.at[:, half],
                    held.at[side, pi // 4, at, :, :, lanes],
                    psem.at[side * 2 + pi // 4],
                ).start()
            i += width // HALF
    for b in range(2):
        rows_of[0, b] = scale_mine[b]
        rows_of[1, b] = scale_beside[b]

    def clear(s, _):
        dense[s] = jnp.zeros(dense.shape[1:], jnp.float32)
        return 0

    lax.fori_loop(0, dense.shape[0], clear, 0)

    def product(side, b, col):
        left = held[side, b, 0].reshape(2 * BLK, 4 * HALF)
        right = jnp.concatenate([held[side, b, core, col], held[side, b, 1 - core, col]], axis=0)
        right = (right.astype(jnp.float32) * rows_of[side, b]).astype(jnp.bfloat16)
        return lax.dot_general(
            left, right, (((1,), (1,)), ((), ())), preferred_element_type=jnp.float32
        )

    def step(n, _):
        side, b, cols = n // 4, (n // 2) % 2, (n % 2) * 2

        @pl.when(cols == 0)
        def _():
            batch = held.at[side, b]
            pltpu.make_async_copy(batch, batch, psem.at[side * 2 + b]).wait()

        parts = [product(side, b, cols + k) for k in range(2)]
        for k in range(2):
            for row in range(NB):
                slot = slots[side * 32 + b * 16 + row * NB + cols + k]
                dense[slot] += parts[k][row * 128 : (row + 1) * 128]
        return 0

    lax.fori_loop(0, 8, step, 0)
    for d in range(8):
        pltpu.make_async_copy(dense.at[pl.ds(d * 16, 16)], outs[d], osem.at[d]).start()
    for d in range(8):
        pltpu.make_async_copy(dense.at[pl.ds(d * 16, 16)], outs[d], osem.at[d]).wait()


def any_spec():
    return pl.BlockSpec(memory_space=pltpu.HBM)


def vmem_spec():
    return pl.BlockSpec(memory_space=pltpu.VMEM)


def smem_spec():
    return pl.BlockSpec(memory_space=pltpu.SMEM)


def density_call(order, place, which, where, chunks, sources, table, weights, xc, home_rows):
    nbasis = NB * BLK
    return pl.pallas_call(
        density_body,
        out_shape=(
            jax.ShapeDtypeStruct((PIECES, 1, HALF), jnp.float32),
            jax.ShapeDtypeStruct((32, PAY_ROWS, 128), jnp.float32),
        ),
        in_specs=[smem_spec()] * 4
        + [any_spec()] * (CHUNKS + 2 * SOURCES + 1)
        + [vmem_spec()] * 3,
        out_specs=(vmem_spec(),) * 2,
        scratch_shapes=[
            pltpu.VMEM((2, nbasis, 128), jnp.float32),
            pltpu.VMEM((2, nbasis, nbasis), jnp.bfloat16),
            pltpu.VMEM((PAY_ROWS, 128), jnp.float32),
            pltpu.SemaphoreType.DMA,
            pltpu.VMEM((CHUNKS, nbasis, HALF), jnp.bfloat16),
            pltpu.VMEM((CHUNKS, nbasis, HALF), jnp.float32),
            pltpu.SemaphoreType.DMA((CHUNKS,)),
            pltpu.SemaphoreType.DMA((CHUNKS,)),
        ],
        compiler_params=pltpu.CompilerParams(vmem_limit_bytes=VMEM_GRANT),
        cost_estimate=pl.CostEstimate(
            flops=2 * 4096 * 1024 * 1024, bytes_accessed=32 << 20, transcendentals=0
        ),
        name="density",
    )(order, place, which, where, *chunks, *sources, table, weights, xc, home_rows)


def potential_call(tables, got, mine, weights, xc, rho, natoms):
    row = jax.ShapeDtypeStruct((PIECES, 1, HALF), jnp.float32)
    return pl.pallas_call(
        potential_body,
        out_shape=(
            jax.ShapeDtypeStruct((natoms, 64), jnp.float32),
            row,
            row,
            jax.ShapeDtypeStruct((1, 128), jnp.float32),
        ),
        in_specs=[any_spec()] * 2 + [vmem_spec()] * 5,
        out_specs=(vmem_spec(),) * 4,
        scratch_shapes=[
            pltpu.VMEM((PIECES, NB * BLK, HALF), jnp.float32),
            pltpu.VMEM((2048, 128), jnp.float32),
            pltpu.VMEM((512, 128), jnp.float32),
            pltpu.SemaphoreType.DMA((PIECES,)),
        ],
        compiler_params=pltpu.CompilerParams(vmem_limit_bytes=VMEM_GRANT),
        cost_estimate=pl.CostEstimate(
            flops=16 << 20, bytes_accessed=16 << 20, transcendentals=0
        ),
        name="potential",
    )(*tables, got, mine, weights, xc, rho)


def ham_call(order, slots, place, chunks, scale_mine, scale_beside):
    return pl.pallas_call(
        ham_body,
        out_shape=(jax.ShapeDtypeStruct((16, 128, BLK), jnp.float32),) * 8,
        in_specs=[smem_spec()] * 3 + [any_spec()] * (2 * CHUNKS) + [vmem_spec()] * 2,
        out_specs=(any_spec(),) * 8,
        scratch_shapes=[
            pltpu.VMEM((128, 128, BLK), jnp.float32),
            pltpu.VMEM((2, 2, 2, NB, 128, 4 * HALF), jnp.bfloat16),
            pltpu.VMEM((2, 2, 1, 4 * HALF), jnp.float32),
            pltpu.SemaphoreType.DMA((4,)),
            pltpu.SemaphoreType.DMA((8,)),
        ],
        compiler_params=pltpu.CompilerParams(vmem_limit_bytes=VMEM_GRANT),
        cost_estimate=pl.CostEstimate(
            flops=4096 * 1024 * 1024, bytes_accessed=24 << 20, transcendentals=0
        ),
        name="ham",
    )(
        order,
        slots,
        place,
        *[c.reshape(NB, 2, 128, c.shape[-1]) for c in chunks],
        scale_mine,
        scale_beside,
    )


def cast(x):
    return x.astype(jnp.float16)


def wide(x):
    return x.astype(jnp.float32)


def ring_sum(low, high, factor):
    up, down = core_perm(1, False), core_perm(-1, False)
    from_below = lax.ppermute(cast(low[2] * factor), "grid", up)
    from_above = lax.ppermute(cast(high[2] * factor), "grid", down)
    below_high = lax.ppermute(cast(high[1] * factor), "grid", up)
    above_low = lax.ppermute(cast(low[3] * factor), "grid", down)
    below_low = lax.ppermute(cast(low[1] * factor + wide(from_below)), "grid", up)
    above_high = lax.ppermute(cast(high[3] * factor + wide(from_above)), "grid", down)
    low = low[0] * factor + wide(below_low) + wide(above_low)
    high = high[0] * factor + wide(below_high) + wide(above_high)
    return [low[0], low[1], high[0], high[1]]


def direct_sum(parts):
    total = parts[0]
    got = [lax.ppermute(cast(parts[d]), "grid", core_perm(d, True)) for d in (2, 1, 3)]
    for g in got:
        total = total + wide(g)
    return total


def one_device(
    basis_values,
    point_coords,
    point_weights,
    xc_kernel,
    gauss_widths,
    atom_coords,
    resp_density,
    tile_list,
    tile_home,
    atom_list,
    atom_home,
):
    groups = lax.axis_size("grid")
    me = lax.axis_index("grid")
    plane = lax.axis_index("pert")
    my_z, my_x, my_c = me // 8, (me // 2) % 4, me % 2
    tile_dev = resp_density.shape[1]
    neighbors = atom_list.shape[1]
    moments = gauss_widths.shape[0]
    natoms = atom_home.shape[0]
    ntiles = tile_home.shape[0]
    slots_here = 2 * neighbors

    own0, own1 = basis_values[:HALF].T, basis_values[HALF:].T
    below0 = lax.ppermute(own0, "pert", ring(1))
    above1 = lax.ppermute(own1, "pert", ring(3))
    below1 = lax.ppermute(own1, "pert", ring(1))
    above0 = lax.ppermute(own0, "pert", ring(3))
    steps = jnp.array([0, 0, 3, 3, 1, 1, 2, 2], jnp.int32)
    halves = jnp.array([0, 1] * 4, jnp.int32)
    order = ((plane + steps) % 4) * 2 + halves

    swap = grid_perm(0, 0, 1)
    first_core = my_c == 0
    top_half, low_half = resp_density[0, :, :128], resp_density[0, :, 128:]
    kept = jnp.where(first_core, top_half, low_half)
    came = lax.ppermute(jnp.where(first_core, low_half, top_half), "grid", swap)
    base = jnp.concatenate(
        [jnp.where(first_core, kept, came), jnp.where(first_core, came, kept)], axis=0
    )
    ring_tiles = [lax.ppermute(base, "grid", core_perm(-d, False)) for d in (1, 2, 3)]

    wanted = tile_list.reshape(-1)
    tile_match = wanted[:, None] == jnp.arange(ntiles, dtype=jnp.int32)[None, :]
    homes = jnp.sum(jnp.where(tile_match, tile_home[None, :], 0), axis=1)
    homes_beside = lax.ppermute(homes, "grid", grid_perm(0, 0, 1))

    every_home = jnp.concatenate([homes, homes_beside])
    owner = every_home // tile_dev
    off_z = (owner // 8 - my_z) % 4
    off_x = ((owner // 2) % 4 - my_x) % 4
    ahead = jnp.where(my_c == 0, off_z * 4 + off_x, off_x * 4 + off_z)
    slots = ahead * (2 * tile_dev) + every_home % (2 * tile_dev)
    core_place = my_c.reshape(1).astype(jnp.int32)

    my_owner = homes // tile_dev
    to_z = (my_owner // 8 - my_z) % 4
    to_x = ((my_owner // 2) % 4 - my_x) % 4
    in_chip = homes % (2 * tile_dev)

    def found(one, two):
        return two * 2 + one // 2, (one % 2) * (2 * tile_dev) + in_chip

    own_first = jnp.where(first_core, to_z, to_x)
    own_second = jnp.where(first_core, to_x, to_z)
    which_own, where_own = found(own_first, own_second)
    which_other, where_other = found(own_second, own_first)
    which = jnp.concatenate([which_own, which_other])
    where = jnp.concatenate([where_own, where_other])

    atom_match = atom_list[:, :, None] == jnp.arange(natoms, dtype=jnp.int32)
    atom_pos = jnp.sum(jnp.where(atom_match[None], atom_coords[:, None, None, :], 0.0), axis=3)
    atom_homes = jnp.sum(jnp.where(atom_match, atom_home, 0), axis=2).reshape(-1)
    delta = point_coords.reshape(3, 2, 4, 1, HALF) - atom_pos[:, :, None, :, None]
    dist_sq = (jnp.sum(delta * delta, axis=0) + SOFTEN).reshape(PIECES, neighbors, 1, HALF)
    spread = (2.0 * gauss_widths * gauss_widths)[None, None, :, None]
    erf_scale = (ROOT_TWO * gauss_widths)[None, None, :, None]
    gauss = jnp.exp(-dist_sq / spread).reshape(PIECES, neighbors * moments, HALF)
    distance = jnp.sqrt(dist_sq)

    def erf_table(part):
        return (lax.erf(part / erf_scale) / part).reshape(
            PIECES // 2, neighbors * moments, HALF
        )

    hart_first = erf_table(distance[: PIECES // 2])
    weights = point_weights.reshape(PIECES, 1, HALF)
    xc = xc_kernel.reshape(PIECES, 1, HALF)

    lane = jnp.arange(128, dtype=jnp.int32)
    here = (lane // 16) == (me % 8)
    home_floats = atom_homes.astype(jnp.float32)
    home_rows = jnp.where(here[None, :], jnp.tile(home_floats.reshape(16, 2).T, (1, 8)), 0.0)
    my_homes = jnp.broadcast_to(home_floats[:, None], (slots_here, 128))

    back, forth = core_perm(-1, True), core_perm(1, True)
    first, slots, home_rows, my_homes, which, where = lax.optimization_barrier(
        (ring_tiles[0], slots, home_rows, my_homes, which, where)
    )
    near = jnp.concatenate([base, first], axis=0)
    other = jnp.concatenate([ring_tiles[1], ring_tiles[2]], axis=0)
    near_ahead = lax.ppermute(near, "grid", back)
    other_behind = lax.ppermute(other, "grid", forth)
    near_behind = lax.ppermute(near, "grid", forth)
    other_ahead = lax.ppermute(other, "grid", back)
    near_far = lax.ppermute(near_ahead, "grid", back)
    other_far = lax.ppermute(other_behind, "grid", forth)
    sources = [
        near, other, near_ahead, other_ahead, near_far, other_far, near_behind, other_behind,
    ]
    sources = sources + [lax.ppermute(s, "grid", swap) for s in sources]

    far0 = lax.ppermute(below0, "pert", ring(1))
    far1 = lax.ppermute(above1, "pert", ring(3))
    chunks = [own0, own1, below0, below1, above0, above1, far0, far1]

    gauss, hart_first = lax.optimization_barrier((gauss, hart_first))
    rho, sent = density_call(
        order, core_place, which, where, chunks, sources, gauss, weights, xc, home_rows
    )
    second, sent, later = lax.optimization_barrier((distance[PIECES // 2 :], sent, chunks))
    beside = [
        lax.ppermute(chunks[i] if i in EARLY_SWAPS else later[i], "grid", swap)
        for i in range(CHUNKS)
    ]
    hart = (hart_first, erf_table(second))
    got = lax.all_to_all(sent, "grid", split_axis=0, concat_axis=0, tiled=True)
    all_coeffs, pot, scale, bound = potential_call(
        hart, got.reshape(groups * PAY_ROWS, 128), my_homes, weights, xc, rho, natoms
    )
    atom_dev = natoms // groups
    own_coeffs = lax.dynamic_slice_in_dim(all_coeffs, me * atom_dev, atom_dev, axis=0)
    ham_bound = PHI_MAX_SQ * 2048 * 0.05 * groups * bound[0, 0] * 1.01 + 1e-20

    scale_beside = lax.ppermute(scale, "grid", swap)
    factor = F16_TOP / ham_bound
    dense = ham_call(
        order,
        slots,
        core_place,
        chunks + beside,
        scale.reshape(2, 1, 4 * HALF),
        scale_beside.reshape(2, 1, 4 * HALF),
    )
    dense = [d.reshape(2, 2 * tile_dev, 128, BLK) for d in dense]
    chip = direct_sum(ring_sum(dense[0::2], dense[1::2], factor))
    chip = chip.reshape(2, tile_dev, 128, BLK)
    keep = jnp.where(first_core, chip[0], chip[1])
    give = jnp.where(first_core, chip[1], chip[0])
    came = wide(lax.ppermute(cast(give), "grid", swap))
    hamiltonian = jnp.concatenate(
        [jnp.where(first_core, keep, came), jnp.where(first_core, came, keep)], axis=1
    ) * (ham_bound / F16_TOP)
    return (hamiltonian[None], own_coeffs[None], pot.reshape(1, -1))


def solution(mesh):
    placed = (
        P(("grid", "pert"), None),
        P(None, "grid"),
        P("grid"),
        P("grid"),
        P(),
        P(),
        P("pert", "grid", None, None),
        P("grid", None),
        P(),
        P("grid", None),
        P(),
    )
    return jax.shard_map(
        one_device,
        mesh=mesh,
        in_specs=placed,
        out_specs=(P("pert", "grid", None, None), P("pert", "grid", None), P("pert", "grid")),
        check_vma=False,
    )
```
